128 devices in a mesh: req: 32 (over z_lo, y, x), tp: 4 (over z_hi, core).
Axes of the slice: x: 4, y: 4, z: 4 (z_hi: 2, z_lo: 2; z = z_hi * 2 + z_lo), core: 2. Of those that a mesh axis runs over, the one named last changes fastest.
Arguments:
- hidden_in: bfloat16 [8192, 2304], P('req'), may hold values from -6 to 6
- cache_lengths: int32 [32], P('req'), may hold values from 128 to 2048, as said below
- key_cache: bfloat16 [32, 2048, 2304], P('req', None, 'tp'), may hold values from -104 to 104
- value_cache: bfloat16 [32, 2048, 2304], P('req', None, 'tp'), may hold values from -6 to 6
- attn_norm: float32 [2304], replicated, may hold values from 0.5 to 1.5
- w_qkv: bfloat16 [3, 2304, 2304], P(None, None, 'tp'), may hold values from -0.125 to 0.125
- w_out: bfloat16 [2304, 2304], P('tp'), may hold values from -0.125 to 0.125
- ffn_norm: float32 [2304], replicated, may hold values from 0.5 to 1.5
- router: bfloat16 [2304, 8], replicated, may hold values from -0.125 to 0.125
- routes: int32 [8192, 2], P('req'), may hold values from 0 to 7, all different within a row; in each aligned block of 256 rows (0 to 255, 256 to 511, ...) at most 96 rows name the same one
- expert_gate: bfloat16 [32, 2304, 1440], P('req', None, 'tp'), may hold values from -0.125 to 0.125
- expert_up: bfloat16 [32, 2304, 1440], P('req', None, 'tp'), may hold values from -0.125 to 0.125
- expert_down: bfloat16 [32, 1440, 2304], P('req', 'tp'), may hold values from -0.078125 to 0.078125
Outputs:
- block_out: bfloat16 [8192, 2304], P(('req', 'tp'))
The draws below stay inside these ranges and needn't reach their ends.
Inputs may be any that keep to these rules, and one draw needn't show every extreme that they name: `cache_lengths`: some request has exactly 2048 cached tokens. `routes`: within the 256 rows of one request no expert is named by more than 96 rows, and in every draw, within some request, an expert is named by exactly 96 rows; a row's two experts differ.
All inputs are finite; a program needn't handle non-finite values.
Results may differ from the reference program's by a relative error of at most 0.013.
Values may be sent and summed in bfloat16 or wider, within the bound.
A program may use at most 192 MiB of HBM per device.

```python
import math
import jax
import jax.numpy as jnp
import numpy as np
from jax import lax

D = 2304
HEAD = 64
FF = 5760
EXPERTS = 8
TOP = 2
TOK = 256
CACHE = 2048
HD = 2304
REQUESTS = 32
TOKENS = 8192
SUB = 4
CAP = 96
N_REQ = 32
N_TP = 4


def draw_cache_lengths(key, part):
    first_key, second_key = jax.random.split(key)
    spread = jax.random.randint(first_key, (REQUESTS,), 0, CACHE + 1)
    lengths = jnp.maximum(CACHE // 16, spread * spread // CACHE)
    chosen = jax.random.randint(second_key, (), 0, REQUESTS)
    return lengths.at[chosen].set(CACHE).astype(jnp.int32)


def draw_key_cache(key, part):
    first_key = jax.random.fold_in(key, 0)
    result = jax.random.truncated_normal(first_key, -6.0, 6.0, (REQUESTS, CACHE, HD), jnp.float32)
    return result.astype(jnp.bfloat16)


def levels(stream_key, shape, cuts, low, largest):
    factor_of = 1.0
    for dim, blocks in cuts:
        heights = jax.random.uniform(jax.random.fold_in(jax.random.fold_in(stream_key, 6), dim), (blocks,), jnp.float32, low / len(cuts), largest / len(cuts))
        factor_of = factor_of * jnp.repeat(jnp.exp(heights), shape[dim] // blocks).reshape((-1,) + (1,) * (len(shape) - 1 - dim))
    return factor_of


def routed_block(own_key, own, number, rows, count, top, most, lean):
    sequence = jax.random.permutation(own_key, count)
    packed, common = portions_of(count, rows * top, most, lean, True), portions_of(count, rows * top, most, lean, False)
    places = jnp.arange(count)

    def named(sizes, rotation):
        used = int((sizes > 0).sum())
        fixed = max(1, used // 4)
        moved = fixed + (places - fixed + rotation * (used - fixed)) % max(1, count - fixed)
        return jnp.zeros((count,), jnp.int32).at[sequence[jnp.where(places < fixed, places, moved)]].set(jnp.asarray(sizes, jnp.int32))

    sizes = jnp.where(number % 4 == 0, named(packed, number // 4), named(common, number - number // 4 - 1))
    mixed = jax.random.permutation(jax.random.fold_in(own, 3), count)
    source_of, sink = mixed[0:count // 2 * 2:2], mixed[1:count // 2 * 2:2]
    margin = jnp.minimum(sizes[source_of] - 1, most - sizes[sink]) // 2
    margin = jnp.where((source_of == sequence[0]) | (sink == sequence[0]) | (sizes[sink] == 0), 0, jnp.maximum(margin, 0))
    moved = jax.random.randint(jax.random.fold_in(own, 4), (count // 2,), 0, 1 << 20) % (margin + 1)
    sizes = sizes.at[source_of].add(-moved).at[sink].add(moved)
    members = jnp.searchsorted(jnp.cumsum(sizes), jnp.arange(rows * top), side="right").astype(jnp.int32)
    listing = members.reshape(top, rows).T
    listing = listing[jax.random.permutation(jax.random.fold_in(own, 1), rows)]
    rotation = jax.random.randint(jax.random.fold_in(own, 2), (rows, 1), 0, top)
    return jnp.take_along_axis(listing, (jnp.arange(top)[None, :] + rotation) % top, axis=1)


def portions_of(number_of, total, bound, lean, full):
    weights = [(1 << 20) // math.isqrt(standing ** lean) + 1 for standing in range(1, number_of + 1)]
    largest = bound if full else min(bound, max(-(-total // number_of), total * weights[0] // sum(weights)))
    least = 1 if total - largest >= number_of - 1 else 0
    counts, spare = [largest] + [least] * (number_of - 1), total - largest - least * (number_of - 1)
    while spare > 0:
        movable = [i for i in range(1, number_of) if counts[i] < largest] or [i for i in range(1, number_of) if counts[i] < bound]
        pool, left = sum([weights[i] for i in movable]), spare
        for i in movable:
            extra = min(bound - counts[i], max(1, left * weights[i] // pool), spare)
            counts[i] = counts[i] + extra
            spare = spare - extra
    return np.array(counts)


def bell_draw(stream_key, dims, scale, limit, pieces=(), kind=jnp.bfloat16):
    array = jax.random.normal(stream_key, dims, jnp.float32) * scale
    if len(pieces) > 0:
        array = levels(stream_key, dims, pieces, -0.22, 0.18) * array
    return jnp.clip(array, min=-limit, max=limit).astype(kind)


def setup_inputs(seed: int = 0) -> dict:
    splits = jax.random.split(jax.random.key(seed), 14)
    hidden_in = bell_draw(splits[0], (TOKENS, D), 1.0, 6.0, ((0, 32),))
    cache_lengths = draw_cache_lengths(jax.random.fold_in(splits[13], 71), 0)
    key_cache = draw_key_cache(jax.random.fold_in(splits[13], 71), 0)
    value_cache = bell_draw(splits[3], (REQUESTS, CACHE, HD), 1.0, 6.0, ((0, 32), (2, 4)))
    attn_norm = jnp.clip(1.0 + 0.1 * jax.random.normal(splits[4], (D,), jnp.float32), 0.5, 1.5)
    w_qkv = bell_draw(splits[5], (3, D, HD), D ** -0.5, 0.125, ((2, 4),))
    w_out = bell_draw(splits[6], (HD, D), HD ** -0.5, 0.125, ((0, 4),))
    ffn_norm = jnp.clip(1.0 + 0.1 * jax.random.normal(splits[7], (D,), jnp.float32), 0.5, 1.5)
    router = bell_draw(splits[8], (D, EXPERTS), D ** -0.5, 0.125)
    routes_keys = jax.random.split(jax.random.fold_in(splits[9], 1), TOKENS // TOK)
    routes_turns = jax.random.permutation(jax.random.fold_in(splits[9], 3), TOKENS // TOK)
    routes = jax.vmap(lambda own, number: routed_block(jax.random.fold_in(splits[9], 2), own, number, TOK, EXPERTS, TOP, CAP, 1))(routes_keys, routes_turns).reshape((TOKENS, TOP))
    expert_gate = bell_draw(splits[10], (EXPERTS * SUB, D, FF // SUB), D ** -0.5, 0.125, ((0, 32), (2, 4)))
    expert_up = bell_draw(splits[11], (EXPERTS * SUB, D, FF // SUB), D ** -0.5, 0.125, ((0, 32), (2, 4)))
    expert_down = bell_draw(splits[12], (EXPERTS * SUB, FF // SUB, D), FF ** -0.5, 0.078125, ((0, 32), (1, 4)))
    return {"hidden_in": hidden_in, "cache_lengths": cache_lengths, "key_cache": key_cache, "value_cache": value_cache, "attn_norm": attn_norm, "w_qkv": w_qkv, "w_out": w_out, "ffn_norm": ffn_norm, "router": router, "routes": routes, "expert_gate": expert_gate, "expert_up": expert_up, "expert_down": expert_down}


EPSILON = 1e-05

def normalize(inputs, scale_gain):
    mean_square = lax.optimization_barrier(jnp.mean(inputs * inputs, axis=-1, keepdims=True))
    return inputs * lax.rsqrt(mean_square + EPSILON) * scale_gain

def rounded(inputs):
    return lax.optimization_barrier(inputs.astype(jnp.bfloat16))

def rotate(inputs, positions):
    half_dim = inputs.shape[-1] // 2
    frequency = jnp.exp(jnp.arange(half_dim, dtype=jnp.float32) * (-2.0 * math.log(10000.0) / inputs.shape[-1]))
    angles = positions.astype(jnp.float32)[:, None] * frequency[None, :]
    cosine = jnp.cos(angles)[:, None, :]
    sine_part = jnp.sin(angles)[:, None, :]
    lower_half = inputs[..., :half_dim]
    upper_half = inputs[..., half_dim:]
    return jnp.concatenate([lower_half * cosine - upper_half * sine_part, lower_half * sine_part + upper_half * cosine], axis=-1)

def attention(queries, all_keys, all_values, length):
    query_count = queries.shape[0]
    cache_len = all_keys.shape[0] - query_count
    scores = jnp.einsum('qhd,khd->hqk', queries.astype(jnp.float32), all_keys.astype(jnp.float32)) * queries.shape[-1] ** (-0.5)
    slot_ids = jnp.arange(cache_len + query_count, dtype=jnp.int32)
    query_ids = jnp.arange(query_count, dtype=jnp.int32)
    is_live = jnp.where(slot_ids[None, :] < cache_len, slot_ids[None, :] < length, slot_ids[None, :] - cache_len <= query_ids[:, None])
    scores = jnp.where(is_live[None], scores, -jnp.inf)
    row_max = lax.optimization_barrier(jnp.max(scores, axis=-1, keepdims=True))
    weights = jnp.exp(scores - row_max)
    totals = lax.optimization_barrier(jnp.sum(weights, axis=-1))
    mixture = jnp.einsum('hqk,khd->qhd', rounded(weights).astype(jnp.float32), all_values.astype(jnp.float32))
    return (mixture / jnp.transpose(totals)[:, :, None]).astype(jnp.bfloat16)

def reference(hidden_in, cache_lengths, key_cache, value_cache, attn_norm, w_qkv, w_out, ffn_norm, router, routes, expert_gate, expert_up, expert_down):
    residual = hidden_in.astype(jnp.float32)
    normed = rounded(normalize(residual, attn_norm))
    projection = w_qkv.astype(jnp.float32)
    local_heads = HD // HEAD

    def one_request(items):
        token_rows, length, cached_keys, cached_values = items
        projected = jnp.einsum('td,cdh->cth', token_rows.astype(jnp.float32), projection)
        positions = length + jnp.arange(TOK, dtype=jnp.int32)
        queries = rounded(rotate(projected[0].reshape(TOK, local_heads, HEAD), positions))
        fresh_keys = rounded(rotate(projected[1].reshape(TOK, local_heads, HEAD), positions))
        fresh_values = rounded(projected[2].reshape(TOK, local_heads, HEAD))
        all_keys = jnp.concatenate([cached_keys.reshape(CACHE, local_heads, HEAD), fresh_keys], axis=0)
        all_values = jnp.concatenate([cached_values.reshape(CACHE, local_heads, HEAD), fresh_values], axis=0)
        return attention(queries, all_keys, all_values, length).reshape(TOK, HD)
    attended = lax.map(one_request, (normed.reshape(REQUESTS, TOK, D), cache_lengths, key_cache, value_cache))
    attended = attended.reshape(TOKENS, HD)
    residual = residual + jnp.dot(attended, w_out, preferred_element_type=jnp.float32)
    moe_input = normalize(residual, ffn_norm).astype(jnp.bfloat16)
    logits = jnp.dot(moe_input, router, preferred_element_type=jnp.float32)
    chosen = jnp.take_along_axis(logits, routes, axis=1)
    first_gate = 1.0 / (1.0 + jnp.exp(chosen[:, 1] - chosen[:, 0]))
    second_gate = 1.0 / (1.0 + jnp.exp(chosen[:, 0] - chosen[:, 1]))
    flat_routes = routes.reshape(-1).astype(jnp.int32)
    onehot = (flat_routes[:, None] == jnp.arange(EXPERTS, dtype=jnp.int32)[None, :]).astype(jnp.int32)
    slot_rank = lax.optimization_barrier(jnp.sum((jnp.cumsum(onehot, axis=0) - onehot) * onehot, axis=1)).astype(jnp.int32)
    slot_count = N_REQ * CAP
    token_ids = (jnp.arange(TOKENS * TOP, dtype=jnp.int32) // TOP).astype(jnp.int32)
    owner = jnp.zeros((EXPERTS, slot_count), jnp.int32).at[flat_routes, slot_rank].set(token_ids)
    gate_all = expert_gate.reshape(EXPERTS, SUB, D, FF // SUB)
    up_all = expert_up.reshape(EXPERTS, SUB, D, FF // SUB)
    down_all = expert_down.reshape(EXPERTS, FF, D)
    piece_len = FF // (SUB * N_TP)

    def one_expert(items):
        owners, gate_part, up_part, down_part = items
        token_rows = moe_input[owners]
        gate_full = jnp.transpose(gate_part, (1, 0, 2)).reshape(D, FF)
        up_full = jnp.transpose(up_part, (1, 0, 2)).reshape(D, FF)
        gate_proj = jnp.dot(token_rows, gate_full, preferred_element_type=jnp.float32)
        up_proj = jnp.dot(token_rows, up_full, preferred_element_type=jnp.float32)
        activation = (jax.nn.silu(gate_proj) * up_proj).astype(jnp.bfloat16)
        totals = jnp.zeros((slot_count, D), jnp.float32)
        for slice_index in range(SUB * N_TP):
            lower = slice_index * piece_len
            partial_value = jnp.dot(activation[:, lower:lower + piece_len], down_part[lower:lower + piece_len], preferred_element_type=jnp.float32)
            totals = totals + rounded(partial_value).astype(jnp.float32)
        return totals
    results = lax.map(one_expert, (owner, gate_all, up_all, down_all))
    picked = results[flat_routes, slot_rank].reshape(TOKENS, TOP, D)
    mixed_out = first_gate[:, None] * picked[:, 0] + second_gate[:, None] * picked[:, 1]
    return (residual + mixed_out).astype(jnp.bfloat16)
```

```python
import math

import jax
import jax.numpy as jnp
from jax import lax
from jax.sharding import PartitionSpec as P

HEAD = 64
TOP = 2
CAP = 96


EPSILON = 1e-05


def normalize(inputs, scale_gain):
    mean_square = jnp.mean(inputs * inputs, axis=-1, keepdims=True)
    return inputs * lax.rsqrt(mean_square + EPSILON) * scale_gain


def rotate(inputs, positions):
    half_dim = inputs.shape[-1] // 2
    frequency = jnp.exp(
        jnp.arange(half_dim, dtype=jnp.float32) * (-2.0 * math.log(10000.0) / inputs.shape[-1])
    )
    angles = positions.astype(jnp.float32)[:, None] * frequency[None, :]
    cosine = jnp.cos(angles)[:, None, :]
    sine_part = jnp.sin(angles)[:, None, :]
    lower_half = inputs[..., :half_dim]
    upper_half = inputs[..., half_dim:]
    return jnp.concatenate(
        [
            lower_half * cosine - upper_half * sine_part,
            lower_half * sine_part + upper_half * cosine,
        ],
        axis=-1,
    )


def attention(queries, all_keys, all_values, length):
    query_count = queries.shape[0]
    cache_len = all_keys.shape[0] - query_count
    scores = jnp.einsum(
        "qhd,khd->hqk", queries, all_keys, preferred_element_type=jnp.float32
    ) * queries.shape[-1] ** (-0.5)
    slot_ids = jnp.arange(cache_len + query_count, dtype=jnp.int32)
    query_ids = jnp.arange(query_count, dtype=jnp.int32)
    is_live = jnp.where(
        slot_ids[None, :] < cache_len,
        slot_ids[None, :] < length,
        slot_ids[None, :] - cache_len <= query_ids[:, None],
    )
    scores = jnp.where(is_live[None], scores, -jnp.inf)
    row_max = jnp.max(scores, axis=-1, keepdims=True)
    weights = jnp.exp(scores - row_max)
    totals = jnp.sum(weights, axis=-1)
    mixture = jnp.einsum(
        "hqk,khd->qhd", weights.astype(jnp.bfloat16), all_values, preferred_element_type=jnp.float32
    )
    return (mixture / jnp.transpose(totals)[:, :, None]).astype(jnp.bfloat16)


def per_device(
    hidden_in,
    cache_lengths,
    key_cache,
    value_cache,
    attn_norm,
    w_qkv,
    w_out,
    ffn_norm,
    router,
    routes,
    expert_gate,
    expert_up,
    expert_down,
):
    token_count = hidden_in.shape[0]
    model_width = hidden_in.shape[1]
    local_lanes = w_qkv.shape[2]
    local_heads = local_lanes // HEAD
    cache_len = key_cache.shape[1]
    token_share = token_count // lax.axis_size("tp")
    offset = lax.axis_index("tp") * token_share
    expert_count = router.shape[1]
    copies = lax.axis_size("req") // expert_count
    residual = hidden_in.astype(jnp.float32)
    normed = normalize(residual, attn_norm).astype(jnp.bfloat16)
    projected = jnp.einsum("td,cdh->cth", normed, w_qkv, preferred_element_type=jnp.float32)
    length = cache_lengths[0]
    positions = length + jnp.arange(token_count, dtype=jnp.int32)
    queries = rotate(projected[0].reshape(token_count, local_heads, HEAD), positions).astype(
        jnp.bfloat16
    )
    fresh_keys = rotate(projected[1].reshape(token_count, local_heads, HEAD), positions).astype(
        jnp.bfloat16
    )
    fresh_values = projected[2].reshape(token_count, local_heads, HEAD).astype(jnp.bfloat16)
    all_keys = jnp.concatenate(
        [key_cache[0].reshape(cache_len, local_heads, HEAD), fresh_keys], axis=0
    )
    all_values = jnp.concatenate(
        [value_cache[0].reshape(cache_len, local_heads, HEAD), fresh_values], axis=0
    )
    attended = attention(queries, all_keys, all_values, length).reshape(token_count, local_lanes)
    summed_attn = lax.psum(
        jnp.dot(attended, w_out, preferred_element_type=jnp.float32).astype(jnp.bfloat16), "tp"
    ).astype(jnp.float32)
    updated = residual + summed_attn
    moe_input = normalize(updated, ffn_norm).astype(jnp.bfloat16)
    own_residual = lax.dynamic_slice_in_dim(updated, offset, token_share, 0)
    logits = jnp.dot(moe_input, router, preferred_element_type=jnp.float32)
    chosen = jnp.take_along_axis(logits, routes, axis=1)
    first_gate = 1.0 / (1.0 + jnp.exp(chosen[:, 1] - chosen[:, 0]))
    second_gate = 1.0 / (1.0 + jnp.exp(chosen[:, 0] - chosen[:, 1]))
    flat_routes = routes.reshape(-1)
    onehot = (flat_routes[:, None] == jnp.arange(expert_count, dtype=jnp.int32)[None, :]).astype(
        jnp.int32
    )
    slot_rank = jnp.sum((jnp.cumsum(onehot, axis=0) - onehot) * onehot, axis=1)
    tp_size = lax.axis_size("tp")
    core = lax.axis_index("tp") % 2
    half_cap = CAP // 2
    pairs = [(i, i ^ 1) for i in range(tp_size)]
    gate_w = jnp.concatenate([expert_gate[0], lax.ppermute(expert_gate[0], "tp", pairs)], axis=1)
    up_w = jnp.concatenate([expert_up[0], lax.ppermute(expert_up[0], "tp", pairs)], axis=1)
    down_w = jnp.concatenate([expert_down[0], lax.ppermute(expert_down[0], "tp", pairs)], axis=0)
    local_rank = slot_rank - core * half_cap
    in_half = (local_rank >= 0) & (local_rank < half_cap)
    slot_ids = jnp.where(in_half, flat_routes * half_cap + local_rank, -1)
    paired = slot_ids.reshape(token_count, TOP)
    slot_range = jnp.arange(expert_count * half_cap, dtype=jnp.int32)
    placing = jnp.any(paired[None, :, :] == slot_range[:, None, None], axis=2).astype(jnp.bfloat16)
    packed = (
        jnp.dot(placing, moe_input, preferred_element_type=jnp.float32)
        .astype(jnp.bfloat16)
        .reshape(expert_count, half_cap, model_width)
    )
    outgoing = jnp.broadcast_to(packed[:, None], (expert_count, copies, half_cap, model_width)).reshape(
        expert_count * copies, half_cap, model_width
    )
    received = lax.all_to_all(outgoing, "req", split_axis=0, concat_axis=0, tiled=True)
    token_rows = received.reshape(-1, model_width)
    gate_proj = jnp.dot(token_rows, gate_w, preferred_element_type=jnp.float32)
    up_proj = jnp.dot(token_rows, up_w, preferred_element_type=jnp.float32)
    activation = (jax.nn.silu(gate_proj) * up_proj).astype(jnp.bfloat16)
    partial_value = jnp.dot(activation, down_w, preferred_element_type=jnp.float32).astype(
        jnp.bfloat16
    )
    returned = lax.all_to_all(
        partial_value.reshape(received.shape), "req", split_axis=0, concat_axis=0, tiled=True
    )
    summed = jnp.sum(
        returned.reshape(expert_count, copies, half_cap, model_width).astype(jnp.float32), axis=1
    ).reshape(expert_count * half_cap, model_width)
    gates = jnp.stack([first_gate, second_gate], axis=1)
    mixing = jnp.sum(
        jnp.where(paired[:, :, None] == slot_range[None, None, :], gates[:, :, None], 0.0), axis=1
    )
    local_sum = jnp.dot(mixing, summed, precision=lax.Precision.HIGHEST)
    moe_own = lax.psum_scatter(
        local_sum.astype(jnp.bfloat16), "tp", scatter_dimension=0, tiled=True
    ).astype(jnp.float32)
    return (own_residual + moe_own).astype(jnp.bfloat16)


def solution(mesh):
    return jax.shard_map(
        per_device,
        mesh=mesh,
        in_specs=(
            P("req", None),
            P("req"),
            P("req", None, "tp"),
            P("req", None, "tp"),
            P(),
            P(None, None, "tp"),
            P("tp", None),
            P(),
            P(),
            P("req", None),
            P("req", None, "tp"),
            P("req", None, "tp"),
            P("req", "tp", None),
        ),
        out_specs=P(("req", "tp"), None),
        check_vma=False,
    )
```

```python
import math

import jax
import jax.numpy as jnp
from jax import lax
from jax.sharding import PartitionSpec as P

HEAD = 64
TOP = 2
CAP = 96


EPSILON = 1e-05


def normalize(inputs, scale_gain):
    mean_square = jnp.mean(inputs * inputs, axis=-1, keepdims=True)
    return inputs * lax.rsqrt(mean_square + EPSILON) * scale_gain


def rotate(inputs, positions):
    half_dim = inputs.shape[-1] // 2
    frequency = jnp.exp(
        jnp.arange(half_dim, dtype=jnp.float32) * (-2.0 * math.log(10000.0) / inputs.shape[-1])
    )
    angles = positions.astype(jnp.float32)[:, None] * frequency[None, :]
    cosine = jnp.cos(angles)[:, None, :]
    sine_part = jnp.sin(angles)[:, None, :]
    lower_half = inputs[..., :half_dim]
    upper_half = inputs[..., half_dim:]
    return jnp.concatenate(
        [
            lower_half * cosine - upper_half * sine_part,
            lower_half * sine_part + upper_half * cosine,
        ],
        axis=-1,
    )


def attention(queries, all_keys, all_values, length):
    query_count = queries.shape[0]
    cache_len = all_keys.shape[0] - query_count
    scores = jnp.einsum(
        "qhd,khd->hqk", queries, all_keys, preferred_element_type=jnp.float32
    ) * queries.shape[-1] ** (-0.5)
    slot_ids = jnp.arange(cache_len + query_count, dtype=jnp.int32)
    query_ids = jnp.arange(query_count, dtype=jnp.int32)
    is_live = jnp.where(
        slot_ids[None, :] < cache_len,
        slot_ids[None, :] < length,
        slot_ids[None, :] - cache_len <= query_ids[:, None],
    )
    scores = jnp.where(is_live[None], scores, -jnp.inf)
    row_max = jnp.max(scores, axis=-1, keepdims=True)
    weights = jnp.exp(scores - row_max)
    totals = jnp.sum(weights, axis=-1)
    mixture = jnp.einsum(
        "hqk,khd->qhd", weights.astype(jnp.bfloat16), all_values, preferred_element_type=jnp.float32
    )
    return (mixture / jnp.transpose(totals)[:, :, None]).astype(jnp.bfloat16)


def tp_allreduce(partial):
    tp_size = lax.axis_size("tp")
    core = lax.axis_index("tp") % 2
    core_pairs = [(i, i ^ 1) for i in range(tp_size)]
    z_pairs = [(i, i ^ 2) for i in range(tp_size)]
    halves = partial.astype(jnp.bfloat16).reshape(2, partial.shape[0] // 2, partial.shape[1])
    keep = jnp.where(core == 0, halves[0], halves[1])
    send = jnp.where(core == 0, halves[1], halves[0])
    chip_sum = (
        keep.astype(jnp.float32) + lax.ppermute(send, "tp", core_pairs).astype(jnp.float32)
    ).astype(jnp.bfloat16)
    total = (
        chip_sum.astype(jnp.float32) + lax.ppermute(chip_sum, "tp", z_pairs).astype(jnp.float32)
    ).astype(jnp.bfloat16)
    other = lax.ppermute(total, "tp", core_pairs)
    return jnp.where(core == 0, jnp.concatenate([total, other]), jnp.concatenate([other, total]))


def tp_reduce_scatter(partial):
    tp_size = lax.axis_size("tp")
    tp_index = lax.axis_index("tp")
    core = tp_index % 2
    upper = tp_index // 2
    core_pairs = [(i, i ^ 1) for i in range(tp_size)]
    z_pairs = [(i, i ^ 2) for i in range(tp_size)]
    blocks = partial.astype(jnp.bfloat16).reshape(2, 2, partial.shape[0] // 4, partial.shape[1])
    keep = jnp.where(core == 0, blocks[:, 0], blocks[:, 1])
    send = jnp.where(core == 0, blocks[:, 1], blocks[:, 0])
    chip_sum = (
        keep.astype(jnp.float32) + lax.ppermute(send, "tp", core_pairs).astype(jnp.float32)
    ).astype(jnp.bfloat16)
    mine = jnp.where(upper == 0, chip_sum[0], chip_sum[1])
    theirs = jnp.where(upper == 0, chip_sum[1], chip_sum[0])
    return mine.astype(jnp.float32) + lax.ppermute(theirs, "tp", z_pairs).astype(jnp.float32)


def per_device(
    hidden_in,
    cache_lengths,
    key_cache,
    value_cache,
    attn_norm,
    w_qkv,
    w_out,
    ffn_norm,
    router,
    routes,
    expert_gate,
    expert_up,
    expert_down,
):
    token_count = hidden_in.shape[0]
    model_width = hidden_in.shape[1]
    local_lanes = w_qkv.shape[2]
    local_heads = local_lanes // HEAD
    cache_len = key_cache.shape[1]
    token_share = token_count // lax.axis_size("tp")
    offset = lax.axis_index("tp") * token_share
    expert_count = router.shape[1]
    copies = lax.axis_size("req") // expert_count
    residual = hidden_in.astype(jnp.float32)
    normed = normalize(residual, attn_norm).astype(jnp.bfloat16)
    projected = jnp.einsum("td,cdh->cth", normed, w_qkv, preferred_element_type=jnp.float32)
    length = cache_lengths[0]
    positions = length + jnp.arange(token_count, dtype=jnp.int32)
    queries = rotate(projected[0].reshape(token_count, local_heads, HEAD), positions).astype(
        jnp.bfloat16
    )
    fresh_keys = rotate(projected[1].reshape(token_count, local_heads, HEAD), positions).astype(
        jnp.bfloat16
    )
    fresh_values = projected[2].reshape(token_count, local_heads, HEAD).astype(jnp.bfloat16)
    all_keys = jnp.concatenate(
        [key_cache[0].reshape(cache_len, local_heads, HEAD), fresh_keys], axis=0
    )
    all_values = jnp.concatenate(
        [value_cache[0].reshape(cache_len, local_heads, HEAD), fresh_values], axis=0
    )
    attended = attention(queries, all_keys, all_values, length).reshape(token_count, local_lanes)
    summed_attn = tp_allreduce(
        jnp.dot(attended, w_out, preferred_element_type=jnp.float32)
    ).astype(jnp.float32)
    updated = residual + summed_attn
    moe_input = normalize(updated, ffn_norm).astype(jnp.bfloat16)
    own_residual = lax.dynamic_slice_in_dim(updated, offset, token_share, 0)
    logits = jnp.dot(moe_input, router, preferred_element_type=jnp.float32)
    chosen = jnp.take_along_axis(logits, routes, axis=1)
    first_gate = 1.0 / (1.0 + jnp.exp(chosen[:, 1] - chosen[:, 0]))
    second_gate = 1.0 / (1.0 + jnp.exp(chosen[:, 0] - chosen[:, 1]))
    flat_routes = routes.reshape(-1)
    onehot = (flat_routes[:, None] == jnp.arange(expert_count, dtype=jnp.int32)[None, :]).astype(
        jnp.int32
    )
    slot_rank = jnp.sum((jnp.cumsum(onehot, axis=0) - onehot) * onehot, axis=1)
    tp_size = lax.axis_size("tp")
    core = lax.axis_index("tp") % 2
    half_cap = CAP // 2
    pairs = [(i, i ^ 1) for i in range(tp_size)]
    gate_w = jnp.concatenate([expert_gate[0], lax.ppermute(expert_gate[0], "tp", pairs)], axis=1)
    up_w = jnp.concatenate([expert_up[0], lax.ppermute(expert_up[0], "tp", pairs)], axis=1)
    down_w = jnp.concatenate([expert_down[0], lax.ppermute(expert_down[0], "tp", pairs)], axis=0)
    local_rank = slot_rank - core * half_cap
    in_half = (local_rank >= 0) & (local_rank < half_cap)
    slot_ids = jnp.where(in_half, flat_routes * half_cap + local_rank, -1)
    paired = slot_ids.reshape(token_count, TOP)
    slot_range = jnp.arange(expert_count * half_cap, dtype=jnp.int32)
    placing = jnp.any(paired[None, :, :] == slot_range[:, None, None], axis=2).astype(jnp.bfloat16)
    packed = (
        jnp.dot(placing, moe_input, preferred_element_type=jnp.float32)
        .astype(jnp.bfloat16)
        .reshape(expert_count, half_cap, model_width)
    )
    outgoing = jnp.broadcast_to(packed[:, None], (expert_count, copies, half_cap, model_width)).reshape(
        expert_count * copies, half_cap, model_width
    )
    received = lax.all_to_all(outgoing, "req", split_axis=0, concat_axis=0, tiled=True)
    token_rows = received.reshape(-1, model_width)
    gate_proj = jnp.dot(token_rows, gate_w, preferred_element_type=jnp.float32)
    up_proj = jnp.dot(token_rows, up_w, preferred_element_type=jnp.float32)
    activation = (jax.nn.silu(gate_proj) * up_proj).astype(jnp.bfloat16)
    partial_value = jnp.dot(activation, down_w, preferred_element_type=jnp.float32).astype(
        jnp.bfloat16
    )
    returned = lax.all_to_all(
        partial_value.reshape(received.shape), "req", split_axis=0, concat_axis=0, tiled=True
    )
    summed = jnp.sum(
        returned.reshape(expert_count, copies, half_cap, model_width).astype(jnp.float32), axis=1
    ).reshape(expert_count * half_cap, model_width)
    gates = jnp.stack([first_gate, second_gate], axis=1)
    mixing = jnp.sum(
        jnp.where(paired[:, :, None] == slot_range[None, None, :], gates[:, :, None], 0.0), axis=1
    )
    local_sum = jnp.dot(mixing, summed, precision=lax.Precision.HIGHEST)
    moe_own = tp_reduce_scatter(local_sum)
    return (own_residual + moe_own).astype(jnp.bfloat16)


def solution(mesh):
    return jax.shard_map(
        per_device,
        mesh=mesh,
        in_specs=(
            P("req", None),
            P("req"),
            P("req", None, "tp"),
            P("req", None, "tp"),
            P(),
            P(None, None, "tp"),
            P("tp", None),
            P(),
            P(),
            P("req", None),
            P("req", None, "tp"),
            P("req", None, "tp"),
            P("req", "tp", None),
        ),
        out_specs=P(("req", "tp"), None),
        check_vma=False,
    )
```

```python
import math

import jax
import jax.numpy as jnp
from jax import lax
from jax.sharding import PartitionSpec as P

HEAD = 64
TOP = 2
CAP = 96


EPSILON = 1e-05


def normalize(inputs, scale_gain):
    mean_square = jnp.mean(inputs * inputs, axis=-1, keepdims=True)
    return inputs * lax.rsqrt(mean_square + EPSILON) * scale_gain


def rotate(inputs, positions):
    half_dim = inputs.shape[-1] // 2
    frequency = jnp.exp(
        jnp.arange(half_dim, dtype=jnp.float32) * (-2.0 * math.log(10000.0) / inputs.shape[-1])
    )
    angles = positions.astype(jnp.float32)[:, None] * frequency[None, :]
    cosine = jnp.cos(angles)[:, None, :]
    sine_part = jnp.sin(angles)[:, None, :]
    lower_half = inputs[..., :half_dim]
    upper_half = inputs[..., half_dim:]
    return jnp.concatenate(
        [
            lower_half * cosine - upper_half * sine_part,
            lower_half * sine_part + upper_half * cosine,
        ],
        axis=-1,
    )


def attention(queries, all_keys, all_values, length):
    query_count = queries.shape[0]
    cache_len = all_keys.shape[0] - query_count
    scores = jnp.einsum(
        "qhd,khd->hqk", queries, all_keys, preferred_element_type=jnp.float32
    ) * queries.shape[-1] ** (-0.5)
    slot_ids = jnp.arange(cache_len + query_count, dtype=jnp.int32)
    query_ids = jnp.arange(query_count, dtype=jnp.int32)
    is_live = jnp.where(
        slot_ids[None, :] < cache_len,
        slot_ids[None, :] < length,
        slot_ids[None, :] - cache_len <= query_ids[:, None],
    )
    scores = jnp.where(is_live[None], scores, -jnp.inf)
    row_max = jnp.max(scores, axis=-1, keepdims=True)
    weights = jnp.exp(scores - row_max)
    totals = jnp.sum(weights, axis=-1)
    mixture = jnp.einsum(
        "hqk,khd->qhd", weights.astype(jnp.bfloat16), all_values, preferred_element_type=jnp.float32
    )
    return (mixture / jnp.transpose(totals)[:, :, None]).astype(jnp.bfloat16)


def tp_allreduce(partial):
    tp_size = lax.axis_size("tp")
    core = lax.axis_index("tp") % 2
    core_pairs = [(i, i ^ 1) for i in range(tp_size)]
    z_pairs = [(i, i ^ 2) for i in range(tp_size)]
    halves = partial.astype(jnp.bfloat16).reshape(2, partial.shape[0] // 2, partial.shape[1])
    keep = jnp.where(core == 0, halves[0], halves[1])
    send = jnp.where(core == 0, halves[1], halves[0])
    chip_sum = (
        keep.astype(jnp.float32) + lax.ppermute(send, "tp", core_pairs).astype(jnp.float32)
    ).astype(jnp.bfloat16)
    total = (
        chip_sum.astype(jnp.float32) + lax.ppermute(chip_sum, "tp", z_pairs).astype(jnp.float32)
    ).astype(jnp.bfloat16)
    other = lax.ppermute(total, "tp", core_pairs)
    return jnp.where(core == 0, jnp.concatenate([total, other]), jnp.concatenate([other, total]))


def tp_reduce_scatter(partial):
    tp_size = lax.axis_size("tp")
    tp_index = lax.axis_index("tp")
    core = tp_index % 2
    upper = tp_index // 2
    core_pairs = [(i, i ^ 1) for i in range(tp_size)]
    z_pairs = [(i, i ^ 2) for i in range(tp_size)]
    blocks = partial.astype(jnp.bfloat16).reshape(2, 2, partial.shape[0] // 4, partial.shape[1])
    keep = jnp.where(core == 0, blocks[:, 0], blocks[:, 1])
    send = jnp.where(core == 0, blocks[:, 1], blocks[:, 0])
    chip_sum = (
        keep.astype(jnp.float32) + lax.ppermute(send, "tp", core_pairs).astype(jnp.float32)
    ).astype(jnp.bfloat16)
    mine = jnp.where(upper == 0, chip_sum[0], chip_sum[1])
    theirs = jnp.where(upper == 0, chip_sum[1], chip_sum[0])
    return mine.astype(jnp.float32) + lax.ppermute(theirs, "tp", z_pairs).astype(jnp.float32)


def per_device(
    hidden_in,
    cache_lengths,
    key_cache,
    value_cache,
    attn_norm,
    w_qkv,
    w_out,
    ffn_norm,
    router,
    routes,
    expert_gate,
    expert_up,
    expert_down,
):
    token_count = hidden_in.shape[0]
    model_width = hidden_in.shape[1]
    local_lanes = w_qkv.shape[2]
    local_heads = local_lanes // HEAD
    cache_len = key_cache.shape[1]
    token_share = token_count // lax.axis_size("tp")
    offset = lax.axis_index("tp") * token_share
    expert_count = router.shape[1]
    copies = lax.axis_size("req") // expert_count
    residual = hidden_in.astype(jnp.float32)
    normed = normalize(residual, attn_norm).astype(jnp.bfloat16)
    projected = jnp.einsum("td,cdh->cth", normed, w_qkv, preferred_element_type=jnp.float32)
    length = cache_lengths[0]
    positions = length + jnp.arange(token_count, dtype=jnp.int32)
    queries = rotate(projected[0].reshape(token_count, local_heads, HEAD), positions).astype(
        jnp.bfloat16
    )
    fresh_keys = rotate(projected[1].reshape(token_count, local_heads, HEAD), positions).astype(
        jnp.bfloat16
    )
    fresh_values = projected[2].reshape(token_count, local_heads, HEAD).astype(jnp.bfloat16)
    all_keys = jnp.concatenate(
        [key_cache[0].reshape(cache_len, local_heads, HEAD), fresh_keys], axis=0
    )
    all_values = jnp.concatenate(
        [value_cache[0].reshape(cache_len, local_heads, HEAD), fresh_values], axis=0
    )
    attended = attention(queries, all_keys, all_values, length).reshape(token_count, local_lanes)
    summed_attn = tp_allreduce(
        jnp.dot(attended, w_out, preferred_element_type=jnp.float32)
    ).astype(jnp.float32)
    updated = residual + summed_attn
    moe_input = normalize(updated, ffn_norm).astype(jnp.bfloat16)
    own_residual = lax.dynamic_slice_in_dim(updated, offset, token_share, 0)
    logits = jnp.dot(moe_input, router, preferred_element_type=jnp.float32)
    chosen = jnp.take_along_axis(logits, routes, axis=1)
    first_gate = 1.0 / (1.0 + jnp.exp(chosen[:, 1] - chosen[:, 0]))
    second_gate = 1.0 / (1.0 + jnp.exp(chosen[:, 0] - chosen[:, 1]))
    flat_routes = routes.reshape(-1)
    onehot = (flat_routes[:, None] == jnp.arange(expert_count, dtype=jnp.int32)[None, :]).astype(
        jnp.int32
    )
    slot_rank = jnp.sum((jnp.cumsum(onehot, axis=0) - onehot) * onehot, axis=1)
    tp_size = lax.axis_size("tp")
    core = lax.axis_index("tp") % 2
    half_cap = CAP // 2
    pairs = [(i, i ^ 1) for i in range(tp_size)]
    gate_w = jnp.concatenate([expert_gate[0], lax.ppermute(expert_gate[0], "tp", pairs)], axis=1)
    up_w = jnp.concatenate([expert_up[0], lax.ppermute(expert_up[0], "tp", pairs)], axis=1)
    down_w = jnp.concatenate([expert_down[0], lax.ppermute(expert_down[0], "tp", pairs)], axis=0)
    local_rank = slot_rank - core * half_cap
    in_half = (local_rank >= 0) & (local_rank < half_cap)
    slot_ids = jnp.where(in_half, flat_routes * half_cap + local_rank, -1)
    paired = slot_ids.reshape(token_count, TOP)
    slot_range = jnp.arange(expert_count * half_cap, dtype=jnp.int32)
    chunk_count = 2
    chunk = half_cap // chunk_count
    chunk_results = []
    for index in range(chunk_count):
        chunk_ids = jnp.where(
            (local_rank >= index * chunk) & (local_rank < (index + 1) * chunk),
            flat_routes * chunk + local_rank - index * chunk,
            -1,
        ).reshape(token_count, TOP)
        chunk_range = jnp.arange(expert_count * chunk, dtype=jnp.int32)
        placing = jnp.any(chunk_ids[None, :, :] == chunk_range[:, None, None], axis=2).astype(
            jnp.bfloat16
        )
        packed = (
            jnp.dot(placing, moe_input, preferred_element_type=jnp.float32)
            .astype(jnp.bfloat16)
            .reshape(expert_count, chunk, model_width)
        )
        outgoing = jnp.broadcast_to(
            packed[:, None], (expert_count, copies, chunk, model_width)
        ).reshape(expert_count * copies, chunk, model_width)
        received = lax.all_to_all(outgoing, "req", split_axis=0, concat_axis=0, tiled=True)
        token_rows = received.reshape(-1, model_width)
        gate_proj = jnp.dot(token_rows, gate_w, preferred_element_type=jnp.float32)
        up_proj = jnp.dot(token_rows, up_w, preferred_element_type=jnp.float32)
        activation = (jax.nn.silu(gate_proj) * up_proj).astype(jnp.bfloat16)
        partial_value = jnp.dot(
            activation, down_w, preferred_element_type=jnp.float32
        ).astype(jnp.bfloat16)
        returned = lax.all_to_all(
            partial_value.reshape(received.shape), "req", split_axis=0, concat_axis=0, tiled=True
        )
        chunk_results.append(
            jnp.sum(
                returned.reshape(expert_count, copies, chunk, model_width).astype(jnp.float32),
                axis=1,
            )
        )
    summed = jnp.concatenate(chunk_results, axis=1).reshape(expert_count * half_cap, model_width)
    gates = jnp.stack([first_gate, second_gate], axis=1)
    mixing = jnp.sum(
        jnp.where(paired[:, :, None] == slot_range[None, None, :], gates[:, :, None], 0.0), axis=1
    )
    local_sum = jnp.dot(mixing, summed, precision=lax.Precision.HIGHEST)
    moe_own = tp_reduce_scatter(local_sum)
    return (own_residual + moe_own).astype(jnp.bfloat16)


def solution(mesh):
    return jax.shard_map(
        per_device,
        mesh=mesh,
        in_specs=(
            P("req", None),
            P("req"),
            P("req", None, "tp"),
            P("req", None, "tp"),
            P(),
            P(None, None, "tp"),
            P("tp", None),
            P(),
            P(),
            P("req", None),
            P("req", None, "tp"),
            P("req", None, "tp"),
            P("req", "tp", None),
        ),
        out_specs=P(("req", "tp"), None),
        check_vma=False,
    )
```

```python
import functools
import math

import jax
import jax.numpy as jnp
from jax import lax
from jax.experimental import pallas as pl
from jax.experimental.pallas import tpu as pltpu
from jax.sharding import PartitionSpec as P

HEAD = 64
TOP = 2
CAP = 96


EPSILON = 1e-05


def normalize(inputs, scale_gain):
    mean_square = jnp.mean(inputs * inputs, axis=-1, keepdims=True)
    return inputs * lax.rsqrt(mean_square + EPSILON) * scale_gain


def rotate(inputs, positions):
    half_dim = inputs.shape[-1] // 2
    frequency = jnp.exp(
        jnp.arange(half_dim, dtype=jnp.float32) * (-2.0 * math.log(10000.0) / inputs.shape[-1])
    )
    angles = positions.astype(jnp.float32)[:, None] * frequency[None, :]
    cosine = jnp.cos(angles)[:, None, :]
    sine_part = jnp.sin(angles)[:, None, :]
    lower_half = inputs[..., :half_dim]
    upper_half = inputs[..., half_dim:]
    return jnp.concatenate(
        [
            lower_half * cosine - upper_half * sine_part,
            lower_half * sine_part + upper_half * cosine,
        ],
        axis=-1,
    )


def attention_kernel(length_ref, query_ref, key_ref, value_ref, out_ref, *, cache_len):
    queries = query_ref[0]
    scores = lax.dot_general(
        queries, key_ref[0], (((1,), (1,)), ((), ())), preferred_element_type=jnp.float32
    ) * (queries.shape[-1] ** -0.5)
    column = lax.broadcasted_iota(jnp.int32, scores.shape, 1)
    row = lax.broadcasted_iota(jnp.int32, scores.shape, 0)
    live = ((column < cache_len) & (column < length_ref[0])) | (
        (column >= cache_len) & (column - cache_len <= row)
    )
    scores = jnp.where(live, scores, -jnp.inf)
    row_max = jnp.max(scores, axis=1, keepdims=True)
    weights = jnp.exp(scores - row_max)
    totals = jnp.sum(weights, axis=1, keepdims=True)
    mixture = jnp.dot(weights.astype(jnp.bfloat16), value_ref[0], preferred_element_type=jnp.float32)
    out_ref[0] = (mixture / totals).astype(out_ref.dtype)


def attention(queries, all_keys, all_values, length):
    query_count, heads, head_dim = queries.shape
    key_count = all_keys.shape[0]
    by_head = lambda x: jnp.transpose(x, (1, 0, 2))
    mixed = pl.pallas_call(
        functools.partial(attention_kernel, cache_len=key_count - query_count),
        out_shape=jax.ShapeDtypeStruct((heads, query_count, head_dim), jnp.bfloat16),
        grid_spec=pltpu.PrefetchScalarGridSpec(
            num_scalar_prefetch=1,
            grid=(heads,),
            in_specs=[
                pl.BlockSpec((1, query_count, head_dim), lambda h, n: (h, 0, 0)),
                pl.BlockSpec((1, key_count, head_dim), lambda h, n: (h, 0, 0)),
                pl.BlockSpec((1, key_count, head_dim), lambda h, n: (h, 0, 0)),
            ],
            out_specs=pl.BlockSpec((1, query_count, head_dim), lambda h, n: (h, 0, 0)),
        ),
    )(length, by_head(queries), by_head(all_keys), by_head(all_values))
    return by_head(mixed)


def tp_allreduce(partial):
    tp_size = lax.axis_size("tp")
    core = lax.axis_index("tp") % 2
    core_pairs = [(i, i ^ 1) for i in range(tp_size)]
    z_pairs = [(i, i ^ 2) for i in range(tp_size)]
    halves = partial.astype(jnp.bfloat16).reshape(2, partial.shape[0] // 2, partial.shape[1])
    keep = jnp.where(core == 0, halves[0], halves[1])
    send = jnp.where(core == 0, halves[1], halves[0])
    chip_sum = (
        keep.astype(jnp.float32) + lax.ppermute(send, "tp", core_pairs).astype(jnp.float32)
    ).astype(jnp.bfloat16)
    total = (
        chip_sum.astype(jnp.float32) + lax.ppermute(chip_sum, "tp", z_pairs).astype(jnp.float32)
    ).astype(jnp.bfloat16)
    other = lax.ppermute(total, "tp", core_pairs)
    return jnp.where(core == 0, jnp.concatenate([total, other]), jnp.concatenate([other, total]))


def tp_reduce_scatter(partial):
    tp_size = lax.axis_size("tp")
    tp_index = lax.axis_index("tp")
    core = tp_index % 2
    upper = tp_index // 2
    core_pairs = [(i, i ^ 1) for i in range(tp_size)]
    z_pairs = [(i, i ^ 2) for i in range(tp_size)]
    blocks = partial.astype(jnp.bfloat16).reshape(2, 2, partial.shape[0] // 4, partial.shape[1])
    keep = jnp.where(core == 0, blocks[:, 0], blocks[:, 1])
    send = jnp.where(core == 0, blocks[:, 1], blocks[:, 0])
    chip_sum = (
        keep.astype(jnp.float32) + lax.ppermute(send, "tp", core_pairs).astype(jnp.float32)
    ).astype(jnp.bfloat16)
    mine = jnp.where(upper == 0, chip_sum[0], chip_sum[1])
    theirs = jnp.where(upper == 0, chip_sum[1], chip_sum[0])
    return mine.astype(jnp.float32) + lax.ppermute(theirs, "tp", z_pairs).astype(jnp.float32)


def per_device(
    hidden_in,
    cache_lengths,
    key_cache,
    value_cache,
    attn_norm,
    w_qkv,
    w_out,
    ffn_norm,
    router,
    routes,
    expert_gate,
    expert_up,
    expert_down,
):
    token_count = hidden_in.shape[0]
    model_width = hidden_in.shape[1]
    local_lanes = w_qkv.shape[2]
    local_heads = local_lanes // HEAD
    cache_len = key_cache.shape[1]
    token_share = token_count // lax.axis_size("tp")
    offset = lax.axis_index("tp") * token_share
    expert_count = router.shape[1]
    copies = lax.axis_size("req") // expert_count
    residual = hidden_in.astype(jnp.float32)
    normed = normalize(residual, attn_norm).astype(jnp.bfloat16)
    projected = jnp.einsum("td,cdh->cth", normed, w_qkv, preferred_element_type=jnp.float32)
    length = cache_lengths[0]
    positions = length + jnp.arange(token_count, dtype=jnp.int32)
    queries = rotate(projected[0].reshape(token_count, local_heads, HEAD), positions).astype(
        jnp.bfloat16
    )
    fresh_keys = rotate(projected[1].reshape(token_count, local_heads, HEAD), positions).astype(
        jnp.bfloat16
    )
    fresh_values = projected[2].reshape(token_count, local_heads, HEAD).astype(jnp.bfloat16)
    all_keys = jnp.concatenate(
        [key_cache[0].reshape(cache_len, local_heads, HEAD), fresh_keys], axis=0
    )
    all_values = jnp.concatenate(
        [value_cache[0].reshape(cache_len, local_heads, HEAD), fresh_values], axis=0
    )
    attended = attention(queries, all_keys, all_values, cache_lengths).reshape(
        token_count, local_lanes
    )
    summed_attn = tp_allreduce(
        jnp.dot(attended, w_out, preferred_element_type=jnp.float32)
    ).astype(jnp.float32)
    updated = residual + summed_attn
    moe_input = normalize(updated, ffn_norm).astype(jnp.bfloat16)
    own_residual = lax.dynamic_slice_in_dim(updated, offset, token_share, 0)
    logits = jnp.dot(moe_input, router, preferred_element_type=jnp.float32)
    chosen = jnp.take_along_axis(logits, routes, axis=1)
    first_gate = 1.0 / (1.0 + jnp.exp(chosen[:, 1] - chosen[:, 0]))
    second_gate = 1.0 / (1.0 + jnp.exp(chosen[:, 0] - chosen[:, 1]))
    flat_routes = routes.reshape(-1)
    onehot = (flat_routes[:, None] == jnp.arange(expert_count, dtype=jnp.int32)[None, :]).astype(
        jnp.int32
    )
    slot_rank = jnp.sum((jnp.cumsum(onehot, axis=0) - onehot) * onehot, axis=1)
    tp_size = lax.axis_size("tp")
    core = lax.axis_index("tp") % 2
    half_cap = CAP // 2
    pairs = [(i, i ^ 1) for i in range(tp_size)]
    gate_w = jnp.concatenate([expert_gate[0], lax.ppermute(expert_gate[0], "tp", pairs)], axis=1)
    up_w = jnp.concatenate([expert_up[0], lax.ppermute(expert_up[0], "tp", pairs)], axis=1)
    down_w = jnp.concatenate([expert_down[0], lax.ppermute(expert_down[0], "tp", pairs)], axis=0)
    local_rank = slot_rank - core * half_cap
    in_half = (local_rank >= 0) & (local_rank < half_cap)
    slot_ids = jnp.where(in_half, flat_routes * half_cap + local_rank, -1)
    paired = slot_ids.reshape(token_count, TOP)
    slot_range = jnp.arange(expert_count * half_cap, dtype=jnp.int32)
    chunk_count = 2
    chunk = half_cap // chunk_count
    chunk_results = []
    for index in range(chunk_count):
        chunk_ids = jnp.where(
            (local_rank >= index * chunk) & (local_rank < (index + 1) * chunk),
            flat_routes * chunk + local_rank - index * chunk,
            -1,
        ).reshape(token_count, TOP)
        chunk_range = jnp.arange(expert_count * chunk, dtype=jnp.int32)
        placing = jnp.any(chunk_ids[None, :, :] == chunk_range[:, None, None], axis=2).astype(
            jnp.bfloat16
        )
        packed = (
            jnp.dot(placing, moe_input, preferred_element_type=jnp.float32)
            .astype(jnp.bfloat16)
            .reshape(expert_count, chunk, model_width)
        )
        outgoing = jnp.broadcast_to(
            packed[:, None], (expert_count, copies, chunk, model_width)
        ).reshape(expert_count * copies, chunk, model_width)
        received = lax.all_to_all(outgoing, "req", split_axis=0, concat_axis=0, tiled=True)
        token_rows = received.reshape(-1, model_width)
        gate_proj = jnp.dot(token_rows, gate_w, preferred_element_type=jnp.float32)
        up_proj = jnp.dot(token_rows, up_w, preferred_element_type=jnp.float32)
        activation = (jax.nn.silu(gate_proj) * up_proj).astype(jnp.bfloat16)
        partial_value = jnp.dot(
            activation, down_w, preferred_element_type=jnp.float32
        ).astype(jnp.bfloat16)
        returned = lax.all_to_all(
            partial_value.reshape(received.shape), "req", split_axis=0, concat_axis=0, tiled=True
        )
        chunk_results.append(
            jnp.sum(
                returned.reshape(expert_count, copies, chunk, model_width).astype(jnp.float32),
                axis=1,
            )
        )
    summed = jnp.concatenate(chunk_results, axis=1).reshape(expert_count * half_cap, model_width)
    gates = jnp.stack([first_gate, second_gate], axis=1)
    mixing = jnp.sum(
        jnp.where(paired[:, :, None] == slot_range[None, None, :], gates[:, :, None], 0.0), axis=1
    )
    local_sum = jnp.dot(mixing, summed, precision=lax.Precision.HIGHEST)
    moe_own = tp_reduce_scatter(local_sum)
    return (own_residual + moe_own).astype(jnp.bfloat16)


def solution(mesh):
    return jax.shard_map(
        per_device,
        mesh=mesh,
        in_specs=(
            P("req", None),
            P("req"),
            P("req", None, "tp"),
            P("req", None, "tp"),
            P(),
            P(None, None, "tp"),
            P("tp", None),
            P(),
            P(),
            P("req", None),
            P("req", None, "tp"),
            P("req", None, "tp"),
            P("req", "tp", None),
        ),
        out_specs=P(("req", "tp"), None),
        check_vma=False,
    )
```

```python
import functools
import math

import jax
import jax.numpy as jnp
from jax import lax
from jax.experimental import pallas as pl
from jax.experimental.pallas import tpu as pltpu
from jax.sharding import PartitionSpec as P

HEAD = 64
TOP = 2
CAP = 96


EPSILON = 1e-05


def normalize(inputs, scale_gain):
    mean_square = jnp.mean(inputs * inputs, axis=-1, keepdims=True)
    return inputs * lax.rsqrt(mean_square + EPSILON) * scale_gain


def rotate(inputs, positions):
    half_dim = inputs.shape[-1] // 2
    frequency = jnp.exp(
        jnp.arange(half_dim, dtype=jnp.float32) * (-2.0 * math.log(10000.0) / inputs.shape[-1])
    )
    angles = positions.astype(jnp.float32)[:, None] * frequency[None, :]
    cosine = jnp.cos(angles)[:, None, :]
    sine_part = jnp.sin(angles)[:, None, :]
    lower_half = inputs[..., :half_dim]
    upper_half = inputs[..., half_dim:]
    return jnp.concatenate(
        [
            lower_half * cosine - upper_half * sine_part,
            lower_half * sine_part + upper_half * cosine,
        ],
        axis=-1,
    )


def attention_kernel(
    length_ref, query_ref, key_ref, value_ref, fresh_key_ref, fresh_value_ref, out_ref, *, head_dim
):
    query_count = query_ref.shape[0]
    cache_len = key_ref.shape[1]
    length = length_ref[0]
    cache_live = lax.broadcasted_iota(jnp.int32, (query_count, cache_len), 1) < length
    fresh_live = lax.broadcasted_iota(
        jnp.int32, (query_count, query_count), 1
    ) <= lax.broadcasted_iota(jnp.int32, (query_count, query_count), 0)
    contract = (((1,), (1,)), ((), ()))
    for head in range(query_ref.shape[1] // head_dim):
        lanes = slice(head * head_dim, (head + 1) * head_dim)
        queries = query_ref[:, lanes]
        cache_scores = jnp.dot(
            queries, key_ref[lanes, :], preferred_element_type=jnp.float32
        ) * (head_dim ** -0.5)
        fresh_scores = jnp.dot(
            queries, fresh_key_ref[lanes, :], preferred_element_type=jnp.float32
        ) * (head_dim ** -0.5)
        cache_scores = jnp.where(cache_live, cache_scores, -jnp.inf)
        fresh_scores = jnp.where(fresh_live, fresh_scores, -jnp.inf)
        row_max = jnp.maximum(
            jnp.max(cache_scores, axis=1, keepdims=True),
            jnp.max(fresh_scores, axis=1, keepdims=True),
        )
        cache_weights = jnp.exp(cache_scores - row_max)
        fresh_weights = jnp.exp(fresh_scores - row_max)
        totals = jnp.sum(cache_weights, axis=1, keepdims=True) + jnp.sum(
            fresh_weights, axis=1, keepdims=True
        )
        mixture = lax.dot_general(
            cache_weights.astype(jnp.bfloat16),
            value_ref[lanes, :],
            contract,
            preferred_element_type=jnp.float32,
        ) + lax.dot_general(
            fresh_weights.astype(jnp.bfloat16),
            fresh_value_ref[lanes, :],
            contract,
            preferred_element_type=jnp.float32,
        )
        out_ref[:, lanes] = (mixture / totals).astype(out_ref.dtype)


def attention(queries, key_cache, value_cache, fresh_keys, fresh_values, length):
    vmem = pl.BlockSpec(memory_space=pltpu.VMEM)
    return pl.pallas_call(
        functools.partial(attention_kernel, head_dim=HEAD),
        out_shape=jax.ShapeDtypeStruct(queries.shape, jnp.bfloat16),
        in_specs=[pl.BlockSpec(memory_space=pltpu.SMEM)] + [vmem] * 5,
        out_specs=vmem,
    )(length, queries, key_cache.T, value_cache.T, fresh_keys.T, fresh_values.T)


def tp_allreduce(partial):
    tp_size = lax.axis_size("tp")
    core = lax.axis_index("tp") % 2
    core_pairs = [(i, i ^ 1) for i in range(tp_size)]
    z_pairs = [(i, i ^ 2) for i in range(tp_size)]
    halves = partial.astype(jnp.bfloat16).reshape(2, partial.shape[0] // 2, partial.shape[1])
    keep = jnp.where(core == 0, halves[0], halves[1])
    send = jnp.where(core == 0, halves[1], halves[0])
    chip_sum = (
        keep.astype(jnp.float32) + lax.ppermute(send, "tp", core_pairs).astype(jnp.float32)
    ).astype(jnp.bfloat16)
    total = (
        chip_sum.astype(jnp.float32) + lax.ppermute(chip_sum, "tp", z_pairs).astype(jnp.float32)
    ).astype(jnp.bfloat16)
    other = lax.ppermute(total, "tp", core_pairs)
    return jnp.where(core == 0, jnp.concatenate([total, other]), jnp.concatenate([other, total]))


def tp_reduce_scatter(partial):
    tp_size = lax.axis_size("tp")
    tp_index = lax.axis_index("tp")
    core = tp_index % 2
    upper = tp_index // 2
    core_pairs = [(i, i ^ 1) for i in range(tp_size)]
    z_pairs = [(i, i ^ 2) for i in range(tp_size)]
    blocks = partial.astype(jnp.bfloat16).reshape(2, 2, partial.shape[0] // 4, partial.shape[1])
    keep = jnp.where(core == 0, blocks[:, 0], blocks[:, 1])
    send = jnp.where(core == 0, blocks[:, 1], blocks[:, 0])
    chip_sum = (
        keep.astype(jnp.float32) + lax.ppermute(send, "tp", core_pairs).astype(jnp.float32)
    ).astype(jnp.bfloat16)
    mine = jnp.where(upper == 0, chip_sum[0], chip_sum[1])
    theirs = jnp.where(upper == 0, chip_sum[1], chip_sum[0])
    return mine.astype(jnp.float32) + lax.ppermute(theirs, "tp", z_pairs).astype(jnp.float32)


def per_device(
    hidden_in,
    cache_lengths,
    key_cache,
    value_cache,
    attn_norm,
    w_qkv,
    w_out,
    ffn_norm,
    router,
    routes,
    expert_gate,
    expert_up,
    expert_down,
):
    token_count = hidden_in.shape[0]
    model_width = hidden_in.shape[1]
    local_lanes = w_qkv.shape[2]
    local_heads = local_lanes // HEAD
    cache_len = key_cache.shape[1]
    token_share = token_count // lax.axis_size("tp")
    offset = lax.axis_index("tp") * token_share
    expert_count = router.shape[1]
    copies = lax.axis_size("req") // expert_count
    residual = hidden_in.astype(jnp.float32)
    normed = normalize(residual, attn_norm).astype(jnp.bfloat16)
    projected = jnp.einsum("td,cdh->cth", normed, w_qkv, preferred_element_type=jnp.float32)
    length = cache_lengths[0]
    positions = length + jnp.arange(token_count, dtype=jnp.int32)
    queries = rotate(projected[0].reshape(token_count, local_heads, HEAD), positions).astype(
        jnp.bfloat16
    )
    fresh_keys = rotate(projected[1].reshape(token_count, local_heads, HEAD), positions).astype(
        jnp.bfloat16
    )
    fresh_values = projected[2].reshape(token_count, local_heads, HEAD).astype(jnp.bfloat16)
    attended = attention(
        queries.reshape(token_count, local_lanes),
        key_cache[0],
        value_cache[0],
        fresh_keys.reshape(token_count, local_lanes),
        fresh_values.reshape(token_count, local_lanes),
        cache_lengths,
    )
    summed_attn = tp_allreduce(
        jnp.dot(attended, w_out, preferred_element_type=jnp.float32)
    ).astype(jnp.float32)
    updated = residual + summed_attn
    moe_input = normalize(updated, ffn_norm).astype(jnp.bfloat16)
    own_residual = lax.dynamic_slice_in_dim(updated, offset, token_share, 0)
    logits = jnp.dot(moe_input, router, preferred_element_type=jnp.float32)
    chosen = jnp.take_along_axis(logits, routes, axis=1)
    first_gate = 1.0 / (1.0 + jnp.exp(chosen[:, 1] - chosen[:, 0]))
    second_gate = 1.0 / (1.0 + jnp.exp(chosen[:, 0] - chosen[:, 1]))
    flat_routes = routes.reshape(-1)
    onehot = (flat_routes[:, None] == jnp.arange(expert_count, dtype=jnp.int32)[None, :]).astype(
        jnp.int32
    )
    slot_rank = jnp.sum((jnp.cumsum(onehot, axis=0) - onehot) * onehot, axis=1)
    tp_size = lax.axis_size("tp")
    core = lax.axis_index("tp") % 2
    half_cap = CAP // 2
    pairs = [(i, i ^ 1) for i in range(tp_size)]
    gate_w = jnp.concatenate([expert_gate[0], lax.ppermute(expert_gate[0], "tp", pairs)], axis=1)
    up_w = jnp.concatenate([expert_up[0], lax.ppermute(expert_up[0], "tp", pairs)], axis=1)
    down_w = jnp.concatenate([expert_down[0], lax.ppermute(expert_down[0], "tp", pairs)], axis=0)
    local_rank = slot_rank - core * half_cap
    in_half = (local_rank >= 0) & (local_rank < half_cap)
    slot_ids = jnp.where(in_half, flat_routes * half_cap + local_rank, -1)
    paired = slot_ids.reshape(token_count, TOP)
    slot_range = jnp.arange(expert_count * half_cap, dtype=jnp.int32)
    chunk_count = 2
    chunk = half_cap // chunk_count
    chunk_results = []
    for index in range(chunk_count):
        chunk_ids = jnp.where(
            (local_rank >= index * chunk) & (local_rank < (index + 1) * chunk),
            flat_routes * chunk + local_rank - index * chunk,
            -1,
        ).reshape(token_count, TOP)
        chunk_range = jnp.arange(expert_count * chunk, dtype=jnp.int32)
        placing = jnp.any(chunk_ids[None, :, :] == chunk_range[:, None, None], axis=2).astype(
            jnp.bfloat16
        )
        packed = (
            jnp.dot(placing, moe_input, preferred_element_type=jnp.float32)
            .astype(jnp.bfloat16)
            .reshape(expert_count, chunk, model_width)
        )
        outgoing = jnp.broadcast_to(
            packed[:, None], (expert_count, copies, chunk, model_width)
        ).reshape(expert_count * copies, chunk, model_width)
        received = lax.all_to_all(outgoing, "req", split_axis=0, concat_axis=0, tiled=True)
        token_rows = received.reshape(-1, model_width)
        gate_proj = jnp.dot(token_rows, gate_w, preferred_element_type=jnp.float32)
        up_proj = jnp.dot(token_rows, up_w, preferred_element_type=jnp.float32)
        activation = (jax.nn.silu(gate_proj) * up_proj).astype(jnp.bfloat16)
        partial_value = jnp.dot(
            activation, down_w, preferred_element_type=jnp.float32
        ).astype(jnp.bfloat16)
        returned = lax.all_to_all(
            partial_value.reshape(received.shape), "req", split_axis=0, concat_axis=0, tiled=True
        )
        chunk_results.append(
            jnp.sum(
                returned.reshape(expert_count, copies, chunk, model_width).astype(jnp.float32),
                axis=1,
            )
        )
    summed = jnp.concatenate(chunk_results, axis=1).reshape(expert_count * half_cap, model_width)
    gates = jnp.stack([first_gate, second_gate], axis=1)
    mixing = jnp.sum(
        jnp.where(paired[:, :, None] == slot_range[None, None, :], gates[:, :, None], 0.0), axis=1
    )
    local_sum = jnp.dot(mixing, summed, precision=lax.Precision.HIGHEST)
    moe_own = tp_reduce_scatter(local_sum)
    return (own_residual + moe_own).astype(jnp.bfloat16)


def solution(mesh):
    return jax.shard_map(
        per_device,
        mesh=mesh,
        in_specs=(
            P("req", None),
            P("req"),
            P("req", None, "tp"),
            P("req", None, "tp"),
            P(),
            P(None, None, "tp"),
            P("tp", None),
            P(),
            P(),
            P("req", None),
            P("req", None, "tp"),
            P("req", None, "tp"),
            P("req", "tp", None),
        ),
        out_specs=P(("req", "tp"), None),
        check_vma=False,
    )
```

```python
import functools
import math

import jax
import jax.numpy as jnp
from jax import lax
from jax.experimental import pallas as pl
from jax.experimental.pallas import tpu as pltpu
from jax.sharding import PartitionSpec as P

HEAD = 64
TOP = 2
CAP = 96


EPSILON = 1e-05


def normalize(inputs, scale_gain):
    mean_square = jnp.mean(inputs * inputs, axis=-1, keepdims=True)
    return inputs * lax.rsqrt(mean_square + EPSILON) * scale_gain


def rotate(inputs, positions):
    half_dim = inputs.shape[-1] // 2
    frequency = jnp.exp(
        jnp.arange(half_dim, dtype=jnp.float32) * (-2.0 * math.log(10000.0) / inputs.shape[-1])
    )
    angles = positions.astype(jnp.float32)[:, None] * frequency[None, :]
    cosine = jnp.cos(angles)[:, None, :]
    sine_part = jnp.sin(angles)[:, None, :]
    lower_half = inputs[..., :half_dim]
    upper_half = inputs[..., half_dim:]
    return jnp.concatenate(
        [
            lower_half * cosine - upper_half * sine_part,
            lower_half * sine_part + upper_half * cosine,
        ],
        axis=-1,
    )


def attention_kernel(
    length_ref, query_ref, key_ref, value_ref, fresh_key_ref, fresh_value_ref, out_ref, *, head_dim
):
    query_count = query_ref.shape[0]
    cache_len = key_ref.shape[1]
    length = length_ref[0]
    cache_live = lax.broadcasted_iota(jnp.int32, (query_count, cache_len), 1) < length
    fresh_live = lax.broadcasted_iota(
        jnp.int32, (query_count, query_count), 1
    ) <= lax.broadcasted_iota(jnp.int32, (query_count, query_count), 0)
    contract = (((1,), (1,)), ((), ()))
    for head in range(query_ref.shape[1] // head_dim):
        lanes = slice(head * head_dim, (head + 1) * head_dim)
        queries = query_ref[:, lanes]
        cache_scores = jnp.dot(
            queries, key_ref[lanes, :], preferred_element_type=jnp.float32
        ) * (head_dim ** -0.5)
        fresh_scores = jnp.dot(
            queries, fresh_key_ref[lanes, :], preferred_element_type=jnp.float32
        ) * (head_dim ** -0.5)
        cache_scores = jnp.where(cache_live, cache_scores, -jnp.inf)
        fresh_scores = jnp.where(fresh_live, fresh_scores, -jnp.inf)
        row_max = jnp.maximum(
            jnp.max(cache_scores, axis=1, keepdims=True),
            jnp.max(fresh_scores, axis=1, keepdims=True),
        )
        cache_weights = jnp.exp(cache_scores - row_max)
        fresh_weights = jnp.exp(fresh_scores - row_max)
        totals = jnp.sum(cache_weights, axis=1, keepdims=True) + jnp.sum(
            fresh_weights, axis=1, keepdims=True
        )
        mixture = lax.dot_general(
            cache_weights.astype(jnp.bfloat16),
            value_ref[lanes, :],
            contract,
            preferred_element_type=jnp.float32,
        ) + lax.dot_general(
            fresh_weights.astype(jnp.bfloat16),
            fresh_value_ref[lanes, :],
            contract,
            preferred_element_type=jnp.float32,
        )
        out_ref[:, lanes] = (mixture / totals).astype(out_ref.dtype)


def attention(queries, key_cache, value_cache, fresh_keys, fresh_values, length):
    vmem = pl.BlockSpec(memory_space=pltpu.VMEM)
    return pl.pallas_call(
        functools.partial(attention_kernel, head_dim=HEAD),
        out_shape=jax.ShapeDtypeStruct(queries.shape, jnp.bfloat16),
        in_specs=[pl.BlockSpec(memory_space=pltpu.SMEM)] + [vmem] * 5,
        out_specs=vmem,
    )(length, queries, key_cache.T, value_cache.T, fresh_keys.T, fresh_values.T)


def all_to_all_kernel(source_ref, target_ref, send_sems, recv_sems):
    count = source_ref.shape[0]
    me = lax.axis_index("req")
    tp_index = lax.axis_index("tp")
    barrier = pltpu.get_barrier_semaphore()
    for step in range(1, count):
        peer = lax.rem(me + step, count)
        pl.semaphore_signal(
            barrier, inc=1, device_id=(peer, tp_index), device_id_type=pl.DeviceIdType.MESH
        )
    pl.semaphore_wait(barrier, count - 1)
    local = pltpu.make_async_copy(source_ref.at[me], target_ref.at[me], send_sems.at[0])
    local.start()
    outgoing = []
    for step in range(1, count):
        peer = lax.rem(me + step, count)
        copy = pltpu.make_async_remote_copy(
            src_ref=source_ref.at[peer],
            dst_ref=target_ref.at[me],
            send_sem=send_sems.at[step],
            recv_sem=recv_sems.at[step],
            device_id=(peer, tp_index),
            device_id_type=pl.DeviceIdType.MESH,
        )
        copy.start()
        outgoing.append(copy)
    local.wait()
    for step in range(1, count):
        outgoing[step - 1].wait_send()
        origin = lax.rem(me + count - step, count)
        pltpu.make_async_remote_copy(
            src_ref=source_ref.at[origin],
            dst_ref=target_ref.at[origin],
            send_sem=send_sems.at[step],
            recv_sem=recv_sems.at[step],
            device_id=(origin, tp_index),
            device_id_type=pl.DeviceIdType.MESH,
        ).wait_recv()


def req_all_to_all(blocks, call_id):
    count = blocks.shape[0]
    return pl.pallas_call(
        all_to_all_kernel,
        out_shape=jax.ShapeDtypeStruct(blocks.shape, blocks.dtype),
        in_specs=[pl.BlockSpec(memory_space=pl.ANY)],
        out_specs=pl.BlockSpec(memory_space=pl.ANY),
        scratch_shapes=[pltpu.SemaphoreType.DMA((count,)), pltpu.SemaphoreType.DMA((count,))],
        compiler_params=pltpu.CompilerParams(collective_id=call_id, has_side_effects=True),
    )(blocks)


def tp_allreduce(partial):
    tp_size = lax.axis_size("tp")
    core = lax.axis_index("tp") % 2
    core_pairs = [(i, i ^ 1) for i in range(tp_size)]
    z_pairs = [(i, i ^ 2) for i in range(tp_size)]
    halves = partial.astype(jnp.bfloat16).reshape(2, partial.shape[0] // 2, partial.shape[1])
    keep = jnp.where(core == 0, halves[0], halves[1])
    send = jnp.where(core == 0, halves[1], halves[0])
    chip_sum = (
        keep.astype(jnp.float32) + lax.ppermute(send, "tp", core_pairs).astype(jnp.float32)
    ).astype(jnp.bfloat16)
    total = (
        chip_sum.astype(jnp.float32) + lax.ppermute(chip_sum, "tp", z_pairs).astype(jnp.float32)
    ).astype(jnp.bfloat16)
    other = lax.ppermute(total, "tp", core_pairs)
    return jnp.where(core == 0, jnp.concatenate([total, other]), jnp.concatenate([other, total]))


def tp_reduce_scatter(partial):
    tp_size = lax.axis_size("tp")
    tp_index = lax.axis_index("tp")
    core = tp_index % 2
    upper = tp_index // 2
    core_pairs = [(i, i ^ 1) for i in range(tp_size)]
    z_pairs = [(i, i ^ 2) for i in range(tp_size)]
    blocks = partial.astype(jnp.bfloat16).reshape(2, 2, partial.shape[0] // 4, partial.shape[1])
    keep = jnp.where(core == 0, blocks[:, 0], blocks[:, 1])
    send = jnp.where(core == 0, blocks[:, 1], blocks[:, 0])
    chip_sum = (
        keep.astype(jnp.float32) + lax.ppermute(send, "tp", core_pairs).astype(jnp.float32)
    ).astype(jnp.bfloat16)
    mine = jnp.where(upper == 0, chip_sum[0], chip_sum[1])
    theirs = jnp.where(upper == 0, chip_sum[1], chip_sum[0])
    return mine.astype(jnp.float32) + lax.ppermute(theirs, "tp", z_pairs).astype(jnp.float32)


def per_device(
    hidden_in,
    cache_lengths,
    key_cache,
    value_cache,
    attn_norm,
    w_qkv,
    w_out,
    ffn_norm,
    router,
    routes,
    expert_gate,
    expert_up,
    expert_down,
):
    token_count = hidden_in.shape[0]
    model_width = hidden_in.shape[1]
    local_lanes = w_qkv.shape[2]
    local_heads = local_lanes // HEAD
    cache_len = key_cache.shape[1]
    token_share = token_count // lax.axis_size("tp")
    offset = lax.axis_index("tp") * token_share
    expert_count = router.shape[1]
    copies = lax.axis_size("req") // expert_count
    residual = hidden_in.astype(jnp.float32)
    normed = normalize(residual, attn_norm).astype(jnp.bfloat16)
    projected = jnp.einsum("td,cdh->cth", normed, w_qkv, preferred_element_type=jnp.float32)
    length = cache_lengths[0]
    positions = length + jnp.arange(token_count, dtype=jnp.int32)
    queries = rotate(projected[0].reshape(token_count, local_heads, HEAD), positions).astype(
        jnp.bfloat16
    )
    fresh_keys = rotate(projected[1].reshape(token_count, local_heads, HEAD), positions).astype(
        jnp.bfloat16
    )
    fresh_values = projected[2].reshape(token_count, local_heads, HEAD).astype(jnp.bfloat16)
    attended = attention(
        queries.reshape(token_count, local_lanes),
        key_cache[0],
        value_cache[0],
        fresh_keys.reshape(token_count, local_lanes),
        fresh_values.reshape(token_count, local_lanes),
        cache_lengths,
    )
    summed_attn = tp_allreduce(
        jnp.dot(attended, w_out, preferred_element_type=jnp.float32)
    ).astype(jnp.float32)
    updated = residual + summed_attn
    moe_input = normalize(updated, ffn_norm).astype(jnp.bfloat16)
    own_residual = lax.dynamic_slice_in_dim(updated, offset, token_share, 0)
    logits = jnp.dot(moe_input, router, preferred_element_type=jnp.float32)
    chosen = jnp.take_along_axis(logits, routes, axis=1)
    first_gate = 1.0 / (1.0 + jnp.exp(chosen[:, 1] - chosen[:, 0]))
    second_gate = 1.0 / (1.0 + jnp.exp(chosen[:, 0] - chosen[:, 1]))
    flat_routes = routes.reshape(-1)
    onehot = (flat_routes[:, None] == jnp.arange(expert_count, dtype=jnp.int32)[None, :]).astype(
        jnp.int32
    )
    slot_rank = jnp.sum((jnp.cumsum(onehot, axis=0) - onehot) * onehot, axis=1)
    tp_size = lax.axis_size("tp")
    core = lax.axis_index("tp") % 2
    half_cap = CAP // 2
    pairs = [(i, i ^ 1) for i in range(tp_size)]
    gate_w = jnp.concatenate([expert_gate[0], lax.ppermute(expert_gate[0], "tp", pairs)], axis=1)
    up_w = jnp.concatenate([expert_up[0], lax.ppermute(expert_up[0], "tp", pairs)], axis=1)
    down_w = jnp.concatenate([expert_down[0], lax.ppermute(expert_down[0], "tp", pairs)], axis=0)
    local_rank = slot_rank - core * half_cap
    in_half = (local_rank >= 0) & (local_rank < half_cap)
    slot_ids = jnp.where(in_half, flat_routes * half_cap + local_rank, -1)
    paired = slot_ids.reshape(token_count, TOP)
    slot_range = jnp.arange(expert_count * half_cap, dtype=jnp.int32)
    chunk_count = 1
    chunk = half_cap // chunk_count
    chunk_results = []
    for index in range(chunk_count):
        chunk_ids = jnp.where(
            (local_rank >= index * chunk) & (local_rank < (index + 1) * chunk),
            flat_routes * chunk + local_rank - index * chunk,
            -1,
        ).reshape(token_count, TOP)
        chunk_range = jnp.arange(expert_count * chunk, dtype=jnp.int32)
        placing = jnp.any(chunk_ids[None, :, :] == chunk_range[:, None, None], axis=2).astype(
            jnp.bfloat16
        )
        packed = (
            jnp.dot(placing, moe_input, preferred_element_type=jnp.float32)
            .astype(jnp.bfloat16)
            .reshape(expert_count, chunk, model_width)
        )
        outgoing = jnp.broadcast_to(
            packed[:, None], (expert_count, copies, chunk, model_width)
        ).reshape(expert_count * copies, chunk, model_width)
        received = req_all_to_all(outgoing, 2 * index)
        token_rows = received.reshape(-1, model_width)
        gate_proj = jnp.dot(token_rows, gate_w, preferred_element_type=jnp.float32)
        up_proj = jnp.dot(token_rows, up_w, preferred_element_type=jnp.float32)
        activation = (jax.nn.silu(gate_proj) * up_proj).astype(jnp.bfloat16)
        partial_value = jnp.dot(
            activation, down_w, preferred_element_type=jnp.float32
        ).astype(jnp.bfloat16)
        returned = req_all_to_all(partial_value.reshape(received.shape), 2 * index + 1)
        chunk_results.append(
            jnp.sum(
                returned.reshape(expert_count, copies, chunk, model_width).astype(jnp.float32),
                axis=1,
            )
        )
    summed = jnp.concatenate(chunk_results, axis=1).reshape(expert_count * half_cap, model_width)
    gates = jnp.stack([first_gate, second_gate], axis=1)
    mixing = jnp.sum(
        jnp.where(paired[:, :, None] == slot_range[None, None, :], gates[:, :, None], 0.0), axis=1
    )
    local_sum = jnp.dot(mixing, summed, precision=lax.Precision.HIGHEST)
    moe_own = tp_reduce_scatter(local_sum)
    return (own_residual + moe_own).astype(jnp.bfloat16)


def solution(mesh):
    return jax.shard_map(
        per_device,
        mesh=mesh,
        in_specs=(
            P("req", None),
            P("req"),
            P("req", None, "tp"),
            P("req", None, "tp"),
            P(),
            P(None, None, "tp"),
            P("tp", None),
            P(),
            P(),
            P("req", None),
            P("req", None, "tp"),
            P("req", None, "tp"),
            P("req", "tp", None),
        ),
        out_specs=P(("req", "tp"), None),
        check_vma=False,
    )
```

```python
import functools
import math

import jax
import jax.numpy as jnp
from jax import lax
from jax.experimental import pallas as pl
from jax.experimental.pallas import tpu as pltpu
from jax.sharding import PartitionSpec as P

HEAD = 64
TOP = 2
CAP = 96


EPSILON = 1e-05


def normalize(inputs, scale_gain):
    mean_square = jnp.mean(inputs * inputs, axis=-1, keepdims=True)
    return inputs * lax.rsqrt(mean_square + EPSILON) * scale_gain


def rotate(inputs, positions):
    half_dim = inputs.shape[-1] // 2
    frequency = jnp.exp(
        jnp.arange(half_dim, dtype=jnp.float32) * (-2.0 * math.log(10000.0) / inputs.shape[-1])
    )
    angles = positions.astype(jnp.float32)[:, None] * frequency[None, :]
    cosine = jnp.cos(angles)[:, None, :]
    sine_part = jnp.sin(angles)[:, None, :]
    lower_half = inputs[..., :half_dim]
    upper_half = inputs[..., half_dim:]
    return jnp.concatenate(
        [
            lower_half * cosine - upper_half * sine_part,
            lower_half * sine_part + upper_half * cosine,
        ],
        axis=-1,
    )


def attention_kernel(
    length_ref, query_ref, key_ref, value_ref, fresh_key_ref, fresh_value_ref, out_ref, *, head_dim
):
    query_count = query_ref.shape[0]
    cache_len = key_ref.shape[1]
    length = length_ref[0]
    cache_live = lax.broadcasted_iota(jnp.int32, (query_count, cache_len), 1) < length
    fresh_live = lax.broadcasted_iota(
        jnp.int32, (query_count, query_count), 1
    ) <= lax.broadcasted_iota(jnp.int32, (query_count, query_count), 0)
    contract = (((1,), (1,)), ((), ()))
    for head in range(query_ref.shape[1] // head_dim):
        lanes = slice(head * head_dim, (head + 1) * head_dim)
        queries = query_ref[:, lanes]
        cache_scores = jnp.dot(
            queries, key_ref[lanes, :], preferred_element_type=jnp.float32
        ) * (head_dim ** -0.5)
        fresh_scores = jnp.dot(
            queries, fresh_key_ref[lanes, :], preferred_element_type=jnp.float32
        ) * (head_dim ** -0.5)
        cache_scores = jnp.where(cache_live, cache_scores, -jnp.inf)
        fresh_scores = jnp.where(fresh_live, fresh_scores, -jnp.inf)
        row_max = jnp.maximum(
            jnp.max(cache_scores, axis=1, keepdims=True),
            jnp.max(fresh_scores, axis=1, keepdims=True),
        )
        cache_weights = jnp.exp(cache_scores - row_max)
        fresh_weights = jnp.exp(fresh_scores - row_max)
        totals = jnp.sum(cache_weights, axis=1, keepdims=True) + jnp.sum(
            fresh_weights, axis=1, keepdims=True
        )
        mixture = lax.dot_general(
            cache_weights.astype(jnp.bfloat16),
            value_ref[lanes, :],
            contract,
            preferred_element_type=jnp.float32,
        ) + lax.dot_general(
            fresh_weights.astype(jnp.bfloat16),
            fresh_value_ref[lanes, :],
            contract,
            preferred_element_type=jnp.float32,
        )
        out_ref[:, lanes] = (mixture / totals).astype(out_ref.dtype)


def attention(queries, key_cache, value_cache, fresh_keys, fresh_values, length):
    vmem = pl.BlockSpec(memory_space=pltpu.VMEM)
    return pl.pallas_call(
        functools.partial(attention_kernel, head_dim=HEAD),
        out_shape=jax.ShapeDtypeStruct(queries.shape, jnp.bfloat16),
        in_specs=[pl.BlockSpec(memory_space=pltpu.SMEM)] + [vmem] * 5,
        out_specs=vmem,
    )(length, queries, key_cache.T, value_cache.T, fresh_keys.T, fresh_values.T)


def tp_allreduce(partial):
    tp_size = lax.axis_size("tp")
    core = lax.axis_index("tp") % 2
    core_pairs = [(i, i ^ 1) for i in range(tp_size)]
    z_pairs = [(i, i ^ 2) for i in range(tp_size)]
    halves = partial.astype(jnp.bfloat16).reshape(2, partial.shape[0] // 2, partial.shape[1])
    keep = jnp.where(core == 0, halves[0], halves[1])
    send = jnp.where(core == 0, halves[1], halves[0])
    chip_sum = (
        keep.astype(jnp.float32) + lax.ppermute(send, "tp", core_pairs).astype(jnp.float32)
    ).astype(jnp.bfloat16)
    total = (
        chip_sum.astype(jnp.float32) + lax.ppermute(chip_sum, "tp", z_pairs).astype(jnp.float32)
    ).astype(jnp.bfloat16)
    other = lax.ppermute(total, "tp", core_pairs)
    return jnp.where(core == 0, jnp.concatenate([total, other]), jnp.concatenate([other, total]))


def tp_reduce_scatter(partial):
    tp_size = lax.axis_size("tp")
    tp_index = lax.axis_index("tp")
    core = tp_index % 2
    upper = tp_index // 2
    core_pairs = [(i, i ^ 1) for i in range(tp_size)]
    z_pairs = [(i, i ^ 2) for i in range(tp_size)]
    blocks = partial.astype(jnp.bfloat16).reshape(2, 2, partial.shape[0] // 4, partial.shape[1])
    keep = jnp.where(core == 0, blocks[:, 0], blocks[:, 1])
    send = jnp.where(core == 0, blocks[:, 1], blocks[:, 0])
    chip_sum = (
        keep.astype(jnp.float32) + lax.ppermute(send, "tp", core_pairs).astype(jnp.float32)
    ).astype(jnp.bfloat16)
    mine = jnp.where(upper == 0, chip_sum[0], chip_sum[1])
    theirs = jnp.where(upper == 0, chip_sum[1], chip_sum[0])
    return mine.astype(jnp.float32) + lax.ppermute(theirs, "tp", z_pairs).astype(jnp.float32)


def per_device(
    hidden_in,
    cache_lengths,
    key_cache,
    value_cache,
    attn_norm,
    w_qkv,
    w_out,
    ffn_norm,
    router,
    routes,
    expert_gate,
    expert_up,
    expert_down,
):
    token_count = hidden_in.shape[0]
    model_width = hidden_in.shape[1]
    local_lanes = w_qkv.shape[2]
    local_heads = local_lanes // HEAD
    cache_len = key_cache.shape[1]
    token_share = token_count // lax.axis_size("tp")
    offset = lax.axis_index("tp") * token_share
    expert_count = router.shape[1]
    residual = hidden_in.astype(jnp.float32)
    normed = normalize(residual, attn_norm).astype(jnp.bfloat16)
    projected = jnp.einsum("td,cdh->cth", normed, w_qkv, preferred_element_type=jnp.float32)
    length = cache_lengths[0]
    positions = length + jnp.arange(token_count, dtype=jnp.int32)
    queries = rotate(projected[0].reshape(token_count, local_heads, HEAD), positions).astype(
        jnp.bfloat16
    )
    fresh_keys = rotate(projected[1].reshape(token_count, local_heads, HEAD), positions).astype(
        jnp.bfloat16
    )
    fresh_values = projected[2].reshape(token_count, local_heads, HEAD).astype(jnp.bfloat16)
    attended = attention(
        queries.reshape(token_count, local_lanes),
        key_cache[0],
        value_cache[0],
        fresh_keys.reshape(token_count, local_lanes),
        fresh_values.reshape(token_count, local_lanes),
        cache_lengths,
    )
    summed_attn = tp_allreduce(
        jnp.dot(attended, w_out, preferred_element_type=jnp.float32)
    ).astype(jnp.float32)
    updated = residual + summed_attn
    moe_input = normalize(updated, ffn_norm).astype(jnp.bfloat16)
    own_residual = lax.dynamic_slice_in_dim(updated, offset, token_share, 0)
    logits = jnp.dot(moe_input, router, preferred_element_type=jnp.float32)
    chosen = jnp.take_along_axis(logits, routes, axis=1)
    first_gate = 1.0 / (1.0 + jnp.exp(chosen[:, 1] - chosen[:, 0]))
    second_gate = 1.0 / (1.0 + jnp.exp(chosen[:, 0] - chosen[:, 1]))
    flat_routes = routes.reshape(-1)
    onehot = (flat_routes[:, None] == jnp.arange(expert_count, dtype=jnp.int32)[None, :]).astype(
        jnp.int32
    )
    slot_rank = jnp.sum((jnp.cumsum(onehot, axis=0) - onehot) * onehot, axis=1)
    tp_size = lax.axis_size("tp")
    core = lax.axis_index("tp") % 2
    half_cap = CAP // 2
    pairs = [(i, i ^ 1) for i in range(tp_size)]
    gate_w = jnp.concatenate([expert_gate[0], lax.ppermute(expert_gate[0], "tp", pairs)], axis=1)
    up_w = jnp.concatenate([expert_up[0], lax.ppermute(expert_up[0], "tp", pairs)], axis=1)
    down_w = jnp.concatenate([expert_down[0], lax.ppermute(expert_down[0], "tp", pairs)], axis=0)
    local_rank = slot_rank - core * half_cap
    in_half = (local_rank >= 0) & (local_rank < half_cap)
    slot_ids = jnp.where(in_half, flat_routes * half_cap + local_rank, -1)
    paired = slot_ids.reshape(token_count, TOP)
    slot_range = jnp.arange(expert_count * half_cap, dtype=jnp.int32)
    chunk_count = 2
    chunk = half_cap // chunk_count
    ring = lax.axis_size("x")
    plus = [(i, (i + 1) % ring) for i in range(ring)]
    minus = [(i, (i - 1) % ring) for i in range(ring)]
    split = expert_count // 2
    chunk_results = []
    for index in range(chunk_count):
        chunk_ids = jnp.where(
            (local_rank >= index * chunk) & (local_rank < (index + 1) * chunk),
            flat_routes * chunk + local_rank - index * chunk,
            -1,
        ).reshape(token_count, TOP)
        chunk_range = jnp.arange(expert_count * chunk, dtype=jnp.int32)
        placing = jnp.any(chunk_ids[None, :, :] == chunk_range[:, None, None], axis=2).astype(
            jnp.bfloat16
        )
        packed = (
            jnp.dot(placing, moe_input, preferred_element_type=jnp.float32)
            .astype(jnp.bfloat16)
            .reshape(expert_count, chunk, model_width)
        )
        own = lax.all_to_all(packed, "grp", split_axis=0, concat_axis=0, tiled=True)
        from_left = lax.ppermute(own, "x", plus)
        from_right = lax.ppermute(own, "x", minus)
        from_far = jnp.concatenate(
            [lax.ppermute(from_left[:split], "x", plus), lax.ppermute(from_right[split:], "x", minus)]
        )
        received = jnp.stack([own, from_left, from_right, from_far])
        token_rows = received.reshape(-1, model_width)
        gate_proj = jnp.dot(token_rows, gate_w, preferred_element_type=jnp.float32)
        up_proj = jnp.dot(token_rows, up_w, preferred_element_type=jnp.float32)
        activation = (jax.nn.silu(gate_proj) * up_proj).astype(jnp.bfloat16)
        partial_value = jnp.dot(
            activation, down_w, preferred_element_type=jnp.float32
        ).astype(jnp.bfloat16).reshape(received.shape)
        far_a = lax.ppermute(partial_value[3, :split], "x", plus)
        far_b = lax.ppermute(partial_value[3, split:], "x", minus)
        to_right = partial_value[2].astype(jnp.float32)
        to_right = jnp.concatenate([to_right[:split] + far_a.astype(jnp.float32), to_right[split:]])
        to_left = partial_value[1].astype(jnp.float32)
        to_left = jnp.concatenate([to_left[:split], to_left[split:] + far_b.astype(jnp.float32)])
        at_x = (
            partial_value[0].astype(jnp.float32)
            + lax.ppermute(to_right.astype(jnp.bfloat16), "x", plus).astype(jnp.float32)
            + lax.ppermute(to_left.astype(jnp.bfloat16), "x", minus).astype(jnp.float32)
        ).astype(jnp.bfloat16)
        returned = lax.all_to_all(at_x, "grp", split_axis=0, concat_axis=0, tiled=True)
        chunk_results.append(returned.astype(jnp.float32))
    summed = jnp.concatenate(chunk_results, axis=1).reshape(expert_count * half_cap, model_width)
    gates = jnp.stack([first_gate, second_gate], axis=1)
    mixing = jnp.sum(
        jnp.where(paired[:, :, None] == slot_range[None, None, :], gates[:, :, None], 0.0), axis=1
    )
    local_sum = jnp.dot(mixing, summed, precision=lax.Precision.HIGHEST)
    moe_own = tp_reduce_scatter(local_sum)
    return (own_residual + moe_own).astype(jnp.bfloat16)


REQ = ("grp", "x")


def solution(mesh):
    def run(*args):
        experts = args[8].shape[1]
        copies = mesh.shape["req"] // experts
        fine = jax.sharding.Mesh(
            mesh.devices.reshape(experts, copies, mesh.shape["tp"]), ("grp", "x", "tp")
        )
        return sharded(fine)(*args)

    return run


def sharded(fine):
    return jax.shard_map(
        per_device,
        mesh=fine,
        in_specs=(
            P(REQ, None),
            P(REQ),
            P(REQ, None, "tp"),
            P(REQ, None, "tp"),
            P(),
            P(None, None, "tp"),
            P("tp", None),
            P(),
            P(),
            P(REQ, None),
            P(REQ, None, "tp"),
            P(REQ, None, "tp"),
            P(REQ, "tp", None),
        ),
        out_specs=P((*REQ, "tp"), None),
        check_vma=False,
    )
```

```python
import functools
import math

import jax
import jax.numpy as jnp
from jax import lax
from jax.experimental import pallas as pl
from jax.experimental.pallas import tpu as pltpu
from jax.sharding import PartitionSpec as P

HEAD = 64
TOP = 2
CAP = 96


EPSILON = 1e-05


def normalize(inputs, scale_gain):
    mean_square = jnp.mean(inputs * inputs, axis=-1, keepdims=True)
    return inputs * lax.rsqrt(mean_square + EPSILON) * scale_gain


def rotate(inputs, positions):
    half_dim = inputs.shape[-1] // 2
    frequency = jnp.exp(
        jnp.arange(half_dim, dtype=jnp.float32) * (-2.0 * math.log(10000.0) / inputs.shape[-1])
    )
    angles = positions.astype(jnp.float32)[:, None] * frequency[None, :]
    cosine = jnp.cos(angles)[:, None, :]
    sine_part = jnp.sin(angles)[:, None, :]
    lower_half = inputs[..., :half_dim]
    upper_half = inputs[..., half_dim:]
    return jnp.concatenate(
        [
            lower_half * cosine - upper_half * sine_part,
            lower_half * sine_part + upper_half * cosine,
        ],
        axis=-1,
    )


def attention_kernel(
    length_ref, query_ref, key_ref, value_ref, fresh_key_ref, fresh_value_ref, out_ref, *, head_dim
):
    query_count = query_ref.shape[0]
    cache_len = key_ref.shape[1]
    length = length_ref[0]
    cache_live = lax.broadcasted_iota(jnp.int32, (query_count, cache_len), 1) < length
    fresh_live = lax.broadcasted_iota(
        jnp.int32, (query_count, query_count), 1
    ) <= lax.broadcasted_iota(jnp.int32, (query_count, query_count), 0)
    contract = (((1,), (1,)), ((), ()))
    for head in range(query_ref.shape[1] // head_dim):
        lanes = slice(head * head_dim, (head + 1) * head_dim)
        queries = query_ref[:, lanes]
        cache_scores = jnp.dot(
            queries, key_ref[lanes, :], preferred_element_type=jnp.float32
        ) * (head_dim ** -0.5)
        fresh_scores = jnp.dot(
            queries, fresh_key_ref[lanes, :], preferred_element_type=jnp.float32
        ) * (head_dim ** -0.5)
        cache_scores = jnp.where(cache_live, cache_scores, -jnp.inf)
        fresh_scores = jnp.where(fresh_live, fresh_scores, -jnp.inf)
        row_max = jnp.maximum(
            jnp.max(cache_scores, axis=1, keepdims=True),
            jnp.max(fresh_scores, axis=1, keepdims=True),
        )
        cache_weights = jnp.exp(cache_scores - row_max)
        fresh_weights = jnp.exp(fresh_scores - row_max)
        totals = jnp.sum(cache_weights, axis=1, keepdims=True) + jnp.sum(
            fresh_weights, axis=1, keepdims=True
        )
        mixture = lax.dot_general(
            cache_weights.astype(jnp.bfloat16),
            value_ref[lanes, :],
            contract,
            preferred_element_type=jnp.float32,
        ) + lax.dot_general(
            fresh_weights.astype(jnp.bfloat16),
            fresh_value_ref[lanes, :],
            contract,
            preferred_element_type=jnp.float32,
        )
        out_ref[:, lanes] = (mixture / totals).astype(out_ref.dtype)


def attention(queries, key_cache, value_cache, fresh_keys, fresh_values, length):
    vmem = pl.BlockSpec(memory_space=pltpu.VMEM)
    return pl.pallas_call(
        functools.partial(attention_kernel, head_dim=HEAD),
        out_shape=jax.ShapeDtypeStruct(queries.shape, jnp.bfloat16),
        in_specs=[pl.BlockSpec(memory_space=pltpu.SMEM)] + [vmem] * 5,
        out_specs=vmem,
    )(length, queries, key_cache.T, value_cache.T, fresh_keys.T, fresh_values.T)


def tp_allreduce(partial):
    tp_size = lax.axis_size("tp")
    core = lax.axis_index("tp") % 2
    core_pairs = [(i, i ^ 1) for i in range(tp_size)]
    z_pairs = [(i, i ^ 2) for i in range(tp_size)]
    halves = partial.astype(jnp.bfloat16).reshape(2, partial.shape[0] // 2, partial.shape[1])
    keep = jnp.where(core == 0, halves[0], halves[1])
    send = jnp.where(core == 0, halves[1], halves[0])
    chip_sum = (
        keep.astype(jnp.float32) + lax.ppermute(send, "tp", core_pairs).astype(jnp.float32)
    ).astype(jnp.bfloat16)
    total = (
        chip_sum.astype(jnp.float32) + lax.ppermute(chip_sum, "tp", z_pairs).astype(jnp.float32)
    ).astype(jnp.bfloat16)
    other = lax.ppermute(total, "tp", core_pairs)
    return jnp.where(core == 0, jnp.concatenate([total, other]), jnp.concatenate([other, total]))


def tp_reduce_scatter(partial):
    tp_size = lax.axis_size("tp")
    tp_index = lax.axis_index("tp")
    core = tp_index % 2
    upper = tp_index // 2
    core_pairs = [(i, i ^ 1) for i in range(tp_size)]
    z_pairs = [(i, i ^ 2) for i in range(tp_size)]
    blocks = partial.astype(jnp.bfloat16).reshape(2, 2, partial.shape[0] // 4, partial.shape[1])
    keep = jnp.where(core == 0, blocks[:, 0], blocks[:, 1])
    send = jnp.where(core == 0, blocks[:, 1], blocks[:, 0])
    chip_sum = (
        keep.astype(jnp.float32) + lax.ppermute(send, "tp", core_pairs).astype(jnp.float32)
    ).astype(jnp.bfloat16)
    mine = jnp.where(upper == 0, chip_sum[0], chip_sum[1])
    theirs = jnp.where(upper == 0, chip_sum[1], chip_sum[0])
    return mine.astype(jnp.float32) + lax.ppermute(theirs, "tp", z_pairs).astype(jnp.float32)


def per_device(
    hidden_in,
    cache_lengths,
    key_cache,
    value_cache,
    attn_norm,
    w_qkv,
    w_out,
    ffn_norm,
    router,
    routes,
    expert_gate,
    expert_up,
    expert_down,
):
    token_count = hidden_in.shape[0]
    model_width = hidden_in.shape[1]
    local_lanes = w_qkv.shape[2]
    local_heads = local_lanes // HEAD
    cache_len = key_cache.shape[1]
    token_share = token_count // lax.axis_size("tp")
    offset = lax.axis_index("tp") * token_share
    expert_count = router.shape[1]
    residual = hidden_in.astype(jnp.float32)
    normed = normalize(residual, attn_norm).astype(jnp.bfloat16)
    projected = jnp.einsum("td,cdh->cth", normed, w_qkv, preferred_element_type=jnp.float32)
    length = cache_lengths[0]
    positions = length + jnp.arange(token_count, dtype=jnp.int32)
    queries = rotate(projected[0].reshape(token_count, local_heads, HEAD), positions).astype(
        jnp.bfloat16
    )
    fresh_keys = rotate(projected[1].reshape(token_count, local_heads, HEAD), positions).astype(
        jnp.bfloat16
    )
    fresh_values = projected[2].reshape(token_count, local_heads, HEAD).astype(jnp.bfloat16)
    attended = attention(
        queries.reshape(token_count, local_lanes),
        key_cache[0],
        value_cache[0],
        fresh_keys.reshape(token_count, local_lanes),
        fresh_values.reshape(token_count, local_lanes),
        cache_lengths,
    )
    summed_attn = tp_allreduce(
        jnp.dot(attended, w_out, preferred_element_type=jnp.float32)
    ).astype(jnp.float32)
    updated = residual + summed_attn
    moe_input = normalize(updated, ffn_norm).astype(jnp.bfloat16)
    own_residual = lax.dynamic_slice_in_dim(updated, offset, token_share, 0)
    logits = jnp.dot(moe_input, router, preferred_element_type=jnp.float32)
    chosen = jnp.take_along_axis(logits, routes, axis=1)
    first_gate = 1.0 / (1.0 + jnp.exp(chosen[:, 1] - chosen[:, 0]))
    second_gate = 1.0 / (1.0 + jnp.exp(chosen[:, 0] - chosen[:, 1]))
    flat_routes = routes.reshape(-1)
    onehot = (flat_routes[:, None] == jnp.arange(expert_count, dtype=jnp.int32)[None, :]).astype(
        jnp.int32
    )
    slot_rank = jnp.sum((jnp.cumsum(onehot, axis=0) - onehot) * onehot, axis=1)
    tp_size = lax.axis_size("tp")
    core = lax.axis_index("tp") % 2
    half_cap = CAP // 2
    pairs = [(i, i ^ 1) for i in range(tp_size)]
    gate_w = jnp.concatenate([expert_gate[0], lax.ppermute(expert_gate[0], "tp", pairs)], axis=1)
    up_w = jnp.concatenate([expert_up[0], lax.ppermute(expert_up[0], "tp", pairs)], axis=1)
    down_w = jnp.concatenate([expert_down[0], lax.ppermute(expert_down[0], "tp", pairs)], axis=0)
    local_rank = slot_rank - core * half_cap
    in_half = (local_rank >= 0) & (local_rank < half_cap)
    slot_ids = jnp.where(in_half, flat_routes * half_cap + local_rank, -1)
    paired = slot_ids.reshape(token_count, TOP)
    slot_range = jnp.arange(expert_count * half_cap, dtype=jnp.int32)
    chunk_count = 1
    chunk = half_cap // chunk_count
    ring = lax.axis_size("x")
    plus = [(i, (i + 1) % ring) for i in range(ring)]
    minus = [(i, (i - 1) % ring) for i in range(ring)]
    split = expert_count // 2

    def expert_ffn(rows):
        flat = rows.reshape(-1, model_width)
        gate_proj = jnp.dot(flat, gate_w, preferred_element_type=jnp.float32)
        up_proj = jnp.dot(flat, up_w, preferred_element_type=jnp.float32)
        activation = (jax.nn.silu(gate_proj) * up_proj).astype(jnp.bfloat16)
        return jnp.dot(activation, down_w, preferred_element_type=jnp.float32).astype(
            jnp.bfloat16
        ).reshape(rows.shape)

    chunk_results = []
    for index in range(chunk_count):
        chunk_ids = jnp.where(
            (local_rank >= index * chunk) & (local_rank < (index + 1) * chunk),
            flat_routes * chunk + local_rank - index * chunk,
            -1,
        ).reshape(token_count, TOP)
        chunk_range = jnp.arange(expert_count * chunk, dtype=jnp.int32)
        placing = jnp.any(chunk_ids[None, :, :] == chunk_range[:, None, None], axis=2).astype(
            jnp.bfloat16
        )
        packed = (
            jnp.dot(placing, moe_input, preferred_element_type=jnp.float32)
            .astype(jnp.bfloat16)
            .reshape(expert_count, chunk, model_width)
        )
        own = lax.all_to_all(packed, "grp", split_axis=0, concat_axis=0, tiled=True)
        from_left = lax.ppermute(own, "x", plus)
        from_right = lax.ppermute(own, "x", minus)
        from_far = jnp.concatenate(
            [lax.ppermute(from_left[:split], "x", plus), lax.ppermute(from_right[split:], "x", minus)]
        )
        own_out = expert_ffn(own)
        left_out = expert_ffn(from_left)
        right_out = expert_ffn(from_right)
        far_out = expert_ffn(from_far)
        far_a = lax.ppermute(lax.ppermute(far_out[:split], "x", plus), "x", plus)
        far_b = lax.ppermute(lax.ppermute(far_out[split:], "x", minus), "x", minus)
        at_x = (
            own_out.astype(jnp.float32)
            + lax.ppermute(right_out, "x", plus).astype(jnp.float32)
            + lax.ppermute(left_out, "x", minus).astype(jnp.float32)
            + jnp.concatenate([far_a, far_b]).astype(jnp.float32)
        ).astype(jnp.bfloat16)
        returned = lax.all_to_all(at_x, "grp", split_axis=0, concat_axis=0, tiled=True)
        chunk_results.append(returned.astype(jnp.float32))
    summed = jnp.concatenate(chunk_results, axis=1).reshape(expert_count * half_cap, model_width)
    gates = jnp.stack([first_gate, second_gate], axis=1)
    mixing = jnp.sum(
        jnp.where(paired[:, :, None] == slot_range[None, None, :], gates[:, :, None], 0.0), axis=1
    )
    local_sum = jnp.dot(mixing, summed, precision=lax.Precision.HIGHEST)
    moe_own = tp_reduce_scatter(local_sum)
    return (own_residual + moe_own).astype(jnp.bfloat16)


REQ = ("grp", "x")


def solution(mesh):
    def run(*args):
        experts = args[8].shape[1]
        copies = mesh.shape["req"] // experts
        fine = jax.sharding.Mesh(
            mesh.devices.reshape(experts, copies, mesh.shape["tp"]), ("grp", "x", "tp")
        )
        return sharded(fine)(*args)

    return run


def sharded(fine):
    return jax.shard_map(
        per_device,
        mesh=fine,
        in_specs=(
            P(REQ, None),
            P(REQ),
            P(REQ, None, "tp"),
            P(REQ, None, "tp"),
            P(),
            P(None, None, "tp"),
            P("tp", None),
            P(),
            P(),
            P(REQ, None),
            P(REQ, None, "tp"),
            P(REQ, None, "tp"),
            P(REQ, "tp", None),
        ),
        out_specs=P((*REQ, "tp"), None),
        check_vma=False,
    )
```

```python
import functools
import math

import jax
import jax.numpy as jnp
from jax import lax
from jax.experimental import pallas as pl
from jax.experimental.pallas import tpu as pltpu
from jax.sharding import PartitionSpec as P

HEAD = 64
TOP = 2
CAP = 96


EPSILON = 1e-05


def normalize(inputs, scale_gain):
    mean_square = jnp.mean(inputs * inputs, axis=-1, keepdims=True)
    return inputs * lax.rsqrt(mean_square + EPSILON) * scale_gain


def rotate(inputs, positions):
    half_dim = inputs.shape[-1] // 2
    frequency = jnp.exp(
        jnp.arange(half_dim, dtype=jnp.float32) * (-2.0 * math.log(10000.0) / inputs.shape[-1])
    )
    angles = positions.astype(jnp.float32)[:, None] * frequency[None, :]
    cosine = jnp.cos(angles)[:, None, :]
    sine_part = jnp.sin(angles)[:, None, :]
    lower_half = inputs[..., :half_dim]
    upper_half = inputs[..., half_dim:]
    return jnp.concatenate(
        [
            lower_half * cosine - upper_half * sine_part,
            lower_half * sine_part + upper_half * cosine,
        ],
        axis=-1,
    )


def attention_kernel(
    length_ref, query_ref, key_ref, value_ref, fresh_key_ref, fresh_value_ref, out_ref, *, head_dim
):
    query_count = query_ref.shape[0]
    cache_len = key_ref.shape[1]
    length = length_ref[0]
    cache_live = lax.broadcasted_iota(jnp.int32, (query_count, cache_len), 1) < length
    fresh_live = lax.broadcasted_iota(
        jnp.int32, (query_count, query_count), 1
    ) <= lax.broadcasted_iota(jnp.int32, (query_count, query_count), 0)
    contract = (((1,), (1,)), ((), ()))
    for head in range(query_ref.shape[1] // head_dim):
        lanes = slice(head * head_dim, (head + 1) * head_dim)
        queries = query_ref[:, lanes]
        cache_scores = jnp.dot(
            queries, key_ref[lanes, :], preferred_element_type=jnp.float32
        ) * (head_dim ** -0.5)
        fresh_scores = jnp.dot(
            queries, fresh_key_ref[lanes, :], preferred_element_type=jnp.float32
        ) * (head_dim ** -0.5)
        cache_scores = jnp.where(cache_live, cache_scores, -jnp.inf)
        fresh_scores = jnp.where(fresh_live, fresh_scores, -jnp.inf)
        row_max = jnp.maximum(
            jnp.max(cache_scores, axis=1, keepdims=True),
            jnp.max(fresh_scores, axis=1, keepdims=True),
        )
        cache_weights = jnp.exp(cache_scores - row_max)
        fresh_weights = jnp.exp(fresh_scores - row_max)
        totals = jnp.sum(cache_weights, axis=1, keepdims=True) + jnp.sum(
            fresh_weights, axis=1, keepdims=True
        )
        mixture = lax.dot_general(
            cache_weights.astype(jnp.bfloat16),
            value_ref[lanes, :],
            contract,
            preferred_element_type=jnp.float32,
        ) + lax.dot_general(
            fresh_weights.astype(jnp.bfloat16),
            fresh_value_ref[lanes, :],
            contract,
            preferred_element_type=jnp.float32,
        )
        out_ref[:, lanes] = (mixture / totals).astype(out_ref.dtype)


def attention(queries, key_cache, value_cache, fresh_keys, fresh_values, length):
    vmem = pl.BlockSpec(memory_space=pltpu.VMEM)
    return pl.pallas_call(
        functools.partial(attention_kernel, head_dim=HEAD),
        out_shape=jax.ShapeDtypeStruct(queries.shape, jnp.bfloat16),
        in_specs=[pl.BlockSpec(memory_space=pltpu.SMEM)] + [vmem] * 5,
        out_specs=vmem,
    )(length, queries, key_cache.T, value_cache.T, fresh_keys.T, fresh_values.T)


def tp_allreduce(partial):
    tp_size = lax.axis_size("tp")
    core = lax.axis_index("tp") % 2
    core_pairs = [(i, i ^ 1) for i in range(tp_size)]
    z_pairs = [(i, i ^ 2) for i in range(tp_size)]
    halves = partial.astype(jnp.bfloat16).reshape(2, partial.shape[0] // 2, partial.shape[1])
    keep = jnp.where(core == 0, halves[0], halves[1])
    send = jnp.where(core == 0, halves[1], halves[0])
    chip_sum = (
        keep.astype(jnp.float32) + lax.ppermute(send, "tp", core_pairs).astype(jnp.float32)
    ).astype(jnp.bfloat16)
    total = (
        chip_sum.astype(jnp.float32) + lax.ppermute(chip_sum, "tp", z_pairs).astype(jnp.float32)
    ).astype(jnp.bfloat16)
    other = lax.ppermute(total, "tp", core_pairs)
    return jnp.where(core == 0, jnp.concatenate([total, other]), jnp.concatenate([other, total]))


def tp_reduce_scatter(partial):
    tp_size = lax.axis_size("tp")
    tp_index = lax.axis_index("tp")
    core = tp_index % 2
    upper = tp_index // 2
    core_pairs = [(i, i ^ 1) for i in range(tp_size)]
    z_pairs = [(i, i ^ 2) for i in range(tp_size)]
    blocks = partial.astype(jnp.bfloat16).reshape(2, 2, partial.shape[0] // 4, partial.shape[1])
    keep = jnp.where(core == 0, blocks[:, 0], blocks[:, 1])
    send = jnp.where(core == 0, blocks[:, 1], blocks[:, 0])
    chip_sum = (
        keep.astype(jnp.float32) + lax.ppermute(send, "tp", core_pairs).astype(jnp.float32)
    ).astype(jnp.bfloat16)
    mine = jnp.where(upper == 0, chip_sum[0], chip_sum[1])
    theirs = jnp.where(upper == 0, chip_sum[1], chip_sum[0])
    return mine.astype(jnp.float32) + lax.ppermute(theirs, "tp", z_pairs).astype(jnp.float32)


def per_device(
    hidden_in,
    cache_lengths,
    key_cache,
    value_cache,
    attn_norm,
    w_qkv,
    w_out,
    ffn_norm,
    router,
    routes,
    expert_gate,
    expert_up,
    expert_down,
):
    token_count = hidden_in.shape[0]
    model_width = hidden_in.shape[1]
    local_lanes = w_qkv.shape[2]
    local_heads = local_lanes // HEAD
    cache_len = key_cache.shape[1]
    token_share = token_count // lax.axis_size("tp")
    offset = lax.axis_index("tp") * token_share
    expert_count = router.shape[1]
    residual = hidden_in.astype(jnp.float32)
    normed = normalize(residual, attn_norm).astype(jnp.bfloat16)
    projected = jnp.einsum("td,cdh->cth", normed, w_qkv, preferred_element_type=jnp.float32)
    length = cache_lengths[0]
    positions = length + jnp.arange(token_count, dtype=jnp.int32)
    queries = rotate(projected[0].reshape(token_count, local_heads, HEAD), positions).astype(
        jnp.bfloat16
    )
    fresh_keys = rotate(projected[1].reshape(token_count, local_heads, HEAD), positions).astype(
        jnp.bfloat16
    )
    fresh_values = projected[2].reshape(token_count, local_heads, HEAD).astype(jnp.bfloat16)
    attended = attention(
        queries.reshape(token_count, local_lanes),
        key_cache[0],
        value_cache[0],
        fresh_keys.reshape(token_count, local_lanes),
        fresh_values.reshape(token_count, local_lanes),
        cache_lengths,
    )
    summed_attn = tp_allreduce(
        jnp.dot(attended, w_out, preferred_element_type=jnp.float32)
    ).astype(jnp.float32)
    updated = residual + summed_attn
    moe_input = normalize(updated, ffn_norm).astype(jnp.bfloat16)
    own_residual = lax.dynamic_slice_in_dim(updated, offset, token_share, 0)
    logits = jnp.dot(moe_input, router, preferred_element_type=jnp.float32)
    chosen = jnp.take_along_axis(logits, routes, axis=1)
    first_gate = 1.0 / (1.0 + jnp.exp(chosen[:, 1] - chosen[:, 0]))
    second_gate = 1.0 / (1.0 + jnp.exp(chosen[:, 0] - chosen[:, 1]))
    flat_routes = routes.reshape(-1)
    onehot = (flat_routes[:, None] == jnp.arange(expert_count, dtype=jnp.int32)[None, :]).astype(
        jnp.int32
    )
    slot_rank = jnp.sum((jnp.cumsum(onehot, axis=0) - onehot) * onehot, axis=1)
    tp_size = lax.axis_size("tp")
    core = lax.axis_index("tp") % 2
    half_cap = CAP // 2
    pairs = [(i, i ^ 1) for i in range(tp_size)]
    gate_w = jnp.concatenate([expert_gate[0], lax.ppermute(expert_gate[0], "tp", pairs)], axis=1)
    up_w = jnp.concatenate([expert_up[0], lax.ppermute(expert_up[0], "tp", pairs)], axis=1)
    down_w = jnp.concatenate([expert_down[0], lax.ppermute(expert_down[0], "tp", pairs)], axis=0)
    local_rank = slot_rank - core * half_cap
    in_half = (local_rank >= 0) & (local_rank < half_cap)
    slot_ids = jnp.where(in_half, flat_routes * half_cap + local_rank, -1)
    paired = slot_ids.reshape(token_count, TOP)
    slot_range = jnp.arange(expert_count * half_cap, dtype=jnp.int32)
    chunk_count = 2
    chunk = half_cap // chunk_count
    ring = lax.axis_size("x")
    plus = [(i, (i + 1) % ring) for i in range(ring)]
    minus = [(i, (i - 1) % ring) for i in range(ring)]
    split = expert_count // 2

    def gate_up(rows):
        flat = rows.reshape(-1, model_width)
        gate_proj = jnp.dot(flat, gate_w, preferred_element_type=jnp.float32)
        up_proj = jnp.dot(flat, up_w, preferred_element_type=jnp.float32)
        return (jax.nn.silu(gate_proj) * up_proj).astype(jnp.bfloat16)

    def ring_out(own):
        from_left = lax.ppermute(own, "x", plus)
        from_right = lax.ppermute(own, "x", minus)
        from_far = jnp.concatenate(
            [lax.ppermute(from_left[:split], "x", plus), lax.ppermute(from_right[split:], "x", minus)]
        )
        return jnp.stack([own, from_left, from_right, from_far])

    def ring_back(partial_value):
        far_a = lax.ppermute(partial_value[3, :split], "x", plus)
        far_b = lax.ppermute(partial_value[3, split:], "x", minus)
        to_right = partial_value[2].astype(jnp.float32)
        to_right = jnp.concatenate([to_right[:split] + far_a.astype(jnp.float32), to_right[split:]])
        to_left = partial_value[1].astype(jnp.float32)
        to_left = jnp.concatenate([to_left[:split], to_left[split:] + far_b.astype(jnp.float32)])
        at_x = (
            partial_value[0].astype(jnp.float32)
            + lax.ppermute(to_right.astype(jnp.bfloat16), "x", plus).astype(jnp.float32)
            + lax.ppermute(to_left.astype(jnp.bfloat16), "x", minus).astype(jnp.float32)
        ).astype(jnp.bfloat16)
        returned = lax.all_to_all(at_x, "grp", split_axis=0, concat_axis=0, tiled=True)
        return returned.astype(jnp.float32)

    owns = []
    for index in range(chunk_count):
        chunk_ids = jnp.where(
            (local_rank >= index * chunk) & (local_rank < (index + 1) * chunk),
            flat_routes * chunk + local_rank - index * chunk,
            -1,
        ).reshape(token_count, TOP)
        chunk_range = jnp.arange(expert_count * chunk, dtype=jnp.int32)
        placing = jnp.any(chunk_ids[None, :, :] == chunk_range[:, None, None], axis=2).astype(
            jnp.bfloat16
        )
        packed = (
            jnp.dot(placing, moe_input, preferred_element_type=jnp.float32)
            .astype(jnp.bfloat16)
            .reshape(expert_count, chunk, model_width)
        )
        owns.append(lax.all_to_all(packed, "grp", split_axis=0, concat_axis=0, tiled=True))
    chunk_results = []
    received = ring_out(owns[0])
    for index in range(chunk_count):
        activation = gate_up(received)
        if index + 1 < chunk_count:
            following, activation = lax.optimization_barrier((owns[index + 1], activation))
        partial_value = jnp.dot(
            activation, down_w, preferred_element_type=jnp.float32
        ).astype(jnp.bfloat16).reshape(received.shape)
        if index + 1 < chunk_count:
            received = ring_out(following)
        chunk_results.append(ring_back(partial_value))
    summed = jnp.concatenate(chunk_results, axis=1).reshape(expert_count * half_cap, model_width)
    gates = jnp.stack([first_gate, second_gate], axis=1)
    mixing = jnp.sum(
        jnp.where(paired[:, :, None] == slot_range[None, None, :], gates[:, :, None], 0.0), axis=1
    )
    local_sum = jnp.dot(mixing, summed, precision=lax.Precision.HIGHEST)
    moe_own = tp_reduce_scatter(local_sum)
    return (own_residual + moe_own).astype(jnp.bfloat16)


REQ = ("grp", "x")


def solution(mesh):
    def run(*args):
        experts = args[8].shape[1]
        copies = mesh.shape["req"] // experts
        fine = jax.sharding.Mesh(
            mesh.devices.reshape(experts, copies, mesh.shape["tp"]), ("grp", "x", "tp")
        )
        return sharded(fine)(*args)

    return run


def sharded(fine):
    return jax.shard_map(
        per_device,
        mesh=fine,
        in_specs=(
            P(REQ, None),
            P(REQ),
            P(REQ, None, "tp"),
            P(REQ, None, "tp"),
            P(),
            P(None, None, "tp"),
            P("tp", None),
            P(),
            P(),
            P(REQ, None),
            P(REQ, None, "tp"),
            P(REQ, None, "tp"),
            P(REQ, "tp", None),
        ),
        out_specs=P((*REQ, "tp"), None),
        check_vma=False,
    )
```

```python
import functools
import math

import jax
import jax.numpy as jnp
from jax import lax
from jax.experimental import pallas as pl
from jax.experimental.pallas import tpu as pltpu
from jax.sharding import PartitionSpec as P

HEAD = 64
TOP = 2
CAP = 96


EPSILON = 1e-05


def normalize(inputs, scale_gain):
    mean_square = jnp.mean(inputs * inputs, axis=-1, keepdims=True)
    return inputs * lax.rsqrt(mean_square + EPSILON) * scale_gain


def rotate(inputs, positions):
    half_dim = inputs.shape[-1] // 2
    frequency = jnp.exp(
        jnp.arange(half_dim, dtype=jnp.float32) * (-2.0 * math.log(10000.0) / inputs.shape[-1])
    )
    angles = positions.astype(jnp.float32)[:, None] * frequency[None, :]
    cosine = jnp.cos(angles)[:, None, :]
    sine_part = jnp.sin(angles)[:, None, :]
    lower_half = inputs[..., :half_dim]
    upper_half = inputs[..., half_dim:]
    return jnp.concatenate(
        [
            lower_half * cosine - upper_half * sine_part,
            lower_half * sine_part + upper_half * cosine,
        ],
        axis=-1,
    )


def attention_kernel(
    length_ref,
    query_ref,
    key_ref,
    value_ref,
    fresh_key_ref,
    fresh_value_ref,
    out_ref,
    *,
    head_dim,
    first_query,
):
    query_count = query_ref.shape[0]
    cache_len = key_ref.shape[1]
    length = length_ref[0]
    cache_live = lax.broadcasted_iota(jnp.int32, (query_count, cache_len), 1) < length
    fresh_count = fresh_key_ref.shape[1]
    fresh_live = lax.broadcasted_iota(
        jnp.int32, (query_count, fresh_count), 1
    ) <= lax.broadcasted_iota(jnp.int32, (query_count, fresh_count), 0) + first_query
    contract = (((1,), (1,)), ((), ()))
    for head in range(query_ref.shape[1] // head_dim):
        lanes = slice(head * head_dim, (head + 1) * head_dim)
        queries = query_ref[:, lanes]
        cache_scores = jnp.dot(
            queries, key_ref[lanes, :], preferred_element_type=jnp.float32
        ) * (head_dim ** -0.5)
        fresh_scores = jnp.dot(
            queries, fresh_key_ref[lanes, :], preferred_element_type=jnp.float32
        ) * (head_dim ** -0.5)
        cache_scores = jnp.where(cache_live, cache_scores, -jnp.inf)
        fresh_scores = jnp.where(fresh_live, fresh_scores, -jnp.inf)
        row_max = jnp.maximum(
            jnp.max(cache_scores, axis=1, keepdims=True),
            jnp.max(fresh_scores, axis=1, keepdims=True),
        )
        cache_weights = jnp.exp(cache_scores - row_max)
        fresh_weights = jnp.exp(fresh_scores - row_max)
        totals = jnp.sum(cache_weights, axis=1, keepdims=True) + jnp.sum(
            fresh_weights, axis=1, keepdims=True
        )
        mixture = lax.dot_general(
            cache_weights.astype(jnp.bfloat16),
            value_ref[lanes, :],
            contract,
            preferred_element_type=jnp.float32,
        ) + lax.dot_general(
            fresh_weights.astype(jnp.bfloat16),
            fresh_value_ref[lanes, :],
            contract,
            preferred_element_type=jnp.float32,
        )
        out_ref[:, lanes] = (mixture / totals).astype(out_ref.dtype)


def attention(queries, key_cache, value_cache, fresh_keys, fresh_values, length, first_query):
    vmem = pl.BlockSpec(memory_space=pltpu.VMEM)
    return pl.pallas_call(
        functools.partial(attention_kernel, head_dim=HEAD, first_query=first_query),
        out_shape=jax.ShapeDtypeStruct(queries.shape, jnp.bfloat16),
        in_specs=[pl.BlockSpec(memory_space=pltpu.SMEM)] + [vmem] * 5,
        out_specs=vmem,
    )(length, queries, key_cache.T, value_cache.T, fresh_keys.T, fresh_values.T)


def tp_allreduce(partial):
    tp_size = lax.axis_size("tp")
    core = lax.axis_index("tp") % 2
    core_pairs = [(i, i ^ 1) for i in range(tp_size)]
    z_pairs = [(i, i ^ 2) for i in range(tp_size)]
    halves = partial.astype(jnp.bfloat16).reshape(2, partial.shape[0] // 2, partial.shape[1])
    keep = jnp.where(core == 0, halves[0], halves[1])
    send = jnp.where(core == 0, halves[1], halves[0])
    chip_sum = (
        keep.astype(jnp.float32) + lax.ppermute(send, "tp", core_pairs).astype(jnp.float32)
    ).astype(jnp.bfloat16)
    total = (
        chip_sum.astype(jnp.float32) + lax.ppermute(chip_sum, "tp", z_pairs).astype(jnp.float32)
    ).astype(jnp.bfloat16)
    other = lax.ppermute(total, "tp", core_pairs)
    return jnp.where(core == 0, jnp.concatenate([total, other]), jnp.concatenate([other, total]))


def tp_reduce_scatter(partial):
    tp_size = lax.axis_size("tp")
    tp_index = lax.axis_index("tp")
    core = tp_index % 2
    upper = tp_index // 2
    core_pairs = [(i, i ^ 1) for i in range(tp_size)]
    z_pairs = [(i, i ^ 2) for i in range(tp_size)]
    blocks = partial.astype(jnp.bfloat16).reshape(2, 2, partial.shape[0] // 4, partial.shape[1])
    keep = jnp.where(core == 0, blocks[:, 0], blocks[:, 1])
    send = jnp.where(core == 0, blocks[:, 1], blocks[:, 0])
    chip_sum = (
        keep.astype(jnp.float32) + lax.ppermute(send, "tp", core_pairs).astype(jnp.float32)
    ).astype(jnp.bfloat16)
    mine = jnp.where(upper == 0, chip_sum[0], chip_sum[1])
    theirs = jnp.where(upper == 0, chip_sum[1], chip_sum[0])
    return mine.astype(jnp.float32) + lax.ppermute(theirs, "tp", z_pairs).astype(jnp.float32)


def per_device(
    hidden_in,
    cache_lengths,
    key_cache,
    value_cache,
    attn_norm,
    w_qkv,
    w_out,
    ffn_norm,
    router,
    routes,
    expert_gate,
    expert_up,
    expert_down,
):
    token_count = hidden_in.shape[0]
    model_width = hidden_in.shape[1]
    local_lanes = w_qkv.shape[2]
    local_heads = local_lanes // HEAD
    cache_len = key_cache.shape[1]
    token_share = token_count // lax.axis_size("tp")
    offset = lax.axis_index("tp") * token_share
    expert_count = router.shape[1]
    residual = hidden_in.astype(jnp.float32)
    normed = normalize(residual, attn_norm).astype(jnp.bfloat16)
    projected = jnp.einsum("td,cdh->cth", normed, w_qkv, preferred_element_type=jnp.float32)
    length = cache_lengths[0]
    positions = length + jnp.arange(token_count, dtype=jnp.int32)
    queries = rotate(projected[0].reshape(token_count, local_heads, HEAD), positions).astype(
        jnp.bfloat16
    )
    fresh_keys = rotate(projected[1].reshape(token_count, local_heads, HEAD), positions).astype(
        jnp.bfloat16
    )
    fresh_values = projected[2].reshape(token_count, local_heads, HEAD).astype(jnp.bfloat16)
    query_rows = queries.reshape(token_count, local_lanes)
    query_half = token_count // 2
    summed_parts = []
    for first in (0, query_half):
        attended = attention(
            query_rows[first : first + query_half],
            key_cache[0],
            value_cache[0],
            fresh_keys.reshape(token_count, local_lanes),
            fresh_values.reshape(token_count, local_lanes),
            cache_lengths,
            first,
        )
        summed_parts.append(
            tp_allreduce(jnp.dot(attended, w_out, preferred_element_type=jnp.float32))
        )
    summed_attn = jnp.concatenate(summed_parts).astype(jnp.float32)
    updated = residual + summed_attn
    moe_input = normalize(updated, ffn_norm).astype(jnp.bfloat16)
    own_residual = lax.dynamic_slice_in_dim(updated, offset, token_share, 0)
    logits = jnp.dot(moe_input, router, preferred_element_type=jnp.float32)
    chosen = jnp.take_along_axis(logits, routes, axis=1)
    first_gate = 1.0 / (1.0 + jnp.exp(chosen[:, 1] - chosen[:, 0]))
    second_gate = 1.0 / (1.0 + jnp.exp(chosen[:, 0] - chosen[:, 1]))
    flat_routes = routes.reshape(-1)
    onehot = (flat_routes[:, None] == jnp.arange(expert_count, dtype=jnp.int32)[None, :]).astype(
        jnp.int32
    )
    slot_rank = jnp.sum((jnp.cumsum(onehot, axis=0) - onehot) * onehot, axis=1)
    tp_size = lax.axis_size("tp")
    core = lax.axis_index("tp") % 2
    half_cap = CAP // 2
    pairs = [(i, i ^ 1) for i in range(tp_size)]
    gate_w = jnp.concatenate([expert_gate[0], lax.ppermute(expert_gate[0], "tp", pairs)], axis=1)
    up_w = jnp.concatenate([expert_up[0], lax.ppermute(expert_up[0], "tp", pairs)], axis=1)
    down_w = jnp.concatenate([expert_down[0], lax.ppermute(expert_down[0], "tp", pairs)], axis=0)
    local_rank = slot_rank - core * half_cap
    in_half = (local_rank >= 0) & (local_rank < half_cap)
    slot_ids = jnp.where(in_half, flat_routes * half_cap + local_rank, -1)
    paired = slot_ids.reshape(token_count, TOP)
    slot_range = jnp.arange(expert_count * half_cap, dtype=jnp.int32)
    chunk_count = 2
    chunk = half_cap // chunk_count
    ring = lax.axis_size("x")
    plus = [(i, (i + 1) % ring) for i in range(ring)]
    minus = [(i, (i - 1) % ring) for i in range(ring)]
    split = expert_count // 2
    chunk_results = []
    for index in range(chunk_count):
        chunk_ids = jnp.where(
            (local_rank >= index * chunk) & (local_rank < (index + 1) * chunk),
            flat_routes * chunk + local_rank - index * chunk,
            -1,
        ).reshape(token_count, TOP)
        chunk_range = jnp.arange(expert_count * chunk, dtype=jnp.int32)
        placing = jnp.any(chunk_ids[None, :, :] == chunk_range[:, None, None], axis=2).astype(
            jnp.bfloat16
        )
        packed = (
            jnp.dot(placing, moe_input, preferred_element_type=jnp.float32)
            .astype(jnp.bfloat16)
            .reshape(expert_count, chunk, model_width)
        )
        own = lax.all_to_all(packed, "grp", split_axis=0, concat_axis=0, tiled=True)
        from_left = lax.ppermute(own, "x", plus)
        from_right = lax.ppermute(own, "x", minus)
        from_far = jnp.concatenate(
            [lax.ppermute(from_left[:split], "x", plus), lax.ppermute(from_right[split:], "x", minus)]
        )
        received = jnp.stack([own, from_left, from_right, from_far])
        token_rows = received.reshape(-1, model_width)
        gate_proj = jnp.dot(token_rows, gate_w, preferred_element_type=jnp.float32)
        up_proj = jnp.dot(token_rows, up_w, preferred_element_type=jnp.float32)
        activation = (jax.nn.silu(gate_proj) * up_proj).astype(jnp.bfloat16)
        partial_value = jnp.dot(
            activation, down_w, preferred_element_type=jnp.float32
        ).astype(jnp.bfloat16).reshape(received.shape)
        far_a = lax.ppermute(partial_value[3, :split], "x", plus)
        far_b = lax.ppermute(partial_value[3, split:], "x", minus)
        to_right = partial_value[2].astype(jnp.float32)
        to_right = jnp.concatenate([to_right[:split] + far_a.astype(jnp.float32), to_right[split:]])
        to_left = partial_value[1].astype(jnp.float32)
        to_left = jnp.concatenate([to_left[:split], to_left[split:] + far_b.astype(jnp.float32)])
        at_x = (
            partial_value[0].astype(jnp.float32)
            + lax.ppermute(to_right.astype(jnp.bfloat16), "x", plus).astype(jnp.float32)
            + lax.ppermute(to_left.astype(jnp.bfloat16), "x", minus).astype(jnp.float32)
        ).astype(jnp.bfloat16)
        returned = lax.all_to_all(at_x, "grp", split_axis=0, concat_axis=0, tiled=True)
        chunk_results.append(returned.astype(jnp.float32))
    summed = jnp.concatenate(chunk_results, axis=1).reshape(expert_count * half_cap, model_width)
    gates = jnp.stack([first_gate, second_gate], axis=1)
    mixing = jnp.sum(
        jnp.where(paired[:, :, None] == slot_range[None, None, :], gates[:, :, None], 0.0), axis=1
    )
    local_sum = jnp.dot(mixing, summed, precision=lax.Precision.HIGHEST)
    moe_own = tp_reduce_scatter(local_sum)
    return (own_residual + moe_own).astype(jnp.bfloat16)


REQ = ("grp", "x")


def solution(mesh):
    def run(*args):
        experts = args[8].shape[1]
        copies = mesh.shape["req"] // experts
        fine = jax.sharding.Mesh(
            mesh.devices.reshape(experts, copies, mesh.shape["tp"]), ("grp", "x", "tp")
        )
        return sharded(fine)(*args)

    return run


def sharded(fine):
    return jax.shard_map(
        per_device,
        mesh=fine,
        in_specs=(
            P(REQ, None),
            P(REQ),
            P(REQ, None, "tp"),
            P(REQ, None, "tp"),
            P(),
            P(None, None, "tp"),
            P("tp", None),
            P(),
            P(),
            P(REQ, None),
            P(REQ, None, "tp"),
            P(REQ, None, "tp"),
            P(REQ, "tp", None),
        ),
        out_specs=P((*REQ, "tp"), None),
        check_vma=False,
    )
```

```python
import functools
import math

import jax
import jax.numpy as jnp
from jax import lax
from jax.experimental import pallas as pl
from jax.experimental.pallas import tpu as pltpu
from jax.sharding import PartitionSpec as P

HEAD = 64
TOP = 2
CAP = 96


EPSILON = 1e-05


def normalize(inputs, scale_gain):
    mean_square = jnp.mean(inputs * inputs, axis=-1, keepdims=True)
    return inputs * lax.rsqrt(mean_square + EPSILON) * scale_gain


def rotate(inputs, positions):
    half_dim = inputs.shape[-1] // 2
    frequency = jnp.exp(
        jnp.arange(half_dim, dtype=jnp.float32) * (-2.0 * math.log(10000.0) / inputs.shape[-1])
    )
    angles = positions.astype(jnp.float32)[:, None] * frequency[None, :]
    cosine = jnp.cos(angles)[:, None, :]
    sine_part = jnp.sin(angles)[:, None, :]
    lower_half = inputs[..., :half_dim]
    upper_half = inputs[..., half_dim:]
    return jnp.concatenate(
        [
            lower_half * cosine - upper_half * sine_part,
            lower_half * sine_part + upper_half * cosine,
        ],
        axis=-1,
    )


def attention_kernel(
    length_ref, query_ref, key_ref, value_ref, fresh_key_ref, fresh_value_ref, out_ref, *, head_dim
):
    query_count = query_ref.shape[0]
    cache_len = key_ref.shape[1]
    length = length_ref[0]
    cache_live = lax.broadcasted_iota(jnp.int32, (query_count, cache_len), 1) < length
    fresh_live = lax.broadcasted_iota(
        jnp.int32, (query_count, query_count), 1
    ) <= lax.broadcasted_iota(jnp.int32, (query_count, query_count), 0)
    contract = (((1,), (1,)), ((), ()))
    for head in range(query_ref.shape[1] // head_dim):
        lanes = slice(head * head_dim, (head + 1) * head_dim)
        queries = query_ref[:, lanes]
        cache_scores = jnp.dot(
            queries, key_ref[lanes, :], preferred_element_type=jnp.float32
        ) * (head_dim ** -0.5)
        fresh_scores = jnp.dot(
            queries, fresh_key_ref[lanes, :], preferred_element_type=jnp.float32
        ) * (head_dim ** -0.5)
        cache_scores = jnp.where(cache_live, cache_scores, -jnp.inf)
        fresh_scores = jnp.where(fresh_live, fresh_scores, -jnp.inf)
        row_max = jnp.maximum(
            jnp.max(cache_scores, axis=1, keepdims=True),
            jnp.max(fresh_scores, axis=1, keepdims=True),
        )
        cache_weights = jnp.exp(cache_scores - row_max)
        fresh_weights = jnp.exp(fresh_scores - row_max)
        totals = jnp.sum(cache_weights, axis=1, keepdims=True) + jnp.sum(
            fresh_weights, axis=1, keepdims=True
        )
        mixture = lax.dot_general(
            cache_weights.astype(jnp.bfloat16),
            value_ref[lanes, :],
            contract,
            preferred_element_type=jnp.float32,
        ) + lax.dot_general(
            fresh_weights.astype(jnp.bfloat16),
            fresh_value_ref[lanes, :],
            contract,
            preferred_element_type=jnp.float32,
        )
        out_ref[:, lanes] = (mixture / totals).astype(out_ref.dtype)


def attention(queries, key_cache, value_cache, fresh_keys, fresh_values, length):
    vmem = pl.BlockSpec(memory_space=pltpu.VMEM)
    return pl.pallas_call(
        functools.partial(attention_kernel, head_dim=HEAD),
        out_shape=jax.ShapeDtypeStruct(queries.shape, jnp.bfloat16),
        in_specs=[pl.BlockSpec(memory_space=pltpu.SMEM)] + [vmem] * 5,
        out_specs=vmem,
    )(length, queries, key_cache.T, value_cache.T, fresh_keys.T, fresh_values.T)


def tp_allreduce(partial):
    tp_size = lax.axis_size("tp")
    core = lax.axis_index("tp") % 2
    core_pairs = [(i, i ^ 1) for i in range(tp_size)]
    z_pairs = [(i, i ^ 2) for i in range(tp_size)]
    halves = partial.astype(jnp.bfloat16).reshape(2, partial.shape[0] // 2, partial.shape[1])
    keep = jnp.where(core == 0, halves[0], halves[1])
    send = jnp.where(core == 0, halves[1], halves[0])
    chip_sum = (
        keep.astype(jnp.float32) + lax.ppermute(send, "tp", core_pairs).astype(jnp.float32)
    ).astype(jnp.bfloat16)
    total = (
        chip_sum.astype(jnp.float32) + lax.ppermute(chip_sum, "tp", z_pairs).astype(jnp.float32)
    ).astype(jnp.bfloat16)
    other = lax.ppermute(total, "tp", core_pairs)
    return jnp.where(core == 0, jnp.concatenate([total, other]), jnp.concatenate([other, total]))


def tp_reduce_scatter(partial):
    tp_size = lax.axis_size("tp")
    tp_index = lax.axis_index("tp")
    core = tp_index % 2
    upper = tp_index // 2
    core_pairs = [(i, i ^ 1) for i in range(tp_size)]
    z_pairs = [(i, i ^ 2) for i in range(tp_size)]
    blocks = partial.astype(jnp.bfloat16).reshape(2, 2, partial.shape[0] // 4, partial.shape[1])
    keep = jnp.where(core == 0, blocks[:, 0], blocks[:, 1])
    send = jnp.where(core == 0, blocks[:, 1], blocks[:, 0])
    chip_sum = (
        keep.astype(jnp.float32) + lax.ppermute(send, "tp", core_pairs).astype(jnp.float32)
    ).astype(jnp.bfloat16)
    mine = jnp.where(upper == 0, chip_sum[0], chip_sum[1])
    theirs = jnp.where(upper == 0, chip_sum[1], chip_sum[0])
    return mine.astype(jnp.float32) + lax.ppermute(theirs, "tp", z_pairs).astype(jnp.float32)


def per_device(
    hidden_in,
    cache_lengths,
    key_cache,
    value_cache,
    attn_norm,
    w_qkv,
    w_out,
    ffn_norm,
    router,
    routes,
    expert_gate,
    expert_up,
    expert_down,
):
    token_count = hidden_in.shape[0]
    model_width = hidden_in.shape[1]
    local_lanes = w_qkv.shape[2]
    local_heads = local_lanes // HEAD
    cache_len = key_cache.shape[1]
    token_share = token_count // lax.axis_size("tp")
    offset = lax.axis_index("tp") * token_share
    expert_count = router.shape[1]
    residual = hidden_in.astype(jnp.float32)
    normed = normalize(residual, attn_norm).astype(jnp.bfloat16)
    projected = jnp.einsum("td,cdh->cth", normed, w_qkv, preferred_element_type=jnp.float32)
    length = cache_lengths[0]
    positions = length + jnp.arange(token_count, dtype=jnp.int32)
    queries = rotate(projected[0].reshape(token_count, local_heads, HEAD), positions).astype(
        jnp.bfloat16
    )
    fresh_keys = rotate(projected[1].reshape(token_count, local_heads, HEAD), positions).astype(
        jnp.bfloat16
    )
    fresh_values = projected[2].reshape(token_count, local_heads, HEAD).astype(jnp.bfloat16)
    attended = attention(
        queries.reshape(token_count, local_lanes),
        key_cache[0],
        value_cache[0],
        fresh_keys.reshape(token_count, local_lanes),
        fresh_values.reshape(token_count, local_lanes),
        cache_lengths,
    )
    summed_attn = tp_allreduce(
        jnp.dot(attended, w_out, preferred_element_type=jnp.float32)
    ).astype(jnp.float32)
    updated = residual + summed_attn
    moe_input = normalize(updated, ffn_norm).astype(jnp.bfloat16)
    own_residual = lax.dynamic_slice_in_dim(updated, offset, token_share, 0)
    logits = jnp.dot(moe_input, router, preferred_element_type=jnp.float32)
    chosen = jnp.take_along_axis(logits, routes, axis=1)
    first_gate = 1.0 / (1.0 + jnp.exp(chosen[:, 1] - chosen[:, 0]))
    second_gate = 1.0 / (1.0 + jnp.exp(chosen[:, 0] - chosen[:, 1]))
    flat_routes = routes.reshape(-1)
    onehot = (flat_routes[:, None] == jnp.arange(expert_count, dtype=jnp.int32)[None, :]).astype(
        jnp.int32
    )
    slot_rank = jnp.sum((jnp.cumsum(onehot, axis=0) - onehot) * onehot, axis=1)
    tp_size = lax.axis_size("tp")
    core = lax.axis_index("tp") % 2
    half_cap = CAP // 2
    pairs = [(i, i ^ 1) for i in range(tp_size)]
    gate_w = jnp.concatenate([expert_gate[0], lax.ppermute(expert_gate[0], "tp", pairs)], axis=1)
    up_w = jnp.concatenate([expert_up[0], lax.ppermute(expert_up[0], "tp", pairs)], axis=1)
    down_w = jnp.concatenate([expert_down[0], lax.ppermute(expert_down[0], "tp", pairs)], axis=0)
    local_rank = slot_rank - core * half_cap
    in_half = (local_rank >= 0) & (local_rank < half_cap)
    slot_ids = jnp.where(in_half, flat_routes * half_cap + local_rank, -1)
    paired = slot_ids.reshape(token_count, TOP)
    slot_range = jnp.arange(expert_count * half_cap, dtype=jnp.int32)
    chunk_count = 3
    chunk = half_cap // chunk_count
    ring = lax.axis_size("x")
    plus = [(i, (i + 1) % ring) for i in range(ring)]
    minus = [(i, (i - 1) % ring) for i in range(ring)]
    split = expert_count // 2
    chunk_results = []
    for index in range(chunk_count):
        chunk_ids = jnp.where(
            (local_rank >= index * chunk) & (local_rank < (index + 1) * chunk),
            flat_routes * chunk + local_rank - index * chunk,
            -1,
        ).reshape(token_count, TOP)
        chunk_range = jnp.arange(expert_count * chunk, dtype=jnp.int32)
        placing = jnp.any(chunk_ids[None, :, :] == chunk_range[:, None, None], axis=2).astype(
            jnp.bfloat16
        )
        packed = (
            jnp.dot(placing, moe_input, preferred_element_type=jnp.float32)
            .astype(jnp.bfloat16)
            .reshape(expert_count, chunk, model_width)
        )
        own = lax.all_to_all(packed, "grp", split_axis=0, concat_axis=0, tiled=True)
        from_left = lax.ppermute(own, "x", plus)
        from_right = lax.ppermute(own, "x", minus)
        from_far = jnp.concatenate(
            [lax.ppermute(from_left[:split], "x", plus), lax.ppermute(from_right[split:], "x", minus)]
        )
        received = jnp.stack([own, from_left, from_right, from_far])
        token_rows = received.reshape(-1, model_width)
        gate_proj = jnp.dot(token_rows, gate_w, preferred_element_type=jnp.float32)
        up_proj = jnp.dot(token_rows, up_w, preferred_element_type=jnp.float32)
        activation = (jax.nn.silu(gate_proj) * up_proj).astype(jnp.bfloat16)
        partial_value = jnp.dot(
            activation, down_w, preferred_element_type=jnp.float32
        ).astype(jnp.bfloat16).reshape(received.shape)
        far_a = lax.ppermute(partial_value[3, :split], "x", plus)
        far_b = lax.ppermute(partial_value[3, split:], "x", minus)
        to_right = partial_value[2].astype(jnp.float32)
        to_right = jnp.concatenate([to_right[:split] + far_a.astype(jnp.float32), to_right[split:]])
        to_left = partial_value[1].astype(jnp.float32)
        to_left = jnp.concatenate([to_left[:split], to_left[split:] + far_b.astype(jnp.float32)])
        at_x = (
            partial_value[0].astype(jnp.float32)
            + lax.ppermute(to_right.astype(jnp.bfloat16), "x", plus).astype(jnp.float32)
            + lax.ppermute(to_left.astype(jnp.bfloat16), "x", minus).astype(jnp.float32)
        ).astype(jnp.bfloat16)
        returned = lax.all_to_all(at_x, "grp", split_axis=0, concat_axis=0, tiled=True)
        chunk_results.append(returned.astype(jnp.float32))
    summed = jnp.concatenate(chunk_results, axis=1).reshape(expert_count * half_cap, model_width)
    gates = jnp.stack([first_gate, second_gate], axis=1)
    mixing = jnp.sum(
        jnp.where(paired[:, :, None] == slot_range[None, None, :], gates[:, :, None], 0.0), axis=1
    )
    local_sum = jnp.dot(mixing, summed, precision=lax.Precision.HIGHEST)
    moe_own = tp_reduce_scatter(local_sum)
    return (own_residual + moe_own).astype(jnp.bfloat16)


REQ = ("grp", "x")


def solution(mesh):
    def run(*args):
        experts = args[8].shape[1]
        copies = mesh.shape["req"] // experts
        fine = jax.sharding.Mesh(
            mesh.devices.reshape(experts, copies, mesh.shape["tp"]), ("grp", "x", "tp")
        )
        return sharded(fine)(*args)

    return run


def sharded(fine):
    return jax.shard_map(
        per_device,
        mesh=fine,
        in_specs=(
            P(REQ, None),
            P(REQ),
            P(REQ, None, "tp"),
            P(REQ, None, "tp"),
            P(),
            P(None, None, "tp"),
            P("tp", None),
            P(),
            P(),
            P(REQ, None),
            P(REQ, None, "tp"),
            P(REQ, None, "tp"),
            P(REQ, "tp", None),
        ),
        out_specs=P((*REQ, "tp"), None),
        check_vma=False,
    )
```

```python
import functools
import math

import jax
import jax.numpy as jnp
from jax import lax
from jax.experimental import pallas as pl
from jax.experimental.pallas import tpu as pltpu
from jax.sharding import PartitionSpec as P

HEAD = 64
TOP = 2
CAP = 96


EPSILON = 1e-05


def normalize(inputs, scale_gain):
    mean_square = jnp.mean(inputs * inputs, axis=-1, keepdims=True)
    return inputs * lax.rsqrt(mean_square + EPSILON) * scale_gain


def rotate(inputs, positions):
    half_dim = inputs.shape[-1] // 2
    frequency = jnp.exp(
        jnp.arange(half_dim, dtype=jnp.float32) * (-2.0 * math.log(10000.0) / inputs.shape[-1])
    )
    angles = positions.astype(jnp.float32)[:, None] * frequency[None, :]
    cosine = jnp.cos(angles)[:, None, :]
    sine_part = jnp.sin(angles)[:, None, :]
    lower_half = inputs[..., :half_dim]
    upper_half = inputs[..., half_dim:]
    return jnp.concatenate(
        [
            lower_half * cosine - upper_half * sine_part,
            lower_half * sine_part + upper_half * cosine,
        ],
        axis=-1,
    )


def attention_kernel(
    length_ref, query_ref, key_ref, value_ref, fresh_key_ref, fresh_value_ref, out_ref, *, head_dim
):
    query_count = query_ref.shape[0]
    cache_len = key_ref.shape[1]
    length = length_ref[0]
    cache_live = lax.broadcasted_iota(jnp.int32, (query_count, cache_len), 1) < length
    fresh_live = lax.broadcasted_iota(
        jnp.int32, (query_count, query_count), 1
    ) <= lax.broadcasted_iota(jnp.int32, (query_count, query_count), 0)
    contract = (((1,), (1,)), ((), ()))
    for head in range(query_ref.shape[1] // head_dim):
        lanes = slice(head * head_dim, (head + 1) * head_dim)
        queries = query_ref[:, lanes]
        cache_scores = jnp.dot(
            queries, key_ref[lanes, :], preferred_element_type=jnp.float32
        ) * (head_dim ** -0.5)
        fresh_scores = jnp.dot(
            queries, fresh_key_ref[lanes, :], preferred_element_type=jnp.float32
        ) * (head_dim ** -0.5)
        cache_scores = jnp.where(cache_live, cache_scores, -jnp.inf)
        fresh_scores = jnp.where(fresh_live, fresh_scores, -jnp.inf)
        row_max = jnp.maximum(
            jnp.max(cache_scores, axis=1, keepdims=True),
            jnp.max(fresh_scores, axis=1, keepdims=True),
        )
        cache_weights = jnp.exp(cache_scores - row_max)
        fresh_weights = jnp.exp(fresh_scores - row_max)
        totals = jnp.sum(cache_weights, axis=1, keepdims=True) + jnp.sum(
            fresh_weights, axis=1, keepdims=True
        )
        mixture = lax.dot_general(
            cache_weights.astype(jnp.bfloat16),
            value_ref[lanes, :],
            contract,
            preferred_element_type=jnp.float32,
        ) + lax.dot_general(
            fresh_weights.astype(jnp.bfloat16),
            fresh_value_ref[lanes, :],
            contract,
            preferred_element_type=jnp.float32,
        )
        out_ref[:, lanes] = (mixture / totals).astype(out_ref.dtype)


def attention(queries, key_cache, value_cache, fresh_keys, fresh_values, length):
    vmem = pl.BlockSpec(memory_space=pltpu.VMEM)
    return pl.pallas_call(
        functools.partial(attention_kernel, head_dim=HEAD),
        out_shape=jax.ShapeDtypeStruct(queries.shape, jnp.bfloat16),
        in_specs=[pl.BlockSpec(memory_space=pltpu.SMEM)] + [vmem] * 5,
        out_specs=vmem,
    )(length, queries, key_cache.T, value_cache.T, fresh_keys.T, fresh_values.T)


def tp_allreduce(partial):
    tp_size = lax.axis_size("tp")
    core = lax.axis_index("tp") % 2
    core_pairs = [(i, i ^ 1) for i in range(tp_size)]
    z_pairs = [(i, i ^ 2) for i in range(tp_size)]
    halves = partial.astype(jnp.bfloat16).reshape(2, partial.shape[0] // 2, partial.shape[1])
    keep = jnp.where(core == 0, halves[0], halves[1])
    send = jnp.where(core == 0, halves[1], halves[0])
    chip_sum = (
        keep.astype(jnp.float32) + lax.ppermute(send, "tp", core_pairs).astype(jnp.float32)
    ).astype(jnp.bfloat16)
    total = (
        chip_sum.astype(jnp.float32) + lax.ppermute(chip_sum, "tp", z_pairs).astype(jnp.float32)
    ).astype(jnp.bfloat16)
    other = lax.ppermute(total, "tp", core_pairs)
    return jnp.where(core == 0, jnp.concatenate([total, other]), jnp.concatenate([other, total]))


def tp_reduce_scatter(partial):
    tp_size = lax.axis_size("tp")
    tp_index = lax.axis_index("tp")
    core = tp_index % 2
    upper = tp_index // 2
    core_pairs = [(i, i ^ 1) for i in range(tp_size)]
    z_pairs = [(i, i ^ 2) for i in range(tp_size)]
    blocks = partial.astype(jnp.bfloat16).reshape(2, 2, partial.shape[0] // 4, partial.shape[1])
    keep = jnp.where(core == 0, blocks[:, 0], blocks[:, 1])
    send = jnp.where(core == 0, blocks[:, 1], blocks[:, 0])
    chip_sum = (
        keep.astype(jnp.float32) + lax.ppermute(send, "tp", core_pairs).astype(jnp.float32)
    ).astype(jnp.bfloat16)
    mine = jnp.where(upper == 0, chip_sum[0], chip_sum[1])
    theirs = jnp.where(upper == 0, chip_sum[1], chip_sum[0])
    return mine.astype(jnp.float32) + lax.ppermute(theirs, "tp", z_pairs).astype(jnp.float32)


def per_device(
    hidden_in,
    cache_lengths,
    key_cache,
    value_cache,
    attn_norm,
    w_qkv,
    w_out,
    ffn_norm,
    router,
    routes,
    expert_gate,
    expert_up,
    expert_down,
):
    token_count = hidden_in.shape[0]
    model_width = hidden_in.shape[1]
    local_lanes = w_qkv.shape[2]
    local_heads = local_lanes // HEAD
    cache_len = key_cache.shape[1]
    token_share = token_count // lax.axis_size("tp")
    offset = lax.axis_index("tp") * token_share
    expert_count = router.shape[1]
    residual = hidden_in.astype(jnp.float32)
    normed = normalize(residual, attn_norm).astype(jnp.bfloat16)
    projected = jnp.einsum("td,cdh->cth", normed, w_qkv, preferred_element_type=jnp.float32)
    length = cache_lengths[0]
    positions = length + jnp.arange(token_count, dtype=jnp.int32)
    queries = rotate(projected[0].reshape(token_count, local_heads, HEAD), positions).astype(
        jnp.bfloat16
    )
    fresh_keys = rotate(projected[1].reshape(token_count, local_heads, HEAD), positions).astype(
        jnp.bfloat16
    )
    fresh_values = projected[2].reshape(token_count, local_heads, HEAD).astype(jnp.bfloat16)
    attended = attention(
        queries.reshape(token_count, local_lanes),
        key_cache[0],
        value_cache[0],
        fresh_keys.reshape(token_count, local_lanes),
        fresh_values.reshape(token_count, local_lanes),
        cache_lengths,
    )
    summed_attn = tp_allreduce(
        jnp.dot(attended, w_out, preferred_element_type=jnp.float32)
    ).astype(jnp.float32)
    updated = residual + summed_attn
    moe_input = normalize(updated, ffn_norm).astype(jnp.bfloat16)
    own_residual = lax.dynamic_slice_in_dim(updated, offset, token_share, 0)
    logits = jnp.dot(moe_input, router, preferred_element_type=jnp.float32)
    chosen = jnp.take_along_axis(logits, routes, axis=1)
    first_gate = 1.0 / (1.0 + jnp.exp(chosen[:, 1] - chosen[:, 0]))
    second_gate = 1.0 / (1.0 + jnp.exp(chosen[:, 0] - chosen[:, 1]))
    flat_routes = routes.reshape(-1)
    onehot = (flat_routes[:, None] == jnp.arange(expert_count, dtype=jnp.int32)[None, :]).astype(
        jnp.int32
    )
    slot_rank = jnp.sum((jnp.cumsum(onehot, axis=0) - onehot) * onehot, axis=1)
    tp_size = lax.axis_size("tp")
    core = lax.axis_index("tp") % 2
    half_cap = CAP // 2
    pairs = [(i, i ^ 1) for i in range(tp_size)]
    gate_w = jnp.concatenate([expert_gate[0], lax.ppermute(expert_gate[0], "tp", pairs)], axis=1)
    up_w = jnp.concatenate([expert_up[0], lax.ppermute(expert_up[0], "tp", pairs)], axis=1)
    down_w = jnp.concatenate([expert_down[0], lax.ppermute(expert_down[0], "tp", pairs)], axis=0)
    local_rank = slot_rank - core * half_cap
    in_half = (local_rank >= 0) & (local_rank < half_cap)
    slot_ids = jnp.where(in_half, flat_routes * half_cap + local_rank, -1)
    paired = slot_ids.reshape(token_count, TOP)
    slot_range = jnp.arange(expert_count * half_cap, dtype=jnp.int32)
    chunk_count = 2
    chunk = half_cap // chunk_count
    ring = lax.axis_size("x")
    plus = [(i, (i + 1) % ring) for i in range(ring)]
    minus = [(i, (i - 1) % ring) for i in range(ring)]
    split = expert_count // 2
    chunk_results = []
    for index in range(chunk_count):
        chunk_ids = jnp.where(
            (local_rank >= index * chunk) & (local_rank < (index + 1) * chunk),
            flat_routes * chunk + local_rank - index * chunk,
            -1,
        ).reshape(token_count, TOP)
        chunk_range = jnp.arange(expert_count * chunk, dtype=jnp.int32)
        placing = jnp.any(chunk_ids[None, :, :] == chunk_range[:, None, None], axis=2).astype(
            jnp.bfloat16
        )
        packed = (
            jnp.dot(placing, moe_input, preferred_element_type=jnp.float32)
            .astype(jnp.bfloat16)
            .reshape(expert_count, chunk, model_width)
        )
        own = lax.all_to_all(packed, "grp", split_axis=0, concat_axis=0, tiled=True)
        from_left = lax.ppermute(own, "x", plus)
        from_right = lax.ppermute(own, "x", minus)
        from_far = jnp.concatenate(
            [lax.ppermute(from_left[:split], "x", plus), lax.ppermute(from_right[split:], "x", minus)]
        )
        received = jnp.stack([own, from_left, from_right, from_far])
        token_rows = received.reshape(-1, model_width)
        gate_proj = jnp.dot(token_rows, gate_w, preferred_element_type=jnp.float32)
        up_proj = jnp.dot(token_rows, up_w, preferred_element_type=jnp.float32)
        activation = (jax.nn.silu(gate_proj) * up_proj).astype(jnp.bfloat16)
        partial_value = jnp.dot(
            activation, down_w, preferred_element_type=jnp.float32
        ).astype(jnp.bfloat16).reshape(received.shape)
        far_a = lax.ppermute(partial_value[3, :split], "x", plus)
        far_b = lax.ppermute(partial_value[3, split:], "x", minus)
        to_right = partial_value[2].astype(jnp.float32)
        to_right = jnp.concatenate([to_right[:split] + far_a.astype(jnp.float32), to_right[split:]])
        to_left = partial_value[1].astype(jnp.float32)
        to_left = jnp.concatenate([to_left[:split], to_left[split:] + far_b.astype(jnp.float32)])
        at_x = (
            partial_value[0].astype(jnp.float32)
            + lax.ppermute(to_right.astype(jnp.bfloat16), "x", plus).astype(jnp.float32)
            + lax.ppermute(to_left.astype(jnp.bfloat16), "x", minus).astype(jnp.float32)
        ).astype(jnp.bfloat16)
        returned = lax.all_to_all(at_x, "grp", split_axis=0, concat_axis=0, tiled=True)
        chunk_results.append(returned.astype(jnp.float32))
    gates = jnp.stack([first_gate, second_gate], axis=1)
    mixing = jnp.sum(
        jnp.where(paired[:, :, None] == slot_range[None, None, :], gates[:, :, None], 0.0), axis=1
    ).reshape(token_count, expert_count, half_cap)
    local_sum = 0.0
    for index, returned in enumerate(chunk_results):
        local_sum = local_sum + jnp.dot(
            mixing[:, :, index * chunk : (index + 1) * chunk].reshape(token_count, -1),
            returned.reshape(-1, model_width),
            precision=lax.Precision.HIGHEST,
        )
    moe_own = tp_reduce_scatter(local_sum)
    return (own_residual + moe_own).astype(jnp.bfloat16)


REQ = ("grp", "x")


def solution(mesh):
    def run(*args):
        experts = args[8].shape[1]
        copies = mesh.shape["req"] // experts
        fine = jax.sharding.Mesh(
            mesh.devices.reshape(experts, copies, mesh.shape["tp"]), ("grp", "x", "tp")
        )
        return sharded(fine)(*args)

    return run


def sharded(fine):
    return jax.shard_map(
        per_device,
        mesh=fine,
        in_specs=(
            P(REQ, None),
            P(REQ),
            P(REQ, None, "tp"),
            P(REQ, None, "tp"),
            P(),
            P(None, None, "tp"),
            P("tp", None),
            P(),
            P(),
            P(REQ, None),
            P(REQ, None, "tp"),
            P(REQ, None, "tp"),
            P(REQ, "tp", None),
        ),
        out_specs=P((*REQ, "tp"), None),
        check_vma=False,
    )
```

```python
import functools
import math

import jax
import jax.numpy as jnp
from jax import lax
from jax.experimental import pallas as pl
from jax.experimental.pallas import tpu as pltpu
from jax.sharding import PartitionSpec as P

HEAD = 64
TOP = 2
CAP = 96


EPSILON = 1e-05


def normalize(inputs, scale_gain):
    mean_square = jnp.mean(inputs * inputs, axis=-1, keepdims=True)
    return inputs * lax.rsqrt(mean_square + EPSILON) * scale_gain


def rotate(inputs, positions):
    half_dim = inputs.shape[-1] // 2
    frequency = jnp.exp(
        jnp.arange(half_dim, dtype=jnp.float32) * (-2.0 * math.log(10000.0) / inputs.shape[-1])
    )
    angles = positions.astype(jnp.float32)[:, None] * frequency[None, :]
    cosine = jnp.cos(angles)[:, None, :]
    sine_part = jnp.sin(angles)[:, None, :]
    lower_half = inputs[..., :half_dim]
    upper_half = inputs[..., half_dim:]
    return jnp.concatenate(
        [
            lower_half * cosine - upper_half * sine_part,
            lower_half * sine_part + upper_half * cosine,
        ],
        axis=-1,
    )


def attention_kernel(
    length_ref, query_ref, key_ref, value_ref, fresh_key_ref, fresh_value_ref, out_ref, *, head_dim
):
    query_count = query_ref.shape[0]
    cache_len = key_ref.shape[1]
    length = length_ref[0]
    cache_live = lax.broadcasted_iota(jnp.int32, (query_count, cache_len), 1) < length
    fresh_live = lax.broadcasted_iota(
        jnp.int32, (query_count, query_count), 1
    ) <= lax.broadcasted_iota(jnp.int32, (query_count, query_count), 0)
    contract = (((1,), (1,)), ((), ()))
    for head in range(query_ref.shape[1] // head_dim):
        lanes = slice(head * head_dim, (head + 1) * head_dim)
        queries = query_ref[:, lanes]
        cache_scores = jnp.dot(
            queries, key_ref[lanes, :], preferred_element_type=jnp.float32
        ) * (head_dim ** -0.5)
        fresh_scores = jnp.dot(
            queries, fresh_key_ref[lanes, :], preferred_element_type=jnp.float32
        ) * (head_dim ** -0.5)
        cache_scores = jnp.where(cache_live, cache_scores, -jnp.inf)
        fresh_scores = jnp.where(fresh_live, fresh_scores, -jnp.inf)
        row_max = jnp.maximum(
            jnp.max(cache_scores, axis=1, keepdims=True),
            jnp.max(fresh_scores, axis=1, keepdims=True),
        )
        cache_weights = jnp.exp(cache_scores - row_max)
        fresh_weights = jnp.exp(fresh_scores - row_max)
        totals = jnp.sum(cache_weights, axis=1, keepdims=True) + jnp.sum(
            fresh_weights, axis=1, keepdims=True
        )
        mixture = lax.dot_general(
            cache_weights.astype(jnp.bfloat16),
            value_ref[lanes, :],
            contract,
            preferred_element_type=jnp.float32,
        ) + lax.dot_general(
            fresh_weights.astype(jnp.bfloat16),
            fresh_value_ref[lanes, :],
            contract,
            preferred_element_type=jnp.float32,
        )
        out_ref[:, lanes] = (mixture / totals).astype(out_ref.dtype)


def attention(queries, key_cache, value_cache, fresh_keys, fresh_values, length):
    vmem = pl.BlockSpec(memory_space=pltpu.VMEM)
    return pl.pallas_call(
        functools.partial(attention_kernel, head_dim=HEAD),
        out_shape=jax.ShapeDtypeStruct(queries.shape, jnp.bfloat16),
        in_specs=[pl.BlockSpec(memory_space=pltpu.SMEM)] + [vmem] * 5,
        out_specs=vmem,
    )(length, queries, key_cache.T, value_cache.T, fresh_keys.T, fresh_values.T)


def tp_allreduce(partial):
    tp_size = lax.axis_size("tp")
    core = lax.axis_index("tp") % 2
    core_pairs = [(i, i ^ 1) for i in range(tp_size)]
    z_pairs = [(i, i ^ 2) for i in range(tp_size)]
    halves = partial.astype(jnp.bfloat16).reshape(2, partial.shape[0] // 2, partial.shape[1])
    keep = jnp.where(core == 0, halves[0], halves[1])
    send = jnp.where(core == 0, halves[1], halves[0])
    chip_sum = (
        keep.astype(jnp.float32) + lax.ppermute(send, "tp", core_pairs).astype(jnp.float32)
    ).astype(jnp.bfloat16)
    total = (
        chip_sum.astype(jnp.float32) + lax.ppermute(chip_sum, "tp", z_pairs).astype(jnp.float32)
    ).astype(jnp.bfloat16)
    other = lax.ppermute(total, "tp", core_pairs)
    return jnp.where(core == 0, jnp.concatenate([total, other]), jnp.concatenate([other, total]))


def tp_reduce_scatter(partial):
    tp_size = lax.axis_size("tp")
    tp_index = lax.axis_index("tp")
    core = tp_index % 2
    upper = tp_index // 2
    core_pairs = [(i, i ^ 1) for i in range(tp_size)]
    z_pairs = [(i, i ^ 2) for i in range(tp_size)]
    blocks = partial.astype(jnp.bfloat16).reshape(2, 2, partial.shape[0] // 4, partial.shape[1])
    keep = jnp.where(core == 0, blocks[:, 0], blocks[:, 1])
    send = jnp.where(core == 0, blocks[:, 1], blocks[:, 0])
    chip_sum = (
        keep.astype(jnp.float32) + lax.ppermute(send, "tp", core_pairs).astype(jnp.float32)
    ).astype(jnp.bfloat16)
    mine = jnp.where(upper == 0, chip_sum[0], chip_sum[1])
    theirs = jnp.where(upper == 0, chip_sum[1], chip_sum[0])
    return mine.astype(jnp.float32) + lax.ppermute(theirs, "tp", z_pairs).astype(jnp.float32)


def per_device(
    hidden_in,
    cache_lengths,
    key_cache,
    value_cache,
    attn_norm,
    w_qkv,
    w_out,
    ffn_norm,
    router,
    routes,
    expert_gate,
    expert_up,
    expert_down,
):
    token_count = hidden_in.shape[0]
    model_width = hidden_in.shape[1]
    local_lanes = w_qkv.shape[2]
    local_heads = local_lanes // HEAD
    cache_len = key_cache.shape[1]
    token_share = token_count // lax.axis_size("tp")
    offset = lax.axis_index("tp") * token_share
    expert_count = router.shape[1]
    residual = hidden_in.astype(jnp.float32)
    normed = normalize(residual, attn_norm).astype(jnp.bfloat16)
    projected = jnp.einsum("td,cdh->cth", normed, w_qkv, preferred_element_type=jnp.float32)
    length = cache_lengths[0]
    positions = length + jnp.arange(token_count, dtype=jnp.int32)
    queries = rotate(projected[0].reshape(token_count, local_heads, HEAD), positions).astype(
        jnp.bfloat16
    )
    fresh_keys = rotate(projected[1].reshape(token_count, local_heads, HEAD), positions).astype(
        jnp.bfloat16
    )
    fresh_values = projected[2].reshape(token_count, local_heads, HEAD).astype(jnp.bfloat16)
    attended = attention(
        queries.reshape(token_count, local_lanes),
        key_cache[0],
        value_cache[0],
        fresh_keys.reshape(token_count, local_lanes),
        fresh_values.reshape(token_count, local_lanes),
        cache_lengths,
    )
    summed_attn = tp_allreduce(
        jnp.dot(attended, w_out, preferred_element_type=jnp.float32)
    ).astype(jnp.float32)
    updated = residual + summed_attn
    moe_input = normalize(updated, ffn_norm).astype(jnp.bfloat16)
    own_residual = lax.dynamic_slice_in_dim(updated, offset, token_share, 0)
    logits = jnp.dot(moe_input, router, preferred_element_type=jnp.float32)
    chosen = jnp.take_along_axis(logits, routes, axis=1)
    first_gate = 1.0 / (1.0 + jnp.exp(chosen[:, 1] - chosen[:, 0]))
    second_gate = 1.0 / (1.0 + jnp.exp(chosen[:, 0] - chosen[:, 1]))
    flat_routes = routes.reshape(-1)
    onehot = (flat_routes[:, None] == jnp.arange(expert_count, dtype=jnp.int32)[None, :]).astype(
        jnp.int32
    )
    slot_rank = jnp.sum((jnp.cumsum(onehot, axis=0) - onehot) * onehot, axis=1)
    tp_size = lax.axis_size("tp")
    core = lax.axis_index("tp") % 2
    half_cap = CAP // 2
    pairs = [(i, i ^ 1) for i in range(tp_size)]
    gate_w = jnp.concatenate([expert_gate[0], lax.ppermute(expert_gate[0], "tp", pairs)], axis=1)
    up_w = jnp.concatenate([expert_up[0], lax.ppermute(expert_up[0], "tp", pairs)], axis=1)
    down_w = jnp.concatenate([expert_down[0], lax.ppermute(expert_down[0], "tp", pairs)], axis=0)
    gate_w, up_w, down_w, moe_input = lax.optimization_barrier((gate_w, up_w, down_w, moe_input))
    local_rank = slot_rank - core * half_cap
    in_half = (local_rank >= 0) & (local_rank < half_cap)
    slot_ids = jnp.where(in_half, flat_routes * half_cap + local_rank, -1)
    paired = slot_ids.reshape(token_count, TOP)
    slot_range = jnp.arange(expert_count * half_cap, dtype=jnp.int32)
    chunk_count = 2
    chunk = half_cap // chunk_count
    ring = lax.axis_size("x")
    plus = [(i, (i + 1) % ring) for i in range(ring)]
    minus = [(i, (i - 1) % ring) for i in range(ring)]
    split = expert_count // 2
    chunk_results = []
    for index in range(chunk_count):
        chunk_ids = jnp.where(
            (local_rank >= index * chunk) & (local_rank < (index + 1) * chunk),
            flat_routes * chunk + local_rank - index * chunk,
            -1,
        ).reshape(token_count, TOP)
        chunk_range = jnp.arange(expert_count * chunk, dtype=jnp.int32)
        placing = jnp.any(chunk_ids[None, :, :] == chunk_range[:, None, None], axis=2).astype(
            jnp.bfloat16
        )
        packed = (
            jnp.dot(placing, moe_input, preferred_element_type=jnp.float32)
            .astype(jnp.bfloat16)
            .reshape(expert_count, chunk, model_width)
        )
        own = lax.all_to_all(packed, "grp", split_axis=0, concat_axis=0, tiled=True)
        from_left = lax.ppermute(own, "x", plus)
        from_right = lax.ppermute(own, "x", minus)
        from_far = jnp.concatenate(
            [lax.ppermute(from_left[:split], "x", plus), lax.ppermute(from_right[split:], "x", minus)]
        )
        received = jnp.stack([own, from_left, from_right, from_far])
        token_rows = received.reshape(-1, model_width)
        gate_proj = jnp.dot(token_rows, gate_w, preferred_element_type=jnp.float32)
        up_proj = jnp.dot(token_rows, up_w, preferred_element_type=jnp.float32)
        activation = (jax.nn.silu(gate_proj) * up_proj).astype(jnp.bfloat16)
        partial_value = jnp.dot(
            activation, down_w, preferred_element_type=jnp.float32
        ).astype(jnp.bfloat16).reshape(received.shape)
        far_a = lax.ppermute(partial_value[3, :split], "x", plus)
        far_b = lax.ppermute(partial_value[3, split:], "x", minus)
        to_right = partial_value[2].astype(jnp.float32)
        to_right = jnp.concatenate([to_right[:split] + far_a.astype(jnp.float32), to_right[split:]])
        to_left = partial_value[1].astype(jnp.float32)
        to_left = jnp.concatenate([to_left[:split], to_left[split:] + far_b.astype(jnp.float32)])
        at_x = (
            partial_value[0].astype(jnp.float32)
            + lax.ppermute(to_right.astype(jnp.bfloat16), "x", plus).astype(jnp.float32)
            + lax.ppermute(to_left.astype(jnp.bfloat16), "x", minus).astype(jnp.float32)
        ).astype(jnp.bfloat16)
        returned = lax.all_to_all(at_x, "grp", split_axis=0, concat_axis=0, tiled=True)
        chunk_results.append(returned.astype(jnp.float32))
    summed = jnp.concatenate(chunk_results, axis=1).reshape(expert_count * half_cap, model_width)
    gates = jnp.stack([first_gate, second_gate], axis=1)
    mixing = jnp.sum(
        jnp.where(paired[:, :, None] == slot_range[None, None, :], gates[:, :, None], 0.0), axis=1
    )
    local_sum = jnp.dot(mixing, summed, precision=lax.Precision.HIGHEST)
    moe_own = tp_reduce_scatter(local_sum)
    return (own_residual + moe_own).astype(jnp.bfloat16)


REQ = ("grp", "x")


def solution(mesh):
    def run(*args):
        experts = args[8].shape[1]
        copies = mesh.shape["req"] // experts
        fine = jax.sharding.Mesh(
            mesh.devices.reshape(experts, copies, mesh.shape["tp"]), ("grp", "x", "tp")
        )
        return sharded(fine)(*args)

    return run


def sharded(fine):
    return jax.shard_map(
        per_device,
        mesh=fine,
        in_specs=(
            P(REQ, None),
            P(REQ),
            P(REQ, None, "tp"),
            P(REQ, None, "tp"),
            P(),
            P(None, None, "tp"),
            P("tp", None),
            P(),
            P(),
            P(REQ, None),
            P(REQ, None, "tp"),
            P(REQ, None, "tp"),
            P(REQ, "tp", None),
        ),
        out_specs=P((*REQ, "tp"), None),
        check_vma=False,
    )
```

```python
import functools
import math

import jax
import jax.numpy as jnp
from jax import lax
from jax.experimental import pallas as pl
from jax.experimental.pallas import tpu as pltpu
from jax.sharding import PartitionSpec as P

HEAD = 64
TOP = 2
CAP = 96


EPSILON = 1e-05


def normalize(inputs, scale_gain):
    mean_square = jnp.mean(inputs * inputs, axis=-1, keepdims=True)
    return inputs * lax.rsqrt(mean_square + EPSILON) * scale_gain


def rotate(inputs, positions):
    half_dim = inputs.shape[-1] // 2
    frequency = jnp.exp(
        jnp.arange(half_dim, dtype=jnp.float32) * (-2.0 * math.log(10000.0) / inputs.shape[-1])
    )
    angles = positions.astype(jnp.float32)[:, None] * frequency[None, :]
    cosine = jnp.cos(angles)[:, None, :]
    sine_part = jnp.sin(angles)[:, None, :]
    lower_half = inputs[..., :half_dim]
    upper_half = inputs[..., half_dim:]
    return jnp.concatenate(
        [
            lower_half * cosine - upper_half * sine_part,
            lower_half * sine_part + upper_half * cosine,
        ],
        axis=-1,
    )


def attention_kernel(
    length_ref, query_ref, key_ref, value_ref, fresh_key_ref, fresh_value_ref, out_ref, *, head_dim
):
    query_count = query_ref.shape[0]
    cache_len = key_ref.shape[1]
    length = length_ref[0]
    cache_live = lax.broadcasted_iota(jnp.int32, (query_count, cache_len), 1) < length
    fresh_live = lax.broadcasted_iota(
        jnp.int32, (query_count, query_count), 1
    ) <= lax.broadcasted_iota(jnp.int32, (query_count, query_count), 0)
    contract = (((1,), (1,)), ((), ()))
    for head in range(query_ref.shape[1] // head_dim):
        lanes = slice(head * head_dim, (head + 1) * head_dim)
        queries = query_ref[:, lanes]
        cache_scores = jnp.dot(
            queries, key_ref[lanes, :], preferred_element_type=jnp.float32
        ) * (head_dim ** -0.5)
        fresh_scores = jnp.dot(
            queries, fresh_key_ref[lanes, :], preferred_element_type=jnp.float32
        ) * (head_dim ** -0.5)
        cache_scores = jnp.where(cache_live, cache_scores, -jnp.inf)
        fresh_scores = jnp.where(fresh_live, fresh_scores, -jnp.inf)
        row_max = jnp.maximum(
            jnp.max(cache_scores, axis=1, keepdims=True),
            jnp.max(fresh_scores, axis=1, keepdims=True),
        )
        cache_weights = jnp.exp(cache_scores - row_max)
        fresh_weights = jnp.exp(fresh_scores - row_max)
        totals = jnp.sum(cache_weights, axis=1, keepdims=True) + jnp.sum(
            fresh_weights, axis=1, keepdims=True
        )
        mixture = lax.dot_general(
            cache_weights.astype(jnp.bfloat16),
            value_ref[lanes, :],
            contract,
            preferred_element_type=jnp.float32,
        ) + lax.dot_general(
            fresh_weights.astype(jnp.bfloat16),
            fresh_value_ref[lanes, :],
            contract,
            preferred_element_type=jnp.float32,
        )
        out_ref[:, lanes] = (mixture / totals).astype(out_ref.dtype)


def attention(queries, key_cache, value_cache, fresh_keys, fresh_values, length):
    vmem = pl.BlockSpec(memory_space=pltpu.VMEM)
    return pl.pallas_call(
        functools.partial(attention_kernel, head_dim=HEAD),
        out_shape=jax.ShapeDtypeStruct(queries.shape, jnp.bfloat16),
        in_specs=[pl.BlockSpec(memory_space=pltpu.SMEM)] + [vmem] * 5,
        out_specs=vmem,
    )(length, queries, key_cache.T, value_cache.T, fresh_keys.T, fresh_values.T)


def tp_allreduce(partial):
    tp_size = lax.axis_size("tp")
    core = lax.axis_index("tp") % 2
    core_pairs = [(i, i ^ 1) for i in range(tp_size)]
    z_pairs = [(i, i ^ 2) for i in range(tp_size)]
    halves = partial.astype(jnp.bfloat16).reshape(2, partial.shape[0] // 2, partial.shape[1])
    keep = jnp.where(core == 0, halves[0], halves[1])
    send = jnp.where(core == 0, halves[1], halves[0])
    chip_sum = (
        keep.astype(jnp.float32) + lax.ppermute(send, "tp", core_pairs).astype(jnp.float32)
    ).astype(jnp.bfloat16)
    total = (
        chip_sum.astype(jnp.float32) + lax.ppermute(chip_sum, "tp", z_pairs).astype(jnp.float32)
    ).astype(jnp.bfloat16)
    other = lax.ppermute(total, "tp", core_pairs)
    return jnp.where(core == 0, jnp.concatenate([total, other]), jnp.concatenate([other, total]))


def tp_reduce_scatter(partial):
    tp_size = lax.axis_size("tp")
    tp_index = lax.axis_index("tp")
    core = tp_index % 2
    upper = tp_index // 2
    core_pairs = [(i, i ^ 1) for i in range(tp_size)]
    z_pairs = [(i, i ^ 2) for i in range(tp_size)]
    blocks = partial.astype(jnp.bfloat16).reshape(2, 2, partial.shape[0] // 4, partial.shape[1])
    keep = jnp.where(core == 0, blocks[:, 0], blocks[:, 1])
    send = jnp.where(core == 0, blocks[:, 1], blocks[:, 0])
    chip_sum = (
        keep.astype(jnp.float32) + lax.ppermute(send, "tp", core_pairs).astype(jnp.float32)
    ).astype(jnp.bfloat16)
    mine = jnp.where(upper == 0, chip_sum[0], chip_sum[1])
    theirs = jnp.where(upper == 0, chip_sum[1], chip_sum[0])
    return mine.astype(jnp.float32) + lax.ppermute(theirs, "tp", z_pairs).astype(jnp.float32)


def per_device(
    hidden_in,
    cache_lengths,
    key_cache,
    value_cache,
    attn_norm,
    w_qkv,
    w_out,
    ffn_norm,
    router,
    routes,
    expert_gate,
    expert_up,
    expert_down,
):
    token_count = hidden_in.shape[0]
    model_width = hidden_in.shape[1]
    local_lanes = w_qkv.shape[2]
    local_heads = local_lanes // HEAD
    cache_len = key_cache.shape[1]
    token_share = token_count // lax.axis_size("tp")
    offset = lax.axis_index("tp") * token_share
    expert_count = router.shape[1]
    residual = hidden_in.astype(jnp.float32)
    normed = normalize(residual, attn_norm).astype(jnp.bfloat16)
    projected = jnp.einsum("td,cdh->cth", normed, w_qkv, preferred_element_type=jnp.float32)
    length = cache_lengths[0]
    positions = length + jnp.arange(token_count, dtype=jnp.int32)
    queries = rotate(projected[0].reshape(token_count, local_heads, HEAD), positions).astype(
        jnp.bfloat16
    )
    fresh_keys = rotate(projected[1].reshape(token_count, local_heads, HEAD), positions).astype(
        jnp.bfloat16
    )
    fresh_values = projected[2].reshape(token_count, local_heads, HEAD).astype(jnp.bfloat16)
    pairs = [(i, i ^ 1) for i in range(lax.axis_size("tp"))]
    gate_w = jnp.concatenate([expert_gate[0], lax.ppermute(expert_gate[0], "tp", pairs)], axis=1)
    up_w = jnp.concatenate([expert_up[0], lax.ppermute(expert_up[0], "tp", pairs)], axis=1)
    down_w = jnp.concatenate([expert_down[0], lax.ppermute(expert_down[0], "tp", pairs)], axis=0)
    gate_w, up_w, down_w, queries = lax.optimization_barrier((gate_w, up_w, down_w, queries))
    attended = attention(
        queries.reshape(token_count, local_lanes),
        key_cache[0],
        value_cache[0],
        fresh_keys.reshape(token_count, local_lanes),
        fresh_values.reshape(token_count, local_lanes),
        cache_lengths,
    )
    summed_attn = tp_allreduce(
        jnp.dot(attended, w_out, preferred_element_type=jnp.float32)
    ).astype(jnp.float32)
    updated = residual + summed_attn
    moe_input = normalize(updated, ffn_norm).astype(jnp.bfloat16)
    own_residual = lax.dynamic_slice_in_dim(updated, offset, token_share, 0)
    logits = jnp.dot(moe_input, router, preferred_element_type=jnp.float32)
    chosen = jnp.take_along_axis(logits, routes, axis=1)
    first_gate = 1.0 / (1.0 + jnp.exp(chosen[:, 1] - chosen[:, 0]))
    second_gate = 1.0 / (1.0 + jnp.exp(chosen[:, 0] - chosen[:, 1]))
    flat_routes = routes.reshape(-1)
    onehot = (flat_routes[:, None] == jnp.arange(expert_count, dtype=jnp.int32)[None, :]).astype(
        jnp.int32
    )
    slot_rank = jnp.sum((jnp.cumsum(onehot, axis=0) - onehot) * onehot, axis=1)
    tp_size = lax.axis_size("tp")
    core = lax.axis_index("tp") % 2
    half_cap = CAP // 2
    local_rank = slot_rank - core * half_cap
    in_half = (local_rank >= 0) & (local_rank < half_cap)
    slot_ids = jnp.where(in_half, flat_routes * half_cap + local_rank, -1)
    paired = slot_ids.reshape(token_count, TOP)
    slot_range = jnp.arange(expert_count * half_cap, dtype=jnp.int32)
    chunk_count = 2
    chunk = half_cap // chunk_count
    ring = lax.axis_size("x")
    plus = [(i, (i + 1) % ring) for i in range(ring)]
    minus = [(i, (i - 1) % ring) for i in range(ring)]
    split = expert_count // 2
    chunk_results = []
    for index in range(chunk_count):
        chunk_ids = jnp.where(
            (local_rank >= index * chunk) & (local_rank < (index + 1) * chunk),
            flat_routes * chunk + local_rank - index * chunk,
            -1,
        ).reshape(token_count, TOP)
        chunk_range = jnp.arange(expert_count * chunk, dtype=jnp.int32)
        placing = jnp.any(chunk_ids[None, :, :] == chunk_range[:, None, None], axis=2).astype(
            jnp.bfloat16
        )
        packed = (
            jnp.dot(placing, moe_input, preferred_element_type=jnp.float32)
            .astype(jnp.bfloat16)
            .reshape(expert_count, chunk, model_width)
        )
        own = lax.all_to_all(packed, "grp", split_axis=0, concat_axis=0, tiled=True)
        from_left = lax.ppermute(own, "x", plus)
        from_right = lax.ppermute(own, "x", minus)
        from_far = jnp.concatenate(
            [lax.ppermute(from_left[:split], "x", plus), lax.ppermute(from_right[split:], "x", minus)]
        )
        received = jnp.stack([own, from_left, from_right, from_far])
        token_rows = received.reshape(-1, model_width)
        gate_proj = jnp.dot(token_rows, gate_w, preferred_element_type=jnp.float32)
        up_proj = jnp.dot(token_rows, up_w, preferred_element_type=jnp.float32)
        activation = (jax.nn.silu(gate_proj) * up_proj).astype(jnp.bfloat16)
        partial_value = jnp.dot(
            activation, down_w, preferred_element_type=jnp.float32
        ).astype(jnp.bfloat16).reshape(received.shape)
        far_a = lax.ppermute(partial_value[3, :split], "x", plus)
        far_b = lax.ppermute(partial_value[3, split:], "x", minus)
        to_right = partial_value[2].astype(jnp.float32)
        to_right = jnp.concatenate([to_right[:split] + far_a.astype(jnp.float32), to_right[split:]])
        to_left = partial_value[1].astype(jnp.float32)
        to_left = jnp.concatenate([to_left[:split], to_left[split:] + far_b.astype(jnp.float32)])
        at_x = (
            partial_value[0].astype(jnp.float32)
            + lax.ppermute(to_right.astype(jnp.bfloat16), "x", plus).astype(jnp.float32)
            + lax.ppermute(to_left.astype(jnp.bfloat16), "x", minus).astype(jnp.float32)
        ).astype(jnp.bfloat16)
        returned = lax.all_to_all(at_x, "grp", split_axis=0, concat_axis=0, tiled=True)
        chunk_results.append(returned.astype(jnp.float32))
    summed = jnp.concatenate(chunk_results, axis=1).reshape(expert_count * half_cap, model_width)
    gates = jnp.stack([first_gate, second_gate], axis=1)
    mixing = jnp.sum(
        jnp.where(paired[:, :, None] == slot_range[None, None, :], gates[:, :, None], 0.0), axis=1
    )
    local_sum = jnp.dot(mixing, summed, precision=lax.Precision.HIGHEST)
    moe_own = tp_reduce_scatter(local_sum)
    return (own_residual + moe_own).astype(jnp.bfloat16)


REQ = ("grp", "x")


def solution(mesh):
    def run(*args):
        experts = args[8].shape[1]
        copies = mesh.shape["req"] // experts
        fine = jax.sharding.Mesh(
            mesh.devices.reshape(experts, copies, mesh.shape["tp"]), ("grp", "x", "tp")
        )
        return sharded(fine)(*args)

    return run


def sharded(fine):
    return jax.shard_map(
        per_device,
        mesh=fine,
        in_specs=(
            P(REQ, None),
            P(REQ),
            P(REQ, None, "tp"),
            P(REQ, None, "tp"),
            P(),
            P(None, None, "tp"),
            P("tp", None),
            P(),
            P(),
            P(REQ, None),
            P(REQ, None, "tp"),
            P(REQ, None, "tp"),
            P(REQ, "tp", None),
        ),
        out_specs=P((*REQ, "tp"), None),
        check_vma=False,
    )
```

```python
import functools
import math

import jax
import jax.numpy as jnp
from jax import lax
from jax.experimental import pallas as pl
from jax.experimental.pallas import tpu as pltpu
from jax.sharding import PartitionSpec as P

HEAD = 64
TOP = 2
CAP = 96


EPSILON = 1e-05


def normalize(inputs, scale_gain):
    mean_square = jnp.mean(inputs * inputs, axis=-1, keepdims=True)
    return inputs * lax.rsqrt(mean_square + EPSILON) * scale_gain


def rotate(inputs, positions):
    half_dim = inputs.shape[-1] // 2
    frequency = jnp.exp(
        jnp.arange(half_dim, dtype=jnp.float32) * (-2.0 * math.log(10000.0) / inputs.shape[-1])
    )
    angles = positions.astype(jnp.float32)[:, None] * frequency[None, :]
    cosine = jnp.cos(angles)[:, None, :]
    sine_part = jnp.sin(angles)[:, None, :]
    lower_half = inputs[..., :half_dim]
    upper_half = inputs[..., half_dim:]
    return jnp.concatenate(
        [
            lower_half * cosine - upper_half * sine_part,
            lower_half * sine_part + upper_half * cosine,
        ],
        axis=-1,
    )


def attention_kernel(
    length_ref, query_ref, key_ref, value_ref, fresh_key_ref, fresh_value_ref, out_ref, *, head_dim
):
    query_count = query_ref.shape[0]
    cache_len = key_ref.shape[1]
    length = length_ref[0]
    cache_live = lax.broadcasted_iota(jnp.int32, (query_count, cache_len), 1) < length
    fresh_live = lax.broadcasted_iota(
        jnp.int32, (query_count, query_count), 1
    ) <= lax.broadcasted_iota(jnp.int32, (query_count, query_count), 0)
    contract = (((1,), (1,)), ((), ()))
    for head in range(query_ref.shape[1] // head_dim):
        lanes = slice(head * head_dim, (head + 1) * head_dim)
        queries = query_ref[:, lanes]
        cache_scores = jnp.dot(
            queries, key_ref[lanes, :], preferred_element_type=jnp.float32
        ) * (head_dim ** -0.5)
        fresh_scores = jnp.dot(
            queries, fresh_key_ref[lanes, :], preferred_element_type=jnp.float32
        ) * (head_dim ** -0.5)
        cache_scores = jnp.where(cache_live, cache_scores, -jnp.inf)
        fresh_scores = jnp.where(fresh_live, fresh_scores, -jnp.inf)
        row_max = jnp.maximum(
            jnp.max(cache_scores, axis=1, keepdims=True),
            jnp.max(fresh_scores, axis=1, keepdims=True),
        )
        cache_weights = jnp.exp(cache_scores - row_max)
        fresh_weights = jnp.exp(fresh_scores - row_max)
        totals = jnp.sum(cache_weights, axis=1, keepdims=True) + jnp.sum(
            fresh_weights, axis=1, keepdims=True
        )
        mixture = lax.dot_general(
            cache_weights.astype(jnp.bfloat16),
            value_ref[lanes, :],
            contract,
            preferred_element_type=jnp.float32,
        ) + lax.dot_general(
            fresh_weights.astype(jnp.bfloat16),
            fresh_value_ref[lanes, :],
            contract,
            preferred_element_type=jnp.float32,
        )
        out_ref[:, lanes] = (mixture / totals).astype(out_ref.dtype)


def attention(queries, key_cache, value_cache, fresh_keys, fresh_values, length):
    vmem = pl.BlockSpec(memory_space=pltpu.VMEM)
    return pl.pallas_call(
        functools.partial(attention_kernel, head_dim=HEAD),
        out_shape=jax.ShapeDtypeStruct(queries.shape, jnp.bfloat16),
        in_specs=[pl.BlockSpec(memory_space=pltpu.SMEM)] + [vmem] * 5,
        out_specs=vmem,
    )(length, queries, key_cache.T, value_cache.T, fresh_keys.T, fresh_values.T)


def tp_allreduce(partial):
    tp_size = lax.axis_size("tp")
    core = lax.axis_index("tp") % 2
    core_pairs = [(i, i ^ 1) for i in range(tp_size)]
    z_pairs = [(i, i ^ 2) for i in range(tp_size)]
    halves = partial.astype(jnp.bfloat16).reshape(2, partial.shape[0] // 2, partial.shape[1])
    keep = jnp.where(core == 0, halves[0], halves[1])
    send = jnp.where(core == 0, halves[1], halves[0])
    chip_sum = (
        keep.astype(jnp.float32) + lax.ppermute(send, "tp", core_pairs).astype(jnp.float32)
    ).astype(jnp.bfloat16)
    total = (
        chip_sum.astype(jnp.float32) + lax.ppermute(chip_sum, "tp", z_pairs).astype(jnp.float32)
    ).astype(jnp.bfloat16)
    other = lax.ppermute(total, "tp", core_pairs)
    return jnp.where(core == 0, jnp.concatenate([total, other]), jnp.concatenate([other, total]))


def tp_reduce_scatter(partial):
    tp_size = lax.axis_size("tp")
    tp_index = lax.axis_index("tp")
    core = tp_index % 2
    upper = tp_index // 2
    core_pairs = [(i, i ^ 1) for i in range(tp_size)]
    z_pairs = [(i, i ^ 2) for i in range(tp_size)]
    blocks = partial.astype(jnp.bfloat16).reshape(2, 2, partial.shape[0] // 4, partial.shape[1])
    keep = jnp.where(core == 0, blocks[:, 0], blocks[:, 1])
    send = jnp.where(core == 0, blocks[:, 1], blocks[:, 0])
    chip_sum = (
        keep.astype(jnp.float32) + lax.ppermute(send, "tp", core_pairs).astype(jnp.float32)
    ).astype(jnp.bfloat16)
    mine = jnp.where(upper == 0, chip_sum[0], chip_sum[1])
    theirs = jnp.where(upper == 0, chip_sum[1], chip_sum[0])
    return mine.astype(jnp.float32) + lax.ppermute(theirs, "tp", z_pairs).astype(jnp.float32)


def per_device(
    hidden_in,
    cache_lengths,
    key_cache,
    value_cache,
    attn_norm,
    w_qkv,
    w_out,
    ffn_norm,
    router,
    routes,
    expert_gate,
    expert_up,
    expert_down,
):
    token_count = hidden_in.shape[0]
    model_width = hidden_in.shape[1]
    local_lanes = w_qkv.shape[2]
    local_heads = local_lanes // HEAD
    cache_len = key_cache.shape[1]
    token_share = token_count // lax.axis_size("tp")
    offset = lax.axis_index("tp") * token_share
    expert_count = router.shape[1]
    residual = hidden_in.astype(jnp.float32)
    normed = normalize(residual, attn_norm).astype(jnp.bfloat16)
    projected = jnp.einsum("td,cdh->cth", normed, w_qkv, preferred_element_type=jnp.float32)
    length = cache_lengths[0]
    positions = length + jnp.arange(token_count, dtype=jnp.int32)
    queries = rotate(projected[0].reshape(token_count, local_heads, HEAD), positions).astype(
        jnp.bfloat16
    )
    fresh_keys = rotate(projected[1].reshape(token_count, local_heads, HEAD), positions).astype(
        jnp.bfloat16
    )
    fresh_values = projected[2].reshape(token_count, local_heads, HEAD).astype(jnp.bfloat16)
    attended = attention(
        queries.reshape(token_count, local_lanes),
        key_cache[0],
        value_cache[0],
        fresh_keys.reshape(token_count, local_lanes),
        fresh_values.reshape(token_count, local_lanes),
        cache_lengths,
    )
    summed_attn = tp_allreduce(
        jnp.dot(attended, w_out, preferred_element_type=jnp.float32)
    ).astype(jnp.float32)
    updated = residual + summed_attn
    moe_input = normalize(updated, ffn_norm).astype(jnp.bfloat16)
    own_residual = lax.dynamic_slice_in_dim(updated, offset, token_share, 0)
    logits = jnp.dot(moe_input, router, preferred_element_type=jnp.float32)
    chosen = jnp.take_along_axis(logits, routes, axis=1)
    first_gate = 1.0 / (1.0 + jnp.exp(chosen[:, 1] - chosen[:, 0]))
    second_gate = 1.0 / (1.0 + jnp.exp(chosen[:, 0] - chosen[:, 1]))
    flat_routes = routes.reshape(-1)
    onehot = (flat_routes[:, None] == jnp.arange(expert_count, dtype=jnp.int32)[None, :]).astype(
        jnp.int32
    )
    slot_rank = jnp.sum((jnp.cumsum(onehot, axis=0) - onehot) * onehot, axis=1)
    tp_size = lax.axis_size("tp")
    core = lax.axis_index("tp") % 2
    half_cap = CAP // 2
    pairs = [(i, i ^ 1) for i in range(tp_size)]
    weight_blocks = [
        (expert_gate[0], expert_up[0], expert_down[0]),
        tuple(lax.ppermute(w[0], "tp", pairs) for w in (expert_gate, expert_up, expert_down)),
    ]
    local_rank = slot_rank - core * half_cap
    in_half = (local_rank >= 0) & (local_rank < half_cap)
    slot_ids = jnp.where(in_half, flat_routes * half_cap + local_rank, -1)
    paired = slot_ids.reshape(token_count, TOP)
    slot_range = jnp.arange(expert_count * half_cap, dtype=jnp.int32)
    chunk_count = 2
    chunk = half_cap // chunk_count
    ring = lax.axis_size("x")
    plus = [(i, (i + 1) % ring) for i in range(ring)]
    minus = [(i, (i - 1) % ring) for i in range(ring)]
    split = expert_count // 2
    chunk_results = []
    for index in range(chunk_count):
        chunk_ids = jnp.where(
            (local_rank >= index * chunk) & (local_rank < (index + 1) * chunk),
            flat_routes * chunk + local_rank - index * chunk,
            -1,
        ).reshape(token_count, TOP)
        chunk_range = jnp.arange(expert_count * chunk, dtype=jnp.int32)
        placing = jnp.any(chunk_ids[None, :, :] == chunk_range[:, None, None], axis=2).astype(
            jnp.bfloat16
        )
        packed = (
            jnp.dot(placing, moe_input, preferred_element_type=jnp.float32)
            .astype(jnp.bfloat16)
            .reshape(expert_count, chunk, model_width)
        )
        own = lax.all_to_all(packed, "grp", split_axis=0, concat_axis=0, tiled=True)
        from_left = lax.ppermute(own, "x", plus)
        from_right = lax.ppermute(own, "x", minus)
        from_far = jnp.concatenate(
            [lax.ppermute(from_left[:split], "x", plus), lax.ppermute(from_right[split:], "x", minus)]
        )
        received = jnp.stack([own, from_left, from_right, from_far])
        token_rows = received.reshape(-1, model_width)
        partial_value = 0.0
        for gate_w, up_w, down_w in weight_blocks:
            gate_proj = jnp.dot(token_rows, gate_w, preferred_element_type=jnp.float32)
            up_proj = jnp.dot(token_rows, up_w, preferred_element_type=jnp.float32)
            activation = (jax.nn.silu(gate_proj) * up_proj).astype(jnp.bfloat16)
            partial_value = partial_value + jnp.dot(
                activation, down_w, preferred_element_type=jnp.float32
            )
        partial_value = partial_value.astype(jnp.bfloat16).reshape(received.shape)
        far_a = lax.ppermute(partial_value[3, :split], "x", plus)
        far_b = lax.ppermute(partial_value[3, split:], "x", minus)
        to_right = partial_value[2].astype(jnp.float32)
        to_right = jnp.concatenate([to_right[:split] + far_a.astype(jnp.float32), to_right[split:]])
        to_left = partial_value[1].astype(jnp.float32)
        to_left = jnp.concatenate([to_left[:split], to_left[split:] + far_b.astype(jnp.float32)])
        at_x = (
            partial_value[0].astype(jnp.float32)
            + lax.ppermute(to_right.astype(jnp.bfloat16), "x", plus).astype(jnp.float32)
            + lax.ppermute(to_left.astype(jnp.bfloat16), "x", minus).astype(jnp.float32)
        ).astype(jnp.bfloat16)
        returned = lax.all_to_all(at_x, "grp", split_axis=0, concat_axis=0, tiled=True)
        chunk_results.append(returned.astype(jnp.float32))
    summed = jnp.concatenate(chunk_results, axis=1).reshape(expert_count * half_cap, model_width)
    gates = jnp.stack([first_gate, second_gate], axis=1)
    mixing = jnp.sum(
        jnp.where(paired[:, :, None] == slot_range[None, None, :], gates[:, :, None], 0.0), axis=1
    )
    local_sum = jnp.dot(mixing, summed, precision=lax.Precision.HIGHEST)
    moe_own = tp_reduce_scatter(local_sum)
    return (own_residual + moe_own).astype(jnp.bfloat16)


REQ = ("grp", "x")


def solution(mesh):
    def run(*args):
        experts = args[8].shape[1]
        copies = mesh.shape["req"] // experts
        fine = jax.sharding.Mesh(
            mesh.devices.reshape(experts, copies, mesh.shape["tp"]), ("grp", "x", "tp")
        )
        return sharded(fine)(*args)

    return run


def sharded(fine):
    return jax.shard_map(
        per_device,
        mesh=fine,
        in_specs=(
            P(REQ, None),
            P(REQ),
            P(REQ, None, "tp"),
            P(REQ, None, "tp"),
            P(),
            P(None, None, "tp"),
            P("tp", None),
            P(),
            P(),
            P(REQ, None),
            P(REQ, None, "tp"),
            P(REQ, None, "tp"),
            P(REQ, "tp", None),
        ),
        out_specs=P((*REQ, "tp"), None),
        check_vma=False,
    )
```

```python
import functools
import math

import jax
import jax.numpy as jnp
from jax import lax
from jax.experimental import pallas as pl
from jax.experimental.pallas import tpu as pltpu
from jax.sharding import PartitionSpec as P

HEAD = 64
TOP = 2
CAP = 96


EPSILON = 1e-05


def normalize(inputs, scale_gain):
    mean_square = jnp.mean(inputs * inputs, axis=-1, keepdims=True)
    return inputs * lax.rsqrt(mean_square + EPSILON) * scale_gain


def rotate(inputs, positions):
    half_dim = inputs.shape[-1] // 2
    frequency = jnp.exp(
        jnp.arange(half_dim, dtype=jnp.float32) * (-2.0 * math.log(10000.0) / inputs.shape[-1])
    )
    angles = positions.astype(jnp.float32)[:, None] * frequency[None, :]
    cosine = jnp.cos(angles)[:, None, :]
    sine_part = jnp.sin(angles)[:, None, :]
    lower_half = inputs[..., :half_dim]
    upper_half = inputs[..., half_dim:]
    return jnp.concatenate(
        [
            lower_half * cosine - upper_half * sine_part,
            lower_half * sine_part + upper_half * cosine,
        ],
        axis=-1,
    )


def attention_kernel(
    length_ref, query_ref, key_ref, value_ref, fresh_key_ref, fresh_value_ref, out_ref, *, head_dim
):
    query_count = query_ref.shape[0]
    cache_len = key_ref.shape[1]
    length = length_ref[0]
    cache_live = lax.broadcasted_iota(jnp.int32, (query_count, cache_len), 1) < length
    fresh_live = lax.broadcasted_iota(
        jnp.int32, (query_count, query_count), 1
    ) <= lax.broadcasted_iota(jnp.int32, (query_count, query_count), 0)
    contract = (((1,), (1,)), ((), ()))
    for head in range(query_ref.shape[1] // head_dim):
        lanes = slice(head * head_dim, (head + 1) * head_dim)
        queries = query_ref[:, lanes]
        cache_scores = jnp.dot(
            queries, key_ref[lanes, :], preferred_element_type=jnp.float32
        ) * (head_dim ** -0.5)
        fresh_scores = jnp.dot(
            queries, fresh_key_ref[lanes, :], preferred_element_type=jnp.float32
        ) * (head_dim ** -0.5)
        cache_scores = jnp.where(cache_live, cache_scores, -jnp.inf)
        fresh_scores = jnp.where(fresh_live, fresh_scores, -jnp.inf)
        row_max = jnp.maximum(
            jnp.max(cache_scores, axis=1, keepdims=True),
            jnp.max(fresh_scores, axis=1, keepdims=True),
        )
        cache_weights = jnp.exp(cache_scores - row_max)
        fresh_weights = jnp.exp(fresh_scores - row_max)
        totals = jnp.sum(cache_weights, axis=1, keepdims=True) + jnp.sum(
            fresh_weights, axis=1, keepdims=True
        )
        mixture = lax.dot_general(
            cache_weights.astype(jnp.bfloat16),
            value_ref[lanes, :],
            contract,
            preferred_element_type=jnp.float32,
        ) + lax.dot_general(
            fresh_weights.astype(jnp.bfloat16),
            fresh_value_ref[lanes, :],
            contract,
            preferred_element_type=jnp.float32,
        )
        out_ref[:, lanes] = (mixture / totals).astype(out_ref.dtype)


def attention(queries, key_cache, value_cache, fresh_keys, fresh_values, length):
    vmem = pl.BlockSpec(memory_space=pltpu.VMEM)
    return pl.pallas_call(
        functools.partial(attention_kernel, head_dim=HEAD),
        out_shape=jax.ShapeDtypeStruct(queries.shape, jnp.bfloat16),
        in_specs=[pl.BlockSpec(memory_space=pltpu.SMEM)] + [vmem] * 5,
        out_specs=vmem,
    )(length, queries, key_cache.T, value_cache.T, fresh_keys.T, fresh_values.T)


def tp_allreduce(partial):
    tp_size = lax.axis_size("tp")
    core = lax.axis_index("tp") % 2
    core_pairs = [(i, i ^ 1) for i in range(tp_size)]
    z_pairs = [(i, i ^ 2) for i in range(tp_size)]
    halves = partial.astype(jnp.bfloat16).reshape(2, partial.shape[0] // 2, partial.shape[1])
    keep = jnp.where(core == 0, halves[0], halves[1])
    send = jnp.where(core == 0, halves[1], halves[0])
    chip_sum = (
        keep.astype(jnp.float32) + lax.ppermute(send, "tp", core_pairs).astype(jnp.float32)
    ).astype(jnp.bfloat16)
    total = (
        chip_sum.astype(jnp.float32) + lax.ppermute(chip_sum, "tp", z_pairs).astype(jnp.float32)
    ).astype(jnp.bfloat16)
    other = lax.ppermute(total, "tp", core_pairs)
    return jnp.where(core == 0, jnp.concatenate([total, other]), jnp.concatenate([other, total]))


def tp_reduce_scatter(partial):
    tp_size = lax.axis_size("tp")
    tp_index = lax.axis_index("tp")
    core = tp_index % 2
    upper = tp_index // 2
    core_pairs = [(i, i ^ 1) for i in range(tp_size)]
    z_pairs = [(i, i ^ 2) for i in range(tp_size)]
    blocks = partial.astype(jnp.bfloat16).reshape(2, 2, partial.shape[0] // 4, partial.shape[1])
    keep = jnp.where(core == 0, blocks[:, 0], blocks[:, 1])
    send = jnp.where(core == 0, blocks[:, 1], blocks[:, 0])
    chip_sum = (
        keep.astype(jnp.float32) + lax.ppermute(send, "tp", core_pairs).astype(jnp.float32)
    ).astype(jnp.bfloat16)
    mine = jnp.where(upper == 0, chip_sum[0], chip_sum[1])
    theirs = jnp.where(upper == 0, chip_sum[1], chip_sum[0])
    return mine.astype(jnp.float32) + lax.ppermute(theirs, "tp", z_pairs).astype(jnp.float32)


def per_device(
    hidden_in,
    cache_lengths,
    key_cache,
    value_cache,
    attn_norm,
    w_qkv,
    w_out,
    ffn_norm,
    router,
    routes,
    expert_gate,
    expert_up,
    expert_down,
):
    token_count = hidden_in.shape[0]
    model_width = hidden_in.shape[1]
    local_lanes = w_qkv.shape[2]
    local_heads = local_lanes // HEAD
    cache_len = key_cache.shape[1]
    token_share = token_count // lax.axis_size("tp")
    offset = lax.axis_index("tp") * token_share
    expert_count = router.shape[1]
    residual = hidden_in.astype(jnp.float32)
    normed = normalize(residual, attn_norm).astype(jnp.bfloat16)
    projected = jnp.einsum("td,cdh->cth", normed, w_qkv, preferred_element_type=jnp.float32)
    length = cache_lengths[0]
    positions = length + jnp.arange(token_count, dtype=jnp.int32)
    queries = rotate(projected[0].reshape(token_count, local_heads, HEAD), positions).astype(
        jnp.bfloat16
    )
    fresh_keys = rotate(projected[1].reshape(token_count, local_heads, HEAD), positions).astype(
        jnp.bfloat16
    )
    fresh_values = projected[2].reshape(token_count, local_heads, HEAD).astype(jnp.bfloat16)
    attended = attention(
        queries.reshape(token_count, local_lanes),
        key_cache[0],
        value_cache[0],
        fresh_keys.reshape(token_count, local_lanes),
        fresh_values.reshape(token_count, local_lanes),
        cache_lengths,
    )
    summed_attn = tp_allreduce(
        jnp.dot(attended, w_out, preferred_element_type=jnp.float32)
    ).astype(jnp.float32)
    updated = residual + summed_attn
    moe_input = normalize(updated, ffn_norm).astype(jnp.bfloat16)
    own_residual = lax.dynamic_slice_in_dim(updated, offset, token_share, 0)
    logits = jnp.dot(moe_input, router, preferred_element_type=jnp.float32)
    chosen = jnp.take_along_axis(logits, routes, axis=1)
    first_gate = 1.0 / (1.0 + jnp.exp(chosen[:, 1] - chosen[:, 0]))
    second_gate = 1.0 / (1.0 + jnp.exp(chosen[:, 0] - chosen[:, 1]))
    flat_routes = routes.reshape(-1)
    onehot = (flat_routes[:, None] == jnp.arange(expert_count, dtype=jnp.int32)[None, :]).astype(
        jnp.int32
    )
    slot_rank = jnp.sum((jnp.cumsum(onehot, axis=0) - onehot) * onehot, axis=1)
    tp_size = lax.axis_size("tp")
    core = lax.axis_index("tp") % 2
    half_cap = CAP // 2
    pairs = [(i, i ^ 1) for i in range(tp_size)]
    gate_w = jnp.concatenate([expert_gate[0], lax.ppermute(expert_gate[0], "tp", pairs)], axis=1)
    up_w = jnp.concatenate([expert_up[0], lax.ppermute(expert_up[0], "tp", pairs)], axis=1)
    down_w = jnp.concatenate([expert_down[0], lax.ppermute(expert_down[0], "tp", pairs)], axis=0)
    local_rank = slot_rank - core * half_cap
    in_half = (local_rank >= 0) & (local_rank < half_cap)
    slot_ids = jnp.where(in_half, flat_routes * half_cap + local_rank, -1)
    paired = slot_ids.reshape(token_count, TOP)
    slot_range = jnp.arange(expert_count * half_cap, dtype=jnp.int32)
    chunk_count = 2
    chunk = half_cap // chunk_count
    ring = lax.axis_size("x")
    plus = [(i, (i + 1) % ring) for i in range(ring)]
    minus = [(i, (i - 1) % ring) for i in range(ring)]
    split = expert_count // 2
    chunk_results = []
    for index in range(chunk_count):
        chunk_ids = jnp.where(
            (local_rank >= index * chunk) & (local_rank < (index + 1) * chunk),
            flat_routes * chunk + local_rank - index * chunk,
            -1,
        ).reshape(token_count, TOP)
        chunk_range = jnp.arange(expert_count * chunk, dtype=jnp.int32)
        placing = jnp.any(chunk_ids[None, :, :] == chunk_range[:, None, None], axis=2).astype(
            jnp.bfloat16
        )
        packed = (
            jnp.dot(placing, moe_input, preferred_element_type=jnp.float32)
            .astype(jnp.bfloat16)
            .reshape(expert_count, chunk, model_width)
        )
        own = lax.all_to_all(packed, "grp", split_axis=0, concat_axis=0, tiled=True)
        from_left = lax.ppermute(own, "x", plus)
        from_right = lax.ppermute(own, "x", minus)
        from_far = jnp.concatenate(
            [lax.ppermute(from_left[:split], "x", plus), lax.ppermute(from_right[split:], "x", minus)]
        )
        received = jnp.stack([own, from_left, from_right, from_far])
        token_rows = received.reshape(-1, model_width)
        gate_proj = jnp.dot(token_rows, gate_w, preferred_element_type=jnp.float32)
        up_proj = jnp.dot(token_rows, up_w, preferred_element_type=jnp.float32)
        activation = (jax.nn.silu(gate_proj) * up_proj).astype(jnp.bfloat16)
        partial_value = jnp.dot(
            activation, down_w, preferred_element_type=jnp.float32
        ).astype(jnp.bfloat16).reshape(received.shape)
        far_a = lax.ppermute(partial_value[3, :split], "x", plus)
        far_b = lax.ppermute(partial_value[3, split:], "x", minus)
        to_right = partial_value[2].astype(jnp.float32)
        to_right = jnp.concatenate([to_right[:split] + far_a.astype(jnp.float32), to_right[split:]])
        to_left = partial_value[1].astype(jnp.float32)
        to_left = jnp.concatenate([to_left[:split], to_left[split:] + far_b.astype(jnp.float32)])
        at_x = (
            partial_value[0].astype(jnp.float32)
            + lax.ppermute(to_right.astype(jnp.bfloat16), "x", plus).astype(jnp.float32)
            + lax.ppermute(to_left.astype(jnp.bfloat16), "x", minus).astype(jnp.float32)
        ).astype(jnp.bfloat16)
        returned = lax.all_to_all(at_x, "grp", split_axis=0, concat_axis=0, tiled=True)
        chunk_results.append(returned.astype(jnp.float32))
    summed = jnp.concatenate(chunk_results, axis=1).reshape(expert_count * half_cap, model_width)
    gates = jnp.stack([first_gate, second_gate], axis=1)
    mixing = jnp.sum(
        jnp.where(paired[:, :, None] == slot_range[None, None, :], gates[:, :, None], 0.0), axis=1
    )
    summed_exact = summed.astype(jnp.bfloat16)
    mixing_high = mixing.astype(jnp.bfloat16)
    mixing_low = (mixing - mixing_high.astype(jnp.float32)).astype(jnp.bfloat16)
    local_sum = jnp.dot(mixing_high, summed_exact, preferred_element_type=jnp.float32) + jnp.dot(
        mixing_low, summed_exact, preferred_element_type=jnp.float32
    )
    moe_own = tp_reduce_scatter(local_sum)
    return (own_residual + moe_own).astype(jnp.bfloat16)


REQ = ("grp", "x")


def solution(mesh):
    def run(*args):
        experts = args[8].shape[1]
        copies = mesh.shape["req"] // experts
        fine = jax.sharding.Mesh(
            mesh.devices.reshape(experts, copies, mesh.shape["tp"]), ("grp", "x", "tp")
        )
        return sharded(fine)(*args)

    return run


def sharded(fine):
    return jax.shard_map(
        per_device,
        mesh=fine,
        in_specs=(
            P(REQ, None),
            P(REQ),
            P(REQ, None, "tp"),
            P(REQ, None, "tp"),
            P(),
            P(None, None, "tp"),
            P("tp", None),
            P(),
            P(),
            P(REQ, None),
            P(REQ, None, "tp"),
            P(REQ, None, "tp"),
            P(REQ, "tp", None),
        ),
        out_specs=P((*REQ, "tp"), None),
        check_vma=False,
    )
```

```python
import functools
import math

import jax
import jax.numpy as jnp
from jax import lax
from jax.experimental import pallas as pl
from jax.experimental.pallas import tpu as pltpu
from jax.sharding import PartitionSpec as P

HEAD = 64
TOP = 2
CAP = 96


EPSILON = 1e-05


def normalize(inputs, scale_gain):
    mean_square = jnp.mean(inputs * inputs, axis=-1, keepdims=True)
    return inputs * lax.rsqrt(mean_square + EPSILON) * scale_gain


def rotate(inputs, positions):
    half_dim = inputs.shape[-1] // 2
    frequency = jnp.exp(
        jnp.arange(half_dim, dtype=jnp.float32) * (-2.0 * math.log(10000.0) / inputs.shape[-1])
    )
    angles = positions.astype(jnp.float32)[:, None] * frequency[None, :]
    cosine = jnp.cos(angles)[:, None, :]
    sine_part = jnp.sin(angles)[:, None, :]
    lower_half = inputs[..., :half_dim]
    upper_half = inputs[..., half_dim:]
    return jnp.concatenate(
        [
            lower_half * cosine - upper_half * sine_part,
            lower_half * sine_part + upper_half * cosine,
        ],
        axis=-1,
    )


def attention_kernel(
    length_ref, query_ref, key_ref, value_ref, fresh_key_ref, fresh_value_ref, out_ref, *, head_dim
):
    query_count = query_ref.shape[1]
    cache_len = key_ref.shape[1]
    length = length_ref[0]
    cache_live = lax.broadcasted_iota(jnp.int32, (query_count, cache_len), 1) < length
    fresh_live = lax.broadcasted_iota(
        jnp.int32, (query_count, query_count), 1
    ) <= lax.broadcasted_iota(jnp.int32, (query_count, query_count), 0)
    by_first = (((0,), (0,)), ((), ()))
    by_second = (((1,), (1,)), ((), ()))

    def one_head(head, carry):
        rows = pl.ds(pl.multiple_of(head * head_dim, head_dim), head_dim)
        queries = query_ref[rows, :]
        cache_scores = lax.dot_general(
            queries, key_ref[rows, :], by_first, preferred_element_type=jnp.float32
        ) * (head_dim ** -0.5)
        fresh_scores = lax.dot_general(
            queries, fresh_key_ref[rows, :], by_first, preferred_element_type=jnp.float32
        ) * (head_dim ** -0.5)
        cache_scores = jnp.where(cache_live, cache_scores, -jnp.inf)
        fresh_scores = jnp.where(fresh_live, fresh_scores, -jnp.inf)
        row_max = jnp.maximum(
            jnp.max(cache_scores, axis=1, keepdims=True),
            jnp.max(fresh_scores, axis=1, keepdims=True),
        )
        cache_weights = jnp.exp(cache_scores - row_max)
        fresh_weights = jnp.exp(fresh_scores - row_max)
        totals = jnp.sum(cache_weights, axis=1, keepdims=True) + jnp.sum(
            fresh_weights, axis=1, keepdims=True
        )
        mixture = lax.dot_general(
            cache_weights.astype(jnp.bfloat16),
            value_ref[rows, :],
            by_second,
            preferred_element_type=jnp.float32,
        ) + lax.dot_general(
            fresh_weights.astype(jnp.bfloat16),
            fresh_value_ref[rows, :],
            by_second,
            preferred_element_type=jnp.float32,
        )
        out_ref[rows, :] = jnp.transpose((mixture / totals).astype(out_ref.dtype))
        return carry

    lax.fori_loop(0, query_ref.shape[0] // head_dim, one_head, 0)


def attention(queries, key_cache, value_cache, fresh_keys, fresh_values, length):
    vmem = pl.BlockSpec(memory_space=pltpu.VMEM)
    return pl.pallas_call(
        functools.partial(attention_kernel, head_dim=HEAD),
        out_shape=jax.ShapeDtypeStruct(queries.T.shape, jnp.bfloat16),
        in_specs=[pl.BlockSpec(memory_space=pltpu.SMEM)] + [vmem] * 5,
        out_specs=vmem,
    )(length, queries.T, key_cache.T, value_cache.T, fresh_keys.T, fresh_values.T).T


def tp_allreduce(partial):
    tp_size = lax.axis_size("tp")
    core = lax.axis_index("tp") % 2
    core_pairs = [(i, i ^ 1) for i in range(tp_size)]
    z_pairs = [(i, i ^ 2) for i in range(tp_size)]
    halves = partial.astype(jnp.bfloat16).reshape(2, partial.shape[0] // 2, partial.shape[1])
    keep = jnp.where(core == 0, halves[0], halves[1])
    send = jnp.where(core == 0, halves[1], halves[0])
    chip_sum = (
        keep.astype(jnp.float32) + lax.ppermute(send, "tp", core_pairs).astype(jnp.float32)
    ).astype(jnp.bfloat16)
    total = (
        chip_sum.astype(jnp.float32) + lax.ppermute(chip_sum, "tp", z_pairs).astype(jnp.float32)
    ).astype(jnp.bfloat16)
    other = lax.ppermute(total, "tp", core_pairs)
    return jnp.where(core == 0, jnp.concatenate([total, other]), jnp.concatenate([other, total]))


def tp_reduce_scatter(partial):
    tp_size = lax.axis_size("tp")
    tp_index = lax.axis_index("tp")
    core = tp_index % 2
    upper = tp_index // 2
    core_pairs = [(i, i ^ 1) for i in range(tp_size)]
    z_pairs = [(i, i ^ 2) for i in range(tp_size)]
    blocks = partial.astype(jnp.bfloat16).reshape(2, 2, partial.shape[0] // 4, partial.shape[1])
    keep = jnp.where(core == 0, blocks[:, 0], blocks[:, 1])
    send = jnp.where(core == 0, blocks[:, 1], blocks[:, 0])
    chip_sum = (
        keep.astype(jnp.float32) + lax.ppermute(send, "tp", core_pairs).astype(jnp.float32)
    ).astype(jnp.bfloat16)
    mine = jnp.where(upper == 0, chip_sum[0], chip_sum[1])
    theirs = jnp.where(upper == 0, chip_sum[1], chip_sum[0])
    return mine.astype(jnp.float32) + lax.ppermute(theirs, "tp", z_pairs).astype(jnp.float32)


def per_device(
    hidden_in,
    cache_lengths,
    key_cache,
    value_cache,
    attn_norm,
    w_qkv,
    w_out,
    ffn_norm,
    router,
    routes,
    expert_gate,
    expert_up,
    expert_down,
):
    token_count = hidden_in.shape[0]
    model_width = hidden_in.shape[1]
    local_lanes = w_qkv.shape[2]
    local_heads = local_lanes // HEAD
    cache_len = key_cache.shape[1]
    token_share = token_count // lax.axis_size("tp")
    offset = lax.axis_index("tp") * token_share
    expert_count = router.shape[1]
    residual = hidden_in.astype(jnp.float32)
    normed = normalize(residual, attn_norm).astype(jnp.bfloat16)
    projected = jnp.einsum("td,cdh->cth", normed, w_qkv, preferred_element_type=jnp.float32)
    length = cache_lengths[0]
    positions = length + jnp.arange(token_count, dtype=jnp.int32)
    queries = rotate(projected[0].reshape(token_count, local_heads, HEAD), positions).astype(
        jnp.bfloat16
    )
    fresh_keys = rotate(projected[1].reshape(token_count, local_heads, HEAD), positions).astype(
        jnp.bfloat16
    )
    fresh_values = projected[2].reshape(token_count, local_heads, HEAD).astype(jnp.bfloat16)
    attended = attention(
        queries.reshape(token_count, local_lanes),
        key_cache[0],
        value_cache[0],
        fresh_keys.reshape(token_count, local_lanes),
        fresh_values.reshape(token_count, local_lanes),
        cache_lengths,
    )
    summed_attn = tp_allreduce(
        jnp.dot(attended, w_out, preferred_element_type=jnp.float32)
    ).astype(jnp.float32)
    updated = residual + summed_attn
    moe_input = normalize(updated, ffn_norm).astype(jnp.bfloat16)
    own_residual = lax.dynamic_slice_in_dim(updated, offset, token_share, 0)
    logits = jnp.dot(moe_input, router, preferred_element_type=jnp.float32)
    chosen = jnp.take_along_axis(logits, routes, axis=1)
    first_gate = 1.0 / (1.0 + jnp.exp(chosen[:, 1] - chosen[:, 0]))
    second_gate = 1.0 / (1.0 + jnp.exp(chosen[:, 0] - chosen[:, 1]))
    flat_routes = routes.reshape(-1)
    onehot = (flat_routes[:, None] == jnp.arange(expert_count, dtype=jnp.int32)[None, :]).astype(
        jnp.int32
    )
    slot_rank = jnp.sum((jnp.cumsum(onehot, axis=0) - onehot) * onehot, axis=1)
    tp_size = lax.axis_size("tp")
    core = lax.axis_index("tp") % 2
    half_cap = CAP // 2
    pairs = [(i, i ^ 1) for i in range(tp_size)]
    gate_w = jnp.concatenate([expert_gate[0], lax.ppermute(expert_gate[0], "tp", pairs)], axis=1)
    up_w = jnp.concatenate([expert_up[0], lax.ppermute(expert_up[0], "tp", pairs)], axis=1)
    down_w = jnp.concatenate([expert_down[0], lax.ppermute(expert_down[0], "tp", pairs)], axis=0)
    local_rank = slot_rank - core * half_cap
    in_half = (local_rank >= 0) & (local_rank < half_cap)
    slot_ids = jnp.where(in_half, flat_routes * half_cap + local_rank, -1)
    paired = slot_ids.reshape(token_count, TOP)
    slot_range = jnp.arange(expert_count * half_cap, dtype=jnp.int32)
    chunk_count = 2
    chunk = half_cap // chunk_count
    ring = lax.axis_size("x")
    plus = [(i, (i + 1) % ring) for i in range(ring)]
    minus = [(i, (i - 1) % ring) for i in range(ring)]
    split = expert_count // 2
    chunk_results = []
    for index in range(chunk_count):
        chunk_ids = jnp.where(
            (local_rank >= index * chunk) & (local_rank < (index + 1) * chunk),
            flat_routes * chunk + local_rank - index * chunk,
            -1,
        ).reshape(token_count, TOP)
        chunk_range = jnp.arange(expert_count * chunk, dtype=jnp.int32)
        placing = jnp.any(chunk_ids[None, :, :] == chunk_range[:, None, None], axis=2).astype(
            jnp.bfloat16
        )
        packed = (
            jnp.dot(placing, moe_input, preferred_element_type=jnp.float32)
            .astype(jnp.bfloat16)
            .reshape(expert_count, chunk, model_width)
        )
        own = lax.all_to_all(packed, "grp", split_axis=0, concat_axis=0, tiled=True)
        from_left = lax.ppermute(own, "x", plus)
        from_right = lax.ppermute(own, "x", minus)
        from_far = jnp.concatenate(
            [lax.ppermute(from_left[:split], "x", plus), lax.ppermute(from_right[split:], "x", minus)]
        )
        received = jnp.stack([own, from_left, from_right, from_far])
        token_rows = received.reshape(-1, model_width)
        gate_proj = jnp.dot(token_rows, gate_w, preferred_element_type=jnp.float32)
        up_proj = jnp.dot(token_rows, up_w, preferred_element_type=jnp.float32)
        activation = (jax.nn.silu(gate_proj) * up_proj).astype(jnp.bfloat16)
        partial_value = jnp.dot(
            activation, down_w, preferred_element_type=jnp.float32
        ).astype(jnp.bfloat16).reshape(received.shape)
        far_a = lax.ppermute(partial_value[3, :split], "x", plus)
        far_b = lax.ppermute(partial_value[3, split:], "x", minus)
        to_right = partial_value[2].astype(jnp.float32)
        to_right = jnp.concatenate([to_right[:split] + far_a.astype(jnp.float32), to_right[split:]])
        to_left = partial_value[1].astype(jnp.float32)
        to_left = jnp.concatenate([to_left[:split], to_left[split:] + far_b.astype(jnp.float32)])
        at_x = (
            partial_value[0].astype(jnp.float32)
            + lax.ppermute(to_right.astype(jnp.bfloat16), "x", plus).astype(jnp.float32)
            + lax.ppermute(to_left.astype(jnp.bfloat16), "x", minus).astype(jnp.float32)
        ).astype(jnp.bfloat16)
        returned = lax.all_to_all(at_x, "grp", split_axis=0, concat_axis=0, tiled=True)
        chunk_results.append(returned.astype(jnp.float32))
    summed = jnp.concatenate(chunk_results, axis=1).reshape(expert_count * half_cap, model_width)
    gates = jnp.stack([first_gate, second_gate], axis=1)
    mixing = jnp.sum(
        jnp.where(paired[:, :, None] == slot_range[None, None, :], gates[:, :, None], 0.0), axis=1
    )
    local_sum = jnp.dot(mixing, summed, precision=lax.Precision.HIGHEST)
    moe_own = tp_reduce_scatter(local_sum)
    return (own_residual + moe_own).astype(jnp.bfloat16)


REQ = ("grp", "x")


def solution(mesh):
    def run(*args):
        experts = args[8].shape[1]
        copies = mesh.shape["req"] // experts
        fine = jax.sharding.Mesh(
            mesh.devices.reshape(experts, copies, mesh.shape["tp"]), ("grp", "x", "tp")
        )
        return sharded(fine)(*args)

    return run


def sharded(fine):
    return jax.shard_map(
        per_device,
        mesh=fine,
        in_specs=(
            P(REQ, None),
            P(REQ),
            P(REQ, None, "tp"),
            P(REQ, None, "tp"),
            P(),
            P(None, None, "tp"),
            P("tp", None),
            P(),
            P(),
            P(REQ, None),
            P(REQ, None, "tp"),
            P(REQ, None, "tp"),
            P(REQ, "tp", None),
        ),
        out_specs=P((*REQ, "tp"), None),
        check_vma=False,
    )
```

```python
import functools
import math

import jax
import jax.numpy as jnp
from jax import lax
from jax.experimental import pallas as pl
from jax.experimental.pallas import tpu as pltpu
from jax.sharding import PartitionSpec as P

HEAD = 64
TOP = 2
CAP = 96


EPSILON = 1e-05


def normalize(inputs, scale_gain):
    mean_square = jnp.mean(inputs * inputs, axis=-1, keepdims=True)
    return inputs * lax.rsqrt(mean_square + EPSILON) * scale_gain


def rotate(inputs, positions):
    half_dim = inputs.shape[-1] // 2
    frequency = jnp.exp(
        jnp.arange(half_dim, dtype=jnp.float32) * (-2.0 * math.log(10000.0) / inputs.shape[-1])
    )
    angles = positions.astype(jnp.float32)[:, None] * frequency[None, :]
    cosine = jnp.cos(angles)[:, None, :]
    sine_part = jnp.sin(angles)[:, None, :]
    lower_half = inputs[..., :half_dim]
    upper_half = inputs[..., half_dim:]
    return jnp.concatenate(
        [
            lower_half * cosine - upper_half * sine_part,
            lower_half * sine_part + upper_half * cosine,
        ],
        axis=-1,
    )


def attention_kernel(
    length_ref, query_ref, key_ref, value_ref, fresh_key_ref, fresh_value_ref, out_ref, *, head_dim
):
    query_count = query_ref.shape[0]
    cache_len = key_ref.shape[1]
    length = length_ref[0]
    cache_live = lax.broadcasted_iota(jnp.int32, (query_count, cache_len), 1) < length
    fresh_live = lax.broadcasted_iota(
        jnp.int32, (query_count, query_count), 1
    ) <= lax.broadcasted_iota(jnp.int32, (query_count, query_count), 0)
    contract = (((1,), (1,)), ((), ()))
    for head in range(query_ref.shape[1] // head_dim):
        lanes = slice(head * head_dim, (head + 1) * head_dim)
        queries = query_ref[:, lanes]
        cache_scores = jnp.dot(
            queries, key_ref[lanes, :], preferred_element_type=jnp.float32
        ) * (head_dim ** -0.5)
        fresh_scores = jnp.dot(
            queries, fresh_key_ref[lanes, :], preferred_element_type=jnp.float32
        ) * (head_dim ** -0.5)
        cache_scores = jnp.where(cache_live, cache_scores, -jnp.inf)
        fresh_scores = jnp.where(fresh_live, fresh_scores, -jnp.inf)
        row_max = jnp.maximum(
            jnp.max(cache_scores, axis=1, keepdims=True),
            jnp.max(fresh_scores, axis=1, keepdims=True),
        )
        cache_weights = jnp.exp(cache_scores - row_max)
        fresh_weights = jnp.exp(fresh_scores - row_max)
        totals = jnp.sum(cache_weights, axis=1, keepdims=True) + jnp.sum(
            fresh_weights, axis=1, keepdims=True
        )
        mixture = lax.dot_general(
            cache_weights.astype(jnp.bfloat16),
            value_ref[lanes, :],
            contract,
            preferred_element_type=jnp.float32,
        ) + lax.dot_general(
            fresh_weights.astype(jnp.bfloat16),
            fresh_value_ref[lanes, :],
            contract,
            preferred_element_type=jnp.float32,
        )
        out_ref[:, lanes] = (mixture / totals).astype(out_ref.dtype)


def attention(queries, key_cache, value_cache, fresh_keys, fresh_values, length):
    vmem = pl.BlockSpec(memory_space=pltpu.VMEM)
    return pl.pallas_call(
        functools.partial(attention_kernel, head_dim=HEAD),
        out_shape=jax.ShapeDtypeStruct(queries.shape, jnp.bfloat16),
        in_specs=[pl.BlockSpec(memory_space=pltpu.SMEM)] + [vmem] * 5,
        out_specs=vmem,
    )(length, queries, key_cache.T, value_cache.T, fresh_keys.T, fresh_values.T)


def tp_allreduce(partial):
    tp_size = lax.axis_size("tp")
    core = lax.axis_index("tp") % 2
    core_pairs = [(i, i ^ 1) for i in range(tp_size)]
    z_pairs = [(i, i ^ 2) for i in range(tp_size)]
    halves = partial.astype(jnp.bfloat16).reshape(2, partial.shape[0] // 2, partial.shape[1])
    keep = jnp.where(core == 0, halves[0], halves[1])
    send = jnp.where(core == 0, halves[1], halves[0])
    chip_sum = (
        keep.astype(jnp.float32) + lax.ppermute(send, "tp", core_pairs).astype(jnp.float32)
    ).astype(jnp.bfloat16)
    total = (
        chip_sum.astype(jnp.float32) + lax.ppermute(chip_sum, "tp", z_pairs).astype(jnp.float32)
    ).astype(jnp.bfloat16)
    other = lax.ppermute(total, "tp", core_pairs)
    return jnp.where(core == 0, jnp.concatenate([total, other]), jnp.concatenate([other, total]))


def tp_reduce_scatter(partial):
    tp_size = lax.axis_size("tp")
    tp_index = lax.axis_index("tp")
    core = tp_index % 2
    upper = tp_index // 2
    core_pairs = [(i, i ^ 1) for i in range(tp_size)]
    z_pairs = [(i, i ^ 2) for i in range(tp_size)]
    blocks = partial.astype(jnp.bfloat16).reshape(2, 2, partial.shape[0] // 4, partial.shape[1])
    keep = jnp.where(core == 0, blocks[:, 0], blocks[:, 1])
    send = jnp.where(core == 0, blocks[:, 1], blocks[:, 0])
    chip_sum = (
        keep.astype(jnp.float32) + lax.ppermute(send, "tp", core_pairs).astype(jnp.float32)
    ).astype(jnp.bfloat16)
    mine = jnp.where(upper == 0, chip_sum[0], chip_sum[1])
    theirs = jnp.where(upper == 0, chip_sum[1], chip_sum[0])
    return mine.astype(jnp.float32) + lax.ppermute(theirs, "tp", z_pairs).astype(jnp.float32)


def per_device(
    hidden_in,
    cache_lengths,
    key_cache,
    value_cache,
    attn_norm,
    w_qkv,
    w_out,
    ffn_norm,
    router,
    routes,
    expert_gate,
    expert_up,
    expert_down,
):
    token_count = hidden_in.shape[0]
    model_width = hidden_in.shape[1]
    local_lanes = w_qkv.shape[2]
    local_heads = local_lanes // HEAD
    cache_len = key_cache.shape[1]
    token_share = token_count // lax.axis_size("tp")
    offset = lax.axis_index("tp") * token_share
    expert_count = router.shape[1]
    residual = hidden_in.astype(jnp.float32)
    normed = normalize(residual, attn_norm).astype(jnp.bfloat16)
    projected = jnp.einsum("td,cdh->cth", normed, w_qkv, preferred_element_type=jnp.float32)
    length = cache_lengths[0]
    positions = length + jnp.arange(token_count, dtype=jnp.int32)
    queries = rotate(projected[0].reshape(token_count, local_heads, HEAD), positions).astype(
        jnp.bfloat16
    )
    fresh_keys = rotate(projected[1].reshape(token_count, local_heads, HEAD), positions).astype(
        jnp.bfloat16
    )
    fresh_values = projected[2].reshape(token_count, local_heads, HEAD).astype(jnp.bfloat16)
    attended = attention(
        queries.reshape(token_count, local_lanes),
        key_cache[0],
        value_cache[0],
        fresh_keys.reshape(token_count, local_lanes),
        fresh_values.reshape(token_count, local_lanes),
        cache_lengths,
    )
    summed_attn = tp_allreduce(
        jnp.dot(attended, w_out, preferred_element_type=jnp.float32)
    ).astype(jnp.float32)
    updated = residual + summed_attn
    moe_input = normalize(updated, ffn_norm).astype(jnp.bfloat16)
    own_residual = lax.dynamic_slice_in_dim(updated, offset, token_share, 0)
    logits = jnp.dot(moe_input, router, preferred_element_type=jnp.float32)
    chosen = jnp.take_along_axis(logits, routes, axis=1)
    first_gate = 1.0 / (1.0 + jnp.exp(chosen[:, 1] - chosen[:, 0]))
    second_gate = 1.0 / (1.0 + jnp.exp(chosen[:, 0] - chosen[:, 1]))
    flat_routes = routes.reshape(-1)
    onehot = (flat_routes[:, None] == jnp.arange(expert_count, dtype=jnp.int32)[None, :]).astype(
        jnp.int32
    )
    slot_rank = jnp.sum((jnp.cumsum(onehot, axis=0) - onehot) * onehot, axis=1)
    tp_size = lax.axis_size("tp")
    core = lax.axis_index("tp") % 2
    half_cap = CAP // 2
    pairs = [(i, i ^ 1) for i in range(tp_size)]
    gate_w = jnp.concatenate([expert_gate[0], lax.ppermute(expert_gate[0], "tp", pairs)], axis=1)
    up_w = jnp.concatenate([expert_up[0], lax.ppermute(expert_up[0], "tp", pairs)], axis=1)
    down_w = jnp.concatenate([expert_down[0], lax.ppermute(expert_down[0], "tp", pairs)], axis=0)
    local_rank = slot_rank - core * half_cap
    in_half = (local_rank >= 0) & (local_rank < half_cap)
    slot_ids = jnp.where(in_half, flat_routes * half_cap + local_rank, -1)
    paired = slot_ids.reshape(token_count, TOP)
    slot_range = jnp.arange(expert_count * half_cap, dtype=jnp.int32)
    bounds = [0, half_cap // 3, half_cap]
    ring = lax.axis_size("x")
    plus = [(i, (i + 1) % ring) for i in range(ring)]
    minus = [(i, (i - 1) % ring) for i in range(ring)]
    split = expert_count // 2
    chunk_results = []
    for low, high in zip(bounds[:-1], bounds[1:]):
        chunk = high - low
        chunk_ids = jnp.where(
            (local_rank >= low) & (local_rank < high),
            flat_routes * chunk + local_rank - low,
            -1,
        ).reshape(token_count, TOP)
        chunk_range = jnp.arange(expert_count * chunk, dtype=jnp.int32)
        placing = jnp.any(chunk_ids[None, :, :] == chunk_range[:, None, None], axis=2).astype(
            jnp.bfloat16
        )
        packed = (
            jnp.dot(placing, moe_input, preferred_element_type=jnp.float32)
            .astype(jnp.bfloat16)
            .reshape(expert_count, chunk, model_width)
        )
        own = lax.all_to_all(packed, "grp", split_axis=0, concat_axis=0, tiled=True)
        from_left = lax.ppermute(own, "x", plus)
        from_right = lax.ppermute(own, "x", minus)
        from_far = jnp.concatenate(
            [lax.ppermute(from_left[:split], "x", plus), lax.ppermute(from_right[split:], "x", minus)]
        )
        received = jnp.stack([own, from_left, from_right, from_far])
        token_rows = received.reshape(-1, model_width)
        gate_proj = jnp.dot(token_rows, gate_w, preferred_element_type=jnp.float32)
        up_proj = jnp.dot(token_rows, up_w, preferred_element_type=jnp.float32)
        activation = (jax.nn.silu(gate_proj) * up_proj).astype(jnp.bfloat16)
        partial_value = jnp.dot(
            activation, down_w, preferred_element_type=jnp.float32
        ).astype(jnp.bfloat16).reshape(received.shape)
        far_a = lax.ppermute(partial_value[3, :split], "x", plus)
        far_b = lax.ppermute(partial_value[3, split:], "x", minus)
        to_right = partial_value[2].astype(jnp.float32)
        to_right = jnp.concatenate([to_right[:split] + far_a.astype(jnp.float32), to_right[split:]])
        to_left = partial_value[1].astype(jnp.float32)
        to_left = jnp.concatenate([to_left[:split], to_left[split:] + far_b.astype(jnp.float32)])
        at_x = (
            partial_value[0].astype(jnp.float32)
            + lax.ppermute(to_right.astype(jnp.bfloat16), "x", plus).astype(jnp.float32)
            + lax.ppermute(to_left.astype(jnp.bfloat16), "x", minus).astype(jnp.float32)
        ).astype(jnp.bfloat16)
        returned = lax.all_to_all(at_x, "grp", split_axis=0, concat_axis=0, tiled=True)
        chunk_results.append(returned.astype(jnp.float32))
    summed = jnp.concatenate(chunk_results, axis=1).reshape(expert_count * half_cap, model_width)
    gates = jnp.stack([first_gate, second_gate], axis=1)
    mixing = jnp.sum(
        jnp.where(paired[:, :, None] == slot_range[None, None, :], gates[:, :, None], 0.0), axis=1
    )
    local_sum = jnp.dot(mixing, summed, precision=lax.Precision.HIGHEST)
    moe_own = tp_reduce_scatter(local_sum)
    return (own_residual + moe_own).astype(jnp.bfloat16)


REQ = ("grp", "x")


def solution(mesh):
    def run(*args):
        experts = args[8].shape[1]
        copies = mesh.shape["req"] // experts
        fine = jax.sharding.Mesh(
            mesh.devices.reshape(experts, copies, mesh.shape["tp"]), ("grp", "x", "tp")
        )
        return sharded(fine)(*args)

    return run


def sharded(fine):
    return jax.shard_map(
        per_device,
        mesh=fine,
        in_specs=(
            P(REQ, None),
            P(REQ),
            P(REQ, None, "tp"),
            P(REQ, None, "tp"),
            P(),
            P(None, None, "tp"),
            P("tp", None),
            P(),
            P(),
            P(REQ, None),
            P(REQ, None, "tp"),
            P(REQ, None, "tp"),
            P(REQ, "tp", None),
        ),
        out_specs=P((*REQ, "tp"), None),
        check_vma=False,
    )
```
